256 devices in a mesh: dp: 8 (over y, core), tm: 4 (over x), height: 8 (over z).
Axes of the slice: x: 4, y: 4, z: 8, core: 2. Of those that a mesh axis runs over, the one named last changes fastest.
Arguments:
- video_latents: bfloat16 [8, 8, 64, 128, 256], P('dp', 'tm', 'height'), may hold values from -48 to 48
- cotangent: bfloat16 [8, 8, 64, 128, 256], P('dp', 'tm', 'height'), may hold values from -48 to 48
- spatial_kernel: bfloat16 [3, 3, 256, 256], replicated, may hold values from -0.125 to 0.125
- temporal_kernel: bfloat16 [3, 256, 256], replicated, may hold values from -0.21875 to 0.21875
Outputs:
- block_output: bfloat16 [8, 8, 64, 128, 256], P('dp', 'tm', 'height')
- input_grad: bfloat16 [8, 8, 64, 128, 256], P('dp', 'tm', 'height')
- clipped_spatial: float32 [3, 3, 256, 256], replicated
- clipped_temporal: float32 [3, 256, 256], replicated
The draws below stay inside these ranges and needn't reach their ends.
All inputs are finite; a program needn't handle non-finite values.
Results may differ from the reference program's by a relative error of at most 0.0018.
The reference program's roundings to bfloat16 on the way (of `activated`, `hidden` and `pre_grad`) count: a program that leaves them out, or rounds other values in their place, can miss the bound.
Values may be sent and summed in bfloat16 or wider, within the bound.
No kernel may reach another device: no remote copies, remote signals or barrier semaphores. Data moves between devices by JAX's collectives and lax.ppermute only.
A program may use at most 128 MiB of HBM per device.

```python
import math
from functools import partial
import jax
import jax.numpy as jnp
from jax import lax

C = 256
GROUPS = 32
COLS = 128
CLIPS = 8
FRAMES = 8
ROWS = 64


def rising_rows():
    positions = jnp.arange(ROWS, dtype=jnp.float32)
    return jnp.exp(jnp.log(3.0) * positions / max(ROWS - 1, 1))


def drawn_field(key, spread):
    subkeys = jax.random.split(key, 2)
    full_shape = (CLIPS, FRAMES, ROWS, COLS, C)
    offset_shape = (CLIPS, FRAMES, 1, 1, C)
    rough_part = jnp.clip(jax.random.normal(subkeys[0], full_shape, jnp.float32), -6.0, 6.0)
    offsets = spread * jnp.clip(jax.random.normal(subkeys[1], offset_shape, jnp.float32), -3.0, 3.0)
    row_scale = rising_rows()
    return (rough_part + offsets) * row_scale[None, None, :, None, None]


def draw_video_latents(key, part):
    return drawn_field(jax.random.fold_in(key, 11), 0.6).astype(jnp.bfloat16)


def draw_cotangent(key, part):
    return drawn_field(jax.random.fold_in(key, 23), 0.8).astype(jnp.bfloat16)


def noise(key, extent, scale, reach, kind=jnp.bfloat16):
    return jnp.clip(scale * jax.random.normal(key, extent, jnp.float32), -reach, reach).astype(kind)


def setup_inputs(seed: int = 0) -> dict:
    key_of = jax.random.split(jax.random.key(seed), 5)
    video_latents = draw_video_latents(jax.random.fold_in(key_of[4], 71), 0)
    cotangent = draw_cotangent(jax.random.fold_in(key_of[4], 71), 0)
    spatial_kernel = noise(key_of[2], (3, 3, C, C), (9 * C) ** -0.5, 0.125)
    temporal_kernel = noise(key_of[3], (3, C, C), (3 * C) ** -0.5, 0.21875)
    return {"video_latents": video_latents, "cotangent": cotangent, "spatial_kernel": spatial_kernel, "temporal_kernel": temporal_kernel}


EPSILON = 1e-05
CLIP_DIVISOR = 20.0

def silu_slope(values):
    sigmoid = jax.nn.sigmoid(values)
    return sigmoid * (1.0 + values * (1.0 - sigmoid))

def mixed_einsum(formula, left_side, right_side):
    return jnp.einsum(formula, left_side.astype(jnp.float32), right_side.astype(jnp.float32), precision=lax.Precision.HIGHEST)

def one_clip(clip_inputs, spatial_kernel, temporal_kernel):
    clip_video, clip_cotangent = clip_inputs
    frames, height_rows, columns, channels = clip_video.shape
    group_width = channels // GROUPS
    members = height_rows * columns * group_width
    latents = clip_video.astype(jnp.float32)
    grouped = latents.reshape(frames, height_rows, columns, GROUPS, group_width)
    mean_value = lax.optimization_barrier(jnp.sum(grouped, axis=(1, 2, 4), keepdims=True)) / members
    second_mean = lax.optimization_barrier(jnp.sum(grouped * grouped, axis=(1, 2, 4), keepdims=True)) / members
    inverse_std = lax.rsqrt(second_mean - mean_value * mean_value + EPSILON)
    normed_grouped = (grouped - mean_value) * inverse_std
    normed = normed_grouped.reshape(latents.shape)
    activated = jax.nn.silu(normed).astype(jnp.bfloat16)
    padded = jnp.pad(activated, ((0, 0), (1, 1), (1, 1), (0, 0)))
    spatial_pre = jnp.zeros(latents.shape, jnp.float32)
    for tap_row in range(3):
        for tap_col in range(3):
            window = padded[:, tap_row:tap_row + height_rows, tap_col:tap_col + columns]
            spatial_pre = spatial_pre + mixed_einsum('fhwc,cd->fhwd', window, spatial_kernel[tap_row, tap_col])
    hidden = jax.nn.silu(spatial_pre).astype(jnp.bfloat16)
    extended = jnp.concatenate((jnp.zeros((2,) + hidden.shape[1:], jnp.bfloat16), hidden), axis=0)
    temporal_sum = jnp.zeros(latents.shape, jnp.float32)
    for tap in range(3):
        temporal_sum = temporal_sum + mixed_einsum('fhwc,cd->fhwd', extended[tap:tap + frames], temporal_kernel[tap])
    block_output = (latents + temporal_sum).astype(jnp.bfloat16)
    cot_extended = jnp.concatenate((clip_cotangent, jnp.zeros((2,) + clip_cotangent.shape[1:], jnp.bfloat16)), axis=0)
    hidden_grad = jnp.zeros(latents.shape, jnp.float32)
    for tap in range(3):
        hidden_grad = hidden_grad + mixed_einsum('fhwd,cd->fhwc', cot_extended[2 - tap:2 - tap + frames], temporal_kernel[tap])
    temporal_grad = jnp.stack([mixed_einsum('fhwc,fhwd->cd', extended[tap:tap + frames], clip_cotangent) for tap in range(3)])
    pre_grad = (hidden_grad * silu_slope(spatial_pre)).astype(jnp.bfloat16)
    grad_padded = jnp.pad(pre_grad, ((0, 0), (1, 1), (1, 1), (0, 0)))
    act_grad = jnp.zeros(latents.shape, jnp.float32)
    spatial_list = []
    for tap_row in range(3):
        for tap_col in range(3):
            shifted = grad_padded[:, 2 - tap_row:2 - tap_row + height_rows, 2 - tap_col:2 - tap_col + columns]
            act_grad = act_grad + mixed_einsum('fhwd,cd->fhwc', shifted, spatial_kernel[tap_row, tap_col])
            window = padded[:, tap_row:tap_row + height_rows, tap_col:tap_col + columns]
            spatial_list.append(mixed_einsum('fhwc,fhwd->cd', window, pre_grad))
    spatial_grad = jnp.stack(spatial_list).reshape(3, 3, channels, channels)
    norm_grad = (act_grad * silu_slope(normed)).reshape(grouped.shape)
    first_mean = lax.optimization_barrier(jnp.sum(norm_grad, axis=(1, 2, 4), keepdims=True)) / members
    second_grad = lax.optimization_barrier(jnp.sum(norm_grad * normed_grouped, axis=(1, 2, 4), keepdims=True)) / members
    input_term = inverse_std * (norm_grad - first_mean - normed_grouped * second_grad)
    input_grad = (clip_cotangent.astype(jnp.float32) + input_term.reshape(latents.shape)).astype(jnp.bfloat16)
    return (block_output, input_grad, spatial_grad, temporal_grad)

def reference(video_latents, cotangent, spatial_kernel, temporal_kernel):
    worker = partial(one_clip, spatial_kernel=spatial_kernel, temporal_kernel=temporal_kernel)
    block_output, input_grad, spatial_parts, temporal_parts = lax.map(worker, (video_latents, cotangent))
    spatial_grad = lax.optimization_barrier(jnp.sum(spatial_parts, axis=0))
    temporal_grad = lax.optimization_barrier(jnp.sum(temporal_parts, axis=0))
    grad_norm = jnp.sqrt(jnp.sum(spatial_grad * spatial_grad) + jnp.sum(temporal_grad * temporal_grad))
    clip_level = C * ROWS * COLS * math.sqrt(CLIPS * FRAMES) / CLIP_DIVISOR
    scale = clip_level / jnp.maximum(grad_norm, clip_level)
    return (block_output, input_grad, spatial_grad * scale, temporal_grad * scale)
```

```python
import math

import jax
import jax.numpy as jnp
from jax import lax
from jax.experimental import pallas as pl
from jax.experimental.pallas import tpu as pltpu
from jax.sharding import Mesh
from jax.sharding import PartitionSpec as P

GROUPS = 32
EPSILON = 1e-05
CLIP_DIVISOR = 20.0
F32 = jnp.float32
BF16 = jnp.bfloat16
DP = ("yh", "yl", "core")
TM = ("xh", "xl")
HEIGHT = ("zh", "zl")
REST = ("yh", "xh", "zh")
ORDERS = (("xl", "yl", "zl"), ("yl", "zl", "xl"), ("zl", "xl", "yl"))
VMEM = pl.BlockSpec(memory_space=pltpu.VMEM)
SMEM = pl.BlockSpec(memory_space=pltpu.SMEM)
NT = (((1,), (1,)), ((), ()))
TN = (((0,), (0,)), ((), ()))


def call(kernel, outs, args, flops, scratch=(), smem=0, limit=40):
    nbytes = sum(a.size * a.dtype.itemsize for a in (*args, *outs))
    specs = [SMEM] * smem + [VMEM] * (len(args) - smem)
    return pl.pallas_call(
        kernel,
        out_shape=tuple(outs),
        in_specs=specs,
        out_specs=tuple(VMEM for _ in outs),
        scratch_shapes=list(scratch),
        compiler_params=pltpu.CompilerParams(vmem_limit_bytes=limit << 20),
        cost_estimate=pl.CostEstimate(flops=flops, bytes_accessed=nbytes, transcendentals=0),
    )(*args)


def out(shape, dtype):
    return jax.ShapeDtypeStruct(shape, dtype)


def dot(a, b, dims=None):
    if dims is None:
        return jnp.dot(a, b, preferred_element_type=F32)
    return lax.dot_general(a, b, dims, preferred_element_type=F32)


def sigmoid(v):
    return 1.0 / (1.0 + jnp.exp(-v))


def store_stats(o_ref, sums):
    rows = []
    for first, second in sums:
        for v in (first, second):
            t = jnp.sum(v, axis=0, keepdims=True)
            rows += [t[:, :128], t[:, 128:]]
    packed = jnp.concatenate(rows, axis=0)
    for peer in range(o_ref.shape[0]):
        o_ref[peer] = packed


def group_totals(st_ref):
    tot = st_ref[0]
    for peer in range(1, st_ref.shape[0]):
        tot = tot + st_ref[peer]
    lane = lax.broadcasted_iota(jnp.int32, tot.shape, 1)
    for d in (1, 2, 4):
        low = (lane & d) == 0
        tot = tot + jnp.where(low, pltpu.roll(tot, 128 - d, 1), pltpu.roll(tot, d, 1))
    res = []
    for f in range(tot.shape[0] // 4):
        r = [tot[4 * f + k : 4 * f + k + 1] for k in range(4)]
        res.append((jnp.concatenate(r[:2], axis=1), jnp.concatenate(r[2:], axis=1)))
    return res


def moments(st_ref, members):
    res = []
    for first, second in group_totals(st_ref):
        mean = first / members
        res.append((mean, lax.rsqrt(second / members - mean * mean + EPSILON)))
    return res


def fold(v):
    return jnp.sum(v.reshape(v.shape[0] // 8, 8, v.shape[1]), axis=0)


def stats_kernel(x_ref, o_ref):
    sums = []
    for f in range(2):

        def step(r, carry):
            v = x_ref[f, pl.ds(pl.multiple_of(r * 128, 128), 128), :].astype(F32)
            return carry[0] + fold(v), carry[1] + fold(v * v)

        zero = jnp.zeros((8, 256), F32)
        sums.append(lax.fori_loop(0, 8, step, (zero, zero)))
    store_stats(o_ref, sums)


def shifted(v):
    row = lax.broadcasted_iota(jnp.int32, v.shape, 0)
    before = jnp.where(row == 0, 0.0, pltpu.roll(v, 1, 0))
    after = jnp.where(row == v.shape[0] - 1, 0.0, pltpu.roll(v, v.shape[0] - 1, 0))
    return before, after


def forward_kernel(members, info, x_ref, up_ref, dn_ref, st_ref, w_ref, act_ref, hid_ref, slope_ref):
    keep_up, keep_dn = info[4].astype(F32), info[5].astype(F32)
    stats = moments(st_ref, members)
    for f in range(2):
        mean, inv = stats[f]

        def put(v, row, keep=None):
            n = (v.astype(F32) - mean) * inv
            a = n * sigmoid(n)
            if keep is not None:
                a = a * keep
            before, after = shifted(a)
            at = pl.ds(row, 128)
            act_ref[f, at, 0:256] = before.astype(BF16)
            act_ref[f, at, 256:512] = a.astype(BF16)
            act_ref[f, at, 512:768] = after.astype(BF16)

        put(up_ref[f], 0, keep_up)
        put(dn_ref[f], 9 * 128, keep_dn)

        def line(r, _):
            at = pl.multiple_of(r * 128, 128)
            put(x_ref[f, pl.ds(at, 128), :], pl.multiple_of(at + 128, 128))
            return 0

        lax.fori_loop(0, 8, line, 0)

        def conv(r, _):
            at = pl.multiple_of(r * 256, 256)
            v = None
            for i in range(3):
                lhs = act_ref[f, pl.ds(pl.multiple_of(at + i * 128, 128), 256), :]
                part = dot(lhs, w_ref[i])
                v = part if v is None else v + part
            s = sigmoid(v)
            hid_ref[f, pl.ds(at, 256), :] = (v * s).astype(BF16)
            slope_ref[f, pl.ds(at, 256), :] = s * (1.0 + v * (1.0 - s))
            return 0

        lax.fori_loop(0, 4, conv, 0)


def pregrad_kernel(cot_ref, later_ref, slope_ref, w_ref, pg_ref, top_ref, bot_ref):
    for f in range(2):

        def part(r, _):
            at = pl.ds(pl.multiple_of(r * 256, 256), 256)
            v = None
            for k in range(3):
                g = f + 2 - k
                lhs = cot_ref[g, at, :] if g < 2 else later_ref[g - 2, at, :]
                p = dot(lhs, w_ref[k], NT)
                v = p if v is None else v + p
            pg_ref[f, at, :] = (v * slope_ref[f, at, :]).astype(BF16)
            return 0

        lax.fori_loop(0, 4, part, 0)
        top_ref[f] = pg_ref[f, 0:128, :]
        bot_ref[f] = pg_ref[f, 896:1024, :]


def grads_kernel(info, act_ref, pg_ref, hid_ref, cot_ref, later_ref, g_ref):
    def put(tap, v):
        for q in range(4):
            b = 4 * tap + q
            pair, third, bits = b // 24, (b % 24) // 8, b % 8
            at = (pair ^ info[0]) * 24 + third * 8 + (bits ^ info[1 + third])
            rh, lh = q % 2, q // 2
            g_ref[at] = v[rh * 128 : rh * 128 + 128, lh * 128 : lh * 128 + 128]

    for i in range(3):
        for j in range(3):
            v = None
            for f in range(2):
                lhs = act_ref[f, i * 128 : i * 128 + 1024, j * 256 : j * 256 + 256]
                p = dot(lhs, pg_ref[f], TN)
                v = p if v is None else v + p
            put(3 * i + j, v)
    for k in range(3):
        v = None
        for f in range(2):
            g = f + 2 - k
            rhs = cot_ref[g] if g < 2 else later_ref[g - 2]
            p = dot(hid_ref[f], rhs, TN)
            v = p if v is None else v + p
        put(9 + k, v)


def backward_kernel(members, pg_ref, up_ref, dn_ref, w_ref, x_ref, st_ref, ng_ref, o_ref, a_ref, b_ref, c_ref):
    stats = moments(st_ref, members)
    sums = []
    for f in range(2):
        mean, inv = stats[f]

        def put(v, row):
            v = v.astype(F32)
            before, after = shifted(v)
            at = pl.ds(row, 128)
            a_ref[f, at, :] = after.astype(BF16)
            b_ref[f, at, :] = v.astype(BF16)
            c_ref[f, at, :] = before.astype(BF16)

        put(up_ref[f], 0)
        put(dn_ref[f], 9 * 128)

        def line(r, _):
            at = pl.multiple_of(r * 128, 128)
            put(pg_ref[f, pl.ds(at, 128), :], pl.multiple_of(at + 128, 128))
            return 0

        lax.fori_loop(0, 8, line, 0)

        def conv(r, carry):
            at = pl.multiple_of(r * 256, 256)
            v = None
            for i in range(3):
                rows = pl.ds(pl.multiple_of(at + (2 - i) * 128, 128), 256)
                for j, ref in enumerate((a_ref, b_ref, c_ref)):
                    p = dot(ref[f, rows, :], w_ref[i, j], NT)
                    v = p if v is None else v + p
            n = (x_ref[f, pl.ds(at, 256), :].astype(F32) - mean) * inv
            s = sigmoid(n)
            ng = v * (s * (1.0 + n * (1.0 - s)))
            ng_ref[f, pl.ds(at, 256), :] = ng
            return carry[0] + fold(ng), carry[1] + fold(ng * n)

        zero = jnp.zeros((8, 256), F32)
        sums.append(lax.fori_loop(0, 4, conv, (zero, zero)))
    store_stats(o_ref, sums)


def input_grad_kernel(members, x_ref, cot_ref, ng_ref, st_ref, gst_ref, o_ref):
    stats = moments(st_ref, members)
    gstats = group_totals(gst_ref)
    for f in range(2):
        mean, inv = stats[f]
        first, second = gstats[f][0] / members, gstats[f][1] / members

        def part(r, _):
            at = pl.ds(pl.multiple_of(r * 128, 128), 128)
            n = (x_ref[f, at, :].astype(F32) - mean) * inv
            term = inv * (ng_ref[f, at, :] - first - n * second)
            o_ref[f, at, :] = (cot_ref[f, at, :].astype(F32) + term).astype(BF16)
            return 0

        lax.fori_loop(0, 8, part, 0)


def block_kernel(x_ref, hid_ref, prev_ref, w_ref, o_ref):
    for f in range(2):

        def part(r, _):
            at = pl.ds(pl.multiple_of(r * 256, 256), 256)
            v = None
            for k in range(3):
                g = f - 2 + k
                lhs = hid_ref[g, at, :] if g >= 0 else prev_ref[g + 2, at, :]
                p = dot(lhs, w_ref[k])
                v = p if v is None else v + p
            o_ref[f, at, :] = (x_ref[f, at, :].astype(F32) + v).astype(BF16)
            return 0

        lax.fori_loop(0, 4, part, 0)


def clip_kernel(clip_level, info, own_ref, other_ref, s_ref, t_ref):
    core = info[0]

    def block(tap, q):
        b = 4 * tap + q
        pair, third, bits = b // 24, (b % 24) // 8, b % 8
        at = third * 8 + (bits ^ info[1 + third])
        mine = (pair ^ core) == 0
        return jnp.where(mine, own_ref[at], other_ref[at])

    acc = jnp.zeros((8, 128), F32)
    for tap in range(12):
        ref, k = (s_ref, tap) if tap < 9 else (t_ref, tap - 9)
        for q in range(4):
            v = block(tap, q)
            rh, lh = q % 2, q // 2
            ref[k, rh * 128 : rh * 128 + 128, lh * 128 : lh * 128 + 128] = v
            acc = acc + fold(v * v)
    total = jnp.sum(jnp.sum(acc, axis=0, keepdims=True), axis=1, keepdims=True)
    scale = clip_level / jnp.maximum(jnp.sqrt(total), clip_level)

    def finish(k, _):
        s_ref[k] = s_ref[k] * scale
        return 0

    lax.fori_loop(0, 9, finish, 0)
    for k in range(3):
        t_ref[k] = t_ref[k] * scale


def swapped(x, axis):
    return lax.ppermute(x, axis, [(0, 1), (1, 0)])


def moved(x, axes, distance):
    n = lax.axis_size(axes)
    route = [(i, i + distance) for i in range(n) if 0 <= i + distance < n]
    return lax.ppermute(x, axes, route)


def reduced(g):
    g = g[:24] + swapped(g[24:], "core")
    parts = [g[8 * t : 8 * t + 8] for t in range(3)]
    for step, half in enumerate((4, 2, 1)):
        got = [swapped(p[half:], ORDERS[t][step]) for t, p in enumerate(parts)]
        parts = [p[:half] + r for p, r in zip(parts, got)]
    pieces = jnp.concatenate([p.reshape(16, 8, 128) for p in parts], axis=1)
    return jnp.sum(lax.all_to_all(pieces, REST, 0, 0, tiled=True), axis=0)


def gathered(own):
    copies = jnp.broadcast_to(own, (16, *own.shape))
    pieces = lax.all_to_all(copies, REST, 0, 0, tiled=True)
    parts = [pieces[:, 8 * t : 8 * t + 8].reshape(1, 128, 128) for t in range(3)]
    for step in (2, 1, 0):
        got = [swapped(p, ORDERS[t][step]) for t, p in enumerate(parts)]
        parts = [jnp.concatenate([p, r], axis=0) for p, r in zip(parts, got)]
    mine = jnp.concatenate(parts, axis=0)
    return mine, swapped(mine, "core")


def body(video_latents, cotangent, spatial_kernel, temporal_kernel):
    batch, frames, rows, columns, channels = video_latents.shape
    peers = lax.axis_size(HEIGHT)
    members = float(rows * peers * columns * (channels // GROUPS))
    clip_level = (
        channels * rows * peers * columns
        * math.sqrt(batch * lax.axis_size(DP) * frames * lax.axis_size(TM))
        / CLIP_DIVISOR
    )
    z = lax.axis_index(HEIGHT)
    bit = {a: lax.axis_index(a) for a in ("xl", "yl", "zl")}
    codes = [4 * bit[a] + 2 * bit[b] + bit[c] for a, b, c in ORDERS]
    info = jnp.stack(
        [lax.axis_index("core"), *codes, (z > 0).astype(jnp.int32), (z < peers - 1).astype(jnp.int32)]
    ).astype(jnp.int32)
    pixels = rows * columns
    flat = (2, pixels, 256)
    x = video_latents.reshape(flat)
    cot = cotangent.reshape(flat)
    w9 = spatial_kernel
    w3 = spatial_kernel.reshape(3, 768, 256)
    gflop = 2 * 2048 * 256 * 256

    later = moved(cot, TM, -1)
    up = moved(x[:, pixels - columns :], HEIGHT, 1)
    dn = moved(x[:, :columns], HEIGHT, -1)
    small = out((8, 8, 128), F32)
    (st,) = call(stats_kernel, [small], [x], 1 << 21)
    st = lax.all_to_all(st, HEIGHT, 0, 0, tiled=True)
    act, hid, slope = call(
        lambda *refs: forward_kernel(members, *refs),
        [out((2, 1280, 768), BF16), out(flat, BF16), out(flat, F32)],
        [info, x, up, dn, st, w3],
        9 * gflop,
        smem=1,
    )
    edge = out((2, columns, 256), BF16)
    pg, top, bot = call(
        pregrad_kernel, [out(flat, BF16), edge, edge], [cot, later, slope, temporal_kernel], 3 * gflop
    )
    gup = moved(bot, HEIGHT, 1)
    gdn = moved(top, HEIGHT, -1)
    (g,) = call(
        grads_kernel, [out((48, 128, 128), F32)], [info, act, pg, hid, cot, later], 12 * gflop, smem=1
    )
    own = reduced(g)
    mine, other = gathered(own)
    clipped_spatial, clipped_temporal = call(
        lambda *refs: clip_kernel(clip_level, *refs),
        [out((9, 256, 256), F32), out((3, 256, 256), F32)],
        [info, mine, other],
        1 << 21,
        smem=1,
    )
    ng, gst = call(
        lambda *refs: backward_kernel(members, *refs),
        [out(flat, F32), small],
        [pg, gup, gdn, w9, x, st],
        9 * gflop,
        scratch=[pltpu.VMEM((2, 1280, 256), BF16)] * 3,
    )
    gst = lax.all_to_all(gst, HEIGHT, 0, 0, tiled=True)
    (input_grad,) = call(
        lambda *refs: input_grad_kernel(members, *refs), [out(flat, BF16)], [x, cot, ng, st, gst], 1 << 21
    )
    prev = moved(hid, TM, 1)
    (block_output,) = call(block_kernel, [out(flat, BF16)], [x, hid, prev, temporal_kernel], 3 * gflop)
    return (
        block_output.reshape(video_latents.shape),
        input_grad.reshape(video_latents.shape),
        clipped_spatial.reshape(spatial_kernel.shape),
        clipped_temporal,
    )


def solution(mesh):
    torus = Mesh(mesh.devices.reshape(2, 2, 2, 2, 2, 4, 2), (*DP, *TM, *HEIGHT))
    field = P(DP, TM, HEIGHT, None, None)
    return jax.shard_map(
        body, mesh=torus, in_specs=(field, field, P(), P()), out_specs=(field, field, P(), P()), check_vma=False
    )
```

```python
import math

import jax
import jax.numpy as jnp
from jax import lax
from jax.experimental import pallas as pl
from jax.experimental.pallas import tpu as pltpu
from jax.sharding import Mesh
from jax.sharding import PartitionSpec as P

GROUPS = 32
tied = lax.optimization_barrier
EPSILON = 1e-05
CLIP_DIVISOR = 20.0
F32 = jnp.float32
BF16 = jnp.bfloat16
DP = ("yh", "yl", "core")
TM = ("xh", "xl")
HEIGHT = ("zh", "zl")
ROUNDS = (("yh", "xh"), ("zh",))
ORDERS = (("xl", "yl", "zl"), ("yl", "zl", "xl"), ("zl", "xl", "yl"))
VMEM = pl.BlockSpec(memory_space=pltpu.VMEM)
SMEM = pl.BlockSpec(memory_space=pltpu.SMEM)
NT = (((1,), (1,)), ((), ()))
TN = (((0,), (0,)), ((), ()))


def call(kernel, outs, args, flops, scratch=(), smem=0, limit=16):
    nbytes = sum(a.size * a.dtype.itemsize for a in (*args, *outs))
    specs = [SMEM] * smem + [VMEM] * (len(args) - smem)
    return pl.pallas_call(
        kernel,
        out_shape=tuple(outs),
        in_specs=specs,
        out_specs=tuple(VMEM for _ in outs),
        scratch_shapes=list(scratch),
        compiler_params=pltpu.CompilerParams(vmem_limit_bytes=limit << 20),
        cost_estimate=pl.CostEstimate(flops=flops, bytes_accessed=nbytes, transcendentals=0),
    )(*args)


def out(shape, dtype):
    return jax.ShapeDtypeStruct(shape, dtype)


def dot(a, b, dims=None):
    if dims is None:
        return jnp.dot(a, b, preferred_element_type=F32)
    return lax.dot_general(a, b, dims, preferred_element_type=F32)


def sigmoid(v):
    return 1.0 / (1.0 + jnp.exp(-v))


def store_stats(o_ref, sums):
    rows = []
    for first, second in sums:
        for v in (first, second):
            t = jnp.sum(v, axis=0, keepdims=True)
            rows += [t[:, :128], t[:, 128:]]
    packed = jnp.concatenate(rows, axis=0)
    for peer in range(o_ref.shape[0]):
        o_ref[peer] = packed


def group_totals(st_ref):
    tot = st_ref[0]
    for peer in range(1, st_ref.shape[0]):
        tot = tot + st_ref[peer]
    lane = lax.broadcasted_iota(jnp.int32, tot.shape, 1)
    for d in (1, 2, 4):
        low = (lane & d) == 0
        tot = tot + jnp.where(low, pltpu.roll(tot, 128 - d, 1), pltpu.roll(tot, d, 1))
    res = []
    for f in range(tot.shape[0] // 4):
        r = [tot[4 * f + k : 4 * f + k + 1] for k in range(4)]
        res.append((jnp.concatenate(r[:2], axis=1), jnp.concatenate(r[2:], axis=1)))
    return res


def moments(st_ref, members):
    res = []
    for first, second in group_totals(st_ref):
        mean = first / members
        res.append((mean, lax.rsqrt(second / members - mean * mean + EPSILON)))
    return res


def fold(v):
    return jnp.sum(v.reshape(v.shape[0] // 8, 8, v.shape[1]), axis=0)


def stats_kernel(x_ref, o_ref, top_ref, bot_ref):
    sums = []
    for f in range(2):
        top_ref[f] = x_ref[f, 0:128, :]
        bot_ref[f] = x_ref[f, 896:1024, :]

        def step(r, carry):
            v = x_ref[f, pl.ds(pl.multiple_of(r * 128, 128), 128), :].astype(F32)
            return carry[0] + fold(v), carry[1] + fold(v * v)

        zero = jnp.zeros((8, 256), F32)
        sums.append(lax.fori_loop(0, 8, step, (zero, zero)))
    store_stats(o_ref, sums)


def shifted(v):
    row = lax.broadcasted_iota(jnp.int32, v.shape, 0)
    before = jnp.where(row == 0, 0.0, pltpu.roll(v, 1, 0))
    after = jnp.where(row == v.shape[0] - 1, 0.0, pltpu.roll(v, v.shape[0] - 1, 0))
    return before, after


def forward_kernel(members, info, x_ref, up_ref, dn_ref, st_ref, w_ref, act_ref, hid_ref, slope_ref):
    keep_up, keep_dn = info[4].astype(F32), info[5].astype(F32)
    stats = moments(st_ref, members)
    for f in range(2):
        mean, inv = stats[f]

        def put(v, row, keep=None):
            n = (v.astype(F32) - mean) * inv
            a = n * sigmoid(n)
            if keep is not None:
                a = a * keep
            before, after = shifted(a)
            at = pl.ds(row, 128)
            act_ref[f, at, 0:256] = before.astype(BF16)
            act_ref[f, at, 256:512] = a.astype(BF16)
            act_ref[f, at, 512:768] = after.astype(BF16)

        put(up_ref[f], 0, keep_up)
        put(dn_ref[f], 9 * 128, keep_dn)

        def line(r, _):
            at = pl.multiple_of(r * 128, 128)
            put(x_ref[f, pl.ds(at, 128), :], pl.multiple_of(at + 128, 128))
            return 0

        lax.fori_loop(0, 8, line, 0)

        def conv(r, _):
            at = pl.multiple_of(r * 256, 256)
            v = None
            for i in range(3):
                lhs = act_ref[f, pl.ds(pl.multiple_of(at + i * 128, 128), 256), :]
                part = dot(lhs, w_ref[i])
                v = part if v is None else v + part
            s = sigmoid(v)
            hid_ref[f, pl.ds(at, 256), :] = (v * s).astype(BF16)
            slope_ref[f, pl.ds(at, 256), :] = s * (1.0 + v * (1.0 - s))
            return 0

        lax.fori_loop(0, 4, conv, 0)


def pregrad_kernel(cot_ref, later_ref, slope_ref, w_ref, pg_ref, top_ref, bot_ref):
    for f in range(2):

        def part(r, _):
            at = pl.ds(pl.multiple_of(r * 256, 256), 256)
            v = None
            for k in range(3):
                g = f + 2 - k
                lhs = cot_ref[g, at, :] if g < 2 else later_ref[g - 2, at, :]
                p = dot(lhs, w_ref[k], NT)
                v = p if v is None else v + p
            pg_ref[f, at, :] = (v * slope_ref[f, at, :]).astype(BF16)
            return 0

        lax.fori_loop(0, 4, part, 0)
        top_ref[f] = pg_ref[f, 0:128, :]
        bot_ref[f] = pg_ref[f, 896:1024, :]


def row_places(info):
    return [
        pl.multiple_of((((s // 4) ^ info[6]) * 4 + ((s % 4) ^ info[7])) * 8, 8) for s in range(16)
    ]


def grads_kernel(info, act_ref, pg_ref, hid_ref, cot_ref, later_ref, g_ref):
    places = row_places(info)

    def put(tap, v):
        for q in range(4):
            b = 4 * tap + q
            pair, third, bits = b // 24, (b % 24) // 8, b % 8
            at = (pair ^ info[0]) * 24 + third * 8 + (bits ^ info[1 + third])
            rh, lh = q % 2, q // 2
            for s in range(16):
                row = rh * 128 + s * 8
                g_ref[at, pl.ds(places[s], 8), :] = v[row : row + 8, lh * 128 : lh * 128 + 128]

    for i in range(3):
        for j in range(3):
            v = None
            for f in range(2):
                lhs = act_ref[f, i * 128 : i * 128 + 1024, j * 256 : j * 256 + 256]
                p = dot(lhs, pg_ref[f], TN)
                v = p if v is None else v + p
            put(3 * i + j, v)
    for k in range(3):
        v = None
        for f in range(2):
            g = f + 2 - k
            rhs = cot_ref[g] if g < 2 else later_ref[g - 2]
            p = dot(hid_ref[f], rhs, TN)
            v = p if v is None else v + p
        put(9 + k, v)


def backward_kernel(members, pg_ref, up_ref, dn_ref, w_ref, x_ref, st_ref, ng_ref, o_ref, a_ref, b_ref, c_ref):
    stats = moments(st_ref, members)
    sums = []
    for f in range(2):
        mean, inv = stats[f]

        def put(v, row):
            v = v.astype(F32)
            before, after = shifted(v)
            at = pl.ds(row, 128)
            a_ref[f, at, :] = after.astype(BF16)
            b_ref[f, at, :] = v.astype(BF16)
            c_ref[f, at, :] = before.astype(BF16)

        put(up_ref[f], 0)
        put(dn_ref[f], 9 * 128)

        def line(r, _):
            at = pl.multiple_of(r * 128, 128)
            put(pg_ref[f, pl.ds(at, 128), :], pl.multiple_of(at + 128, 128))
            return 0

        lax.fori_loop(0, 8, line, 0)

        def conv(r, carry):
            at = pl.multiple_of(r * 256, 256)
            v = None
            for i in range(3):
                rows = pl.ds(pl.multiple_of(at + (2 - i) * 128, 128), 256)
                for j, ref in enumerate((a_ref, b_ref, c_ref)):
                    p = dot(ref[f, rows, :], w_ref[i, j], NT)
                    v = p if v is None else v + p
            n = (x_ref[f, pl.ds(at, 256), :].astype(F32) - mean) * inv
            s = sigmoid(n)
            ng = v * (s * (1.0 + n * (1.0 - s)))
            ng_ref[f, pl.ds(at, 256), :] = ng
            return carry[0] + fold(ng), carry[1] + fold(ng * n)

        zero = jnp.zeros((8, 256), F32)
        sums.append(lax.fori_loop(0, 4, conv, (zero, zero)))
    store_stats(o_ref, sums)


def input_grad_kernel(members, x_ref, cot_ref, ng_ref, st_ref, gst_ref, o_ref):
    stats = moments(st_ref, members)
    gstats = group_totals(gst_ref)
    for f in range(2):
        mean, inv = stats[f]
        first, second = gstats[f][0] / members, gstats[f][1] / members

        def part(r, _):
            at = pl.ds(pl.multiple_of(r * 128, 128), 128)
            n = (x_ref[f, at, :].astype(F32) - mean) * inv
            term = inv * (ng_ref[f, at, :] - first - n * second)
            o_ref[f, at, :] = (cot_ref[f, at, :].astype(F32) + term).astype(BF16)
            return 0

        lax.fori_loop(0, 8, part, 0)


def block_kernel(x_ref, hid_ref, prev_ref, w_ref, o_ref):
    for f in range(2):

        def part(r, _):
            at = pl.ds(pl.multiple_of(r * 256, 256), 256)
            v = None
            for k in range(3):
                g = f - 2 + k
                lhs = hid_ref[g, at, :] if g >= 0 else prev_ref[g + 2, at, :]
                p = dot(lhs, w_ref[k])
                v = p if v is None else v + p
            o_ref[f, at, :] = (x_ref[f, at, :].astype(F32) + v).astype(BF16)
            return 0

        lax.fori_loop(0, 4, part, 0)


def clip_kernel(clip_level, info, *refs):
    s_ref, t_ref = refs[12:]
    places = row_places(info)
    acc = jnp.zeros((8, 128), F32)
    for tap in range(12):
        ref, k = (s_ref, tap) if tap < 9 else (t_ref, tap - 9)
        for q in range(4):
            b = 4 * tap + q
            pair, third, bits = b // 24, (b % 24) // 8, b % 8
            at = bits ^ info[1 + third]
            low, slot = at < 4, at & 3
            mine = (pair ^ info[0]) == 0
            rh, lh = q % 2, q // 2
            for s in range(16):
                rows = pl.ds(places[s], 8)
                own_low, own_high, low_ref, high_ref = refs[4 * third : 4 * third + 4]
                v = jnp.where(
                    mine,
                    jnp.where(low, own_low[slot, rows, :], own_high[slot, rows, :]),
                    jnp.where(low, low_ref[slot, rows, :], high_ref[slot, rows, :]),
                )
                row = rh * 128 + s * 8
                ref[k, row : row + 8, lh * 128 : lh * 128 + 128] = v
                acc = acc + v * v
    total = jnp.sum(jnp.sum(acc, axis=0, keepdims=True), axis=1, keepdims=True)
    scale = clip_level / jnp.maximum(jnp.sqrt(total), clip_level)

    def finish(k, _):
        s_ref[k] = s_ref[k] * scale
        return 0

    lax.fori_loop(0, 9, finish, 0)
    for k in range(3):
        t_ref[k] = t_ref[k] * scale


def in_hbm(x):
    return pltpu.with_memory_space_constraint(x, pltpu.HBM)


def swapped(x, axis):
    return lax.ppermute(x, axis, [(0, 1), (1, 0)])


def moved(x, axes, distance):
    n = lax.axis_size(axes)
    route = [(i, i + distance) for i in range(n) if 0 <= i + distance < n]
    return lax.ppermute(x, axes, route)


def others(pieces, axes):
    n = lax.axis_size(axes)
    return [
        lax.ppermute(pieces(d), axes, [(i, i ^ d) for i in range(n)]) for d in range(1, n)
    ]


def halved(parts, step):
    half = parts[0].shape[0] // 2
    keep, send = tied(([p[:half] for p in parts], [p[half:] for p in parts]))
    got = tied([swapped(p, ORDERS[t][step]) for t, p in enumerate(send)])
    return [p + r for p, r in zip(keep, got)]


def doubled(parts, step):
    return tied([swapped(p, ORDERS[t][step]) for t, p in enumerate(parts)])


def quartered(m, axes):
    m = m.reshape(3, 4, m.shape[1] // 4, 128)
    total = m[:, 0]
    for r in others(lambda d: m[:, d], axes):
        total = total + r
    return total


def spread(m, axes):
    pieces = [m, *others(lambda d: m, axes)]
    return jnp.stack(pieces, axis=1).reshape(3, 4 * m.shape[1], 128)


def body(video_latents, cotangent, spatial_kernel, temporal_kernel):
    batch, frames, rows, columns, channels = video_latents.shape
    peers = lax.axis_size(HEIGHT)
    members = float(rows * peers * columns * (channels // GROUPS))
    clip_level = (
        channels * rows * peers * columns
        * math.sqrt(batch * lax.axis_size(DP) * frames * lax.axis_size(TM))
        / CLIP_DIVISOR
    )
    z = lax.axis_index(HEIGHT)
    bit = {a: lax.axis_index(a) for a in ("xl", "yl", "zl")}
    codes = [4 * bit[a] + 2 * bit[b] + bit[c] for a, b, c in ORDERS]
    info = jnp.stack(
        [
            lax.axis_index("core"),
            *codes,
            (z > 0).astype(jnp.int32),
            (z < peers - 1).astype(jnp.int32),
            *[lax.axis_index(axes) for axes in ROUNDS],
        ]
    ).astype(jnp.int32)
    pixels = rows * columns
    flat = (2, pixels, 256)
    x = video_latents.reshape(flat)
    cot = cotangent.reshape(flat)
    w9 = spatial_kernel
    w3 = spatial_kernel.reshape(3, 768, 256)
    gflop = 2 * 2048 * 256 * 256

    later = moved(cot, TM, -1)
    small = out((8, 8, 128), F32)
    edge = out((2, columns, 256), BF16)
    st, x_top, x_bot = call(stats_kernel, [small, edge, edge], [x], 1 << 21)
    st = in_hbm(lax.all_to_all(st, HEIGHT, 0, 0, tiled=True))
    up = in_hbm(moved(x_bot, HEIGHT, 1))
    dn = in_hbm(moved(x_top, HEIGHT, -1))
    act, hid, slope = call(
        lambda *refs: forward_kernel(members, *refs),
        [out((2, 1280, 768), BF16), out(flat, BF16), out(flat, F32)],
        [info, x, up, dn, st, w3],
        9 * gflop,
        smem=1,
    )
    pg, top, bot = call(
        pregrad_kernel, [out(flat, BF16), edge, edge], [cot, later, slope, temporal_kernel], 3 * gflop
    )
    gup = moved(bot, HEIGHT, 1)
    gdn = moved(top, HEIGHT, -1)
    (g,) = call(
        grads_kernel, [out((48, 128, 128), F32)], [info, act, pg, hid, cot, later], 12 * gflop, smem=1
    )
    g, gup, gdn = tied((g, gup, gdn))
    g = g[:24] + swapped(g[24:], "core")
    parts = halved([g[8 * t : 8 * t + 8] for t in range(3)], 0)
    ng, gst = call(
        lambda *refs: backward_kernel(members, *refs),
        [out(flat, F32), small],
        [pg, gup, gdn, w9, x, st],
        9 * gflop,
        scratch=[pltpu.VMEM((2, 1280, 256), BF16)] * 3,
    )
    parts, ng, gst = tied((parts, ng, gst))
    gst = in_hbm(lax.all_to_all(gst, HEIGHT, 0, 0, tiled=True))
    parts = halved(parts, 1)
    parts = halved(parts, 2)
    parts, hid_sent, gst = tied((parts, hid, gst))
    prev = moved(hid_sent, TM, 1)
    own = quartered(jnp.concatenate(parts, axis=0), ROUNDS[0])
    own = quartered(own, ROUNDS[1])
    (input_grad,) = call(
        lambda *refs: input_grad_kernel(members, *refs), [out(flat, BF16)], [x, cot, ng, st, gst], 1 << 21
    )
    full = spread(own, ROUNDS[1])
    full, input_grad = tied((full, input_grad))
    full = spread(full, ROUNDS[0])
    parts = [full[t : t + 1] for t in range(3)]
    parts = [jnp.concatenate([p, r]) for p, r in zip(parts, doubled(parts, 2))]
    (block_output,) = call(block_kernel, [out(flat, BF16)], [x, hid, prev, temporal_kernel], 3 * gflop)
    parts, block_output = tied((parts, block_output))
    parts = [jnp.concatenate([p, r]) for p, r in zip(parts, doubled(parts, 1))]
    high = doubled(parts, 0)
    pieces = []
    for p, h in zip(parts, high):
        pieces += [p, h, swapped(p, "core"), swapped(h, "core")]
    clipped_spatial, clipped_temporal = call(
        lambda *refs: clip_kernel(clip_level, *refs),
        [out((9, 256, 256), F32), out((3, 256, 256), F32)],
        [info, *pieces],
        1 << 21,
        smem=1,
    )
    return (
        block_output.reshape(video_latents.shape),
        input_grad.reshape(video_latents.shape),
        clipped_spatial.reshape(spatial_kernel.shape),
        clipped_temporal,
    )


def solution(mesh):
    torus = Mesh(mesh.devices.reshape(2, 2, 2, 2, 2, 4, 2), (*DP, *TM, *HEIGHT))
    field = P(DP, TM, HEIGHT, None, None)
    return jax.shard_map(
        body, mesh=torus, in_specs=(field, field, P(), P()), out_specs=(field, field, P(), P()), check_vma=False
    )
```

```python
import math

import jax
import jax.numpy as jnp
from jax import lax
from jax.experimental import pallas as pl
from jax.experimental.pallas import tpu as pltpu
from jax.sharding import Mesh
from jax.sharding import PartitionSpec as P

GROUPS = 32
tied = lax.optimization_barrier
EPSILON = 1e-05
CLIP_DIVISOR = 20.0
F32 = jnp.float32
BF16 = jnp.bfloat16
DP = ("y", "core")
TM = "tm"
HEIGHT = "height"
CHIPS = ("y", "tm", "height")
UNIT = 2.0**40
VMEM = pl.BlockSpec(memory_space=pltpu.VMEM)
SMEM = pl.BlockSpec(memory_space=pltpu.SMEM)
ANY = pl.BlockSpec(memory_space=pl.ANY)
NT = (((1,), (1,)), ((), ()))
TN = (((0,), (0,)), ((), ()))


def call(kernel, outs, args, flops, scratch=(), smem=0, limit=16, loose=()):
    nbytes = sum(a.size * a.dtype.itemsize for a in (*args, *outs))
    specs = [SMEM] * smem + [ANY if i in loose else VMEM for i in range(smem, len(args))]
    return pl.pallas_call(
        kernel,
        out_shape=tuple(outs),
        in_specs=specs,
        out_specs=tuple(VMEM for _ in outs),
        scratch_shapes=list(scratch),
        compiler_params=pltpu.CompilerParams(vmem_limit_bytes=limit << 20),
        cost_estimate=pl.CostEstimate(flops=flops, bytes_accessed=nbytes, transcendentals=0),
    )(*args)


def out(shape, dtype):
    return jax.ShapeDtypeStruct(shape, dtype)


def dot(a, b, dims=None):
    if dims is None:
        return jnp.dot(a, b, preferred_element_type=F32)
    return lax.dot_general(a, b, dims, preferred_element_type=F32)


def sigmoid(v):
    return 1.0 / (1.0 + jnp.exp(-v))


def store_stats(o_ref, sums):
    rows = []
    for first, second in sums:
        for v in (first, second):
            t = jnp.sum(v, axis=0, keepdims=True)
            rows += [t[:, :128], t[:, 128:]]
    packed = jnp.concatenate(rows, axis=0)
    for peer in range(o_ref.shape[0]):
        o_ref[peer] = packed


def group_totals(st_ref):
    tot = st_ref[0]
    for peer in range(1, st_ref.shape[0]):
        tot = tot + st_ref[peer]
    lane = lax.broadcasted_iota(jnp.int32, tot.shape, 1)
    for d in (1, 2, 4):
        low = (lane & d) == 0
        tot = tot + jnp.where(low, pltpu.roll(tot, 128 - d, 1), pltpu.roll(tot, d, 1))
    res = []
    for f in range(tot.shape[0] // 4):
        r = [tot[4 * f + k : 4 * f + k + 1] for k in range(4)]
        res.append((jnp.concatenate(r[:2], axis=1), jnp.concatenate(r[2:], axis=1)))
    return res


def moments(st_ref, members):
    res = []
    for first, second in group_totals(st_ref):
        mean = first / members
        res.append((mean, lax.rsqrt(second / members - mean * mean + EPSILON)))
    return res


def fetched(*pairs, sems):
    copies = [pltpu.make_async_copy(a, b, sems.at[i]) for i, (a, b) in enumerate(pairs)]
    for c in copies:
        c.start()
    for c in copies:
        c.wait()


def fold(v):
    return jnp.sum(v.reshape(v.shape[0] // 8, 8, v.shape[1]), axis=0)


def stats_kernel(x_ref, o_ref, top_ref, bot_ref):
    sums = []
    for f in range(2):
        top_ref[f] = x_ref[f, 0:128, :]
        bot_ref[f] = x_ref[f, 896:1024, :]

        def step(r, carry):
            v = x_ref[f, pl.ds(pl.multiple_of(r * 128, 128), 128), :].astype(F32)
            return carry[0] + fold(v), carry[1] + fold(v * v)

        zero = jnp.zeros((8, 256), F32)
        sums.append(lax.fori_loop(0, 8, step, (zero, zero)))
    store_stats(o_ref, sums)


def shifted(v):
    row = lax.broadcasted_iota(jnp.int32, v.shape, 0)
    before = jnp.where(row == 0, 0.0, pltpu.roll(v, 1, 0))
    after = jnp.where(row == v.shape[0] - 1, 0.0, pltpu.roll(v, v.shape[0] - 1, 0))
    return before, after


def forward_kernel(
    members, info, x_ref, up_hbm, dn_hbm, st_hbm, w_ref, act_ref, hid_ref, slope_ref, up_ref, dn_ref, st_ref, sems
):
    fetched((st_hbm, st_ref), (up_hbm, up_ref), (dn_hbm, dn_ref), sems=sems)
    keep_up = (info[1] > 0).astype(F32)
    keep_dn = (info[2] > 0).astype(F32)
    stats = moments(st_ref, members)
    for f in range(2):
        mean, inv = stats[f]

        def put(v, row, keep=None):
            n = (v.astype(F32) - mean) * inv
            a = n * sigmoid(n)
            if keep is not None:
                a = a * keep
            before, after = shifted(a)
            at = pl.ds(row, 128)
            act_ref[f, at, 0:256] = before.astype(BF16)
            act_ref[f, at, 256:512] = a.astype(BF16)
            act_ref[f, at, 512:768] = after.astype(BF16)

        put(up_ref[f], 0, keep_up)
        put(dn_ref[f], 9 * 128, keep_dn)

        def line(r, _):
            at = pl.multiple_of(r * 128, 128)
            put(x_ref[f, pl.ds(at, 128), :], pl.multiple_of(at + 128, 128))
            return 0

        lax.fori_loop(0, 8, line, 0)

        def conv(r, _):
            at = pl.multiple_of(r * 256, 256)
            v = None
            for i in range(3):
                lhs = act_ref[f, pl.ds(pl.multiple_of(at + i * 128, 128), 256), :]
                part = dot(lhs, w_ref[i])
                v = part if v is None else v + part
            s = sigmoid(v)
            hid_ref[f, pl.ds(at, 256), :] = (v * s).astype(BF16)
            slope_ref[f, pl.ds(at, 256), :] = s * (1.0 + v * (1.0 - s))
            return 0

        lax.fori_loop(0, 4, conv, 0)


def pregrad_kernel(cot_ref, later_ref, slope_ref, w_ref, pg_ref, top_ref, bot_ref):
    for f in range(2):

        def part(r, _):
            at = pl.ds(pl.multiple_of(r * 256, 256), 256)
            v = None
            for k in range(3):
                g = f + 2 - k
                lhs = cot_ref[g, at, :] if g < 2 else later_ref[g - 2, at, :]
                p = dot(lhs, w_ref[k], NT)
                v = p if v is None else v + p
            pg_ref[f, at, :] = (v * slope_ref[f, at, :]).astype(BF16)
            return 0

        lax.fori_loop(0, 4, part, 0)
        top_ref[f] = pg_ref[f, 0:128, :]
        bot_ref[f] = pg_ref[f, 896:1024, :]


def grads_kernel(info, act_ref, pg_ref, hid_ref, cot_ref, later_ref, keep_ref, send_ref):
    def put(tap, v):
        mine = info[0] == tap // 6
        for lh in range(2):
            at = ((tap % 6) * 2 + lh) * 256
            half = v[:, lh * 128 : lh * 128 + 128]

            @pl.when(mine)
            def _():
                keep_ref[at : at + 256, :] = half

            @pl.when(jnp.logical_not(mine))
            def _():
                send_ref[at : at + 256, :] = half

    for i in range(3):
        for j in range(3):
            v = None
            for f in range(2):
                lhs = act_ref[f, i * 128 : i * 128 + 1024, j * 256 : j * 256 + 256]
                p = dot(lhs, pg_ref[f], TN)
                v = p if v is None else v + p
            put(3 * i + j, v)
    for k in range(3):
        v = None
        for f in range(2):
            g = f + 2 - k
            rhs = cot_ref[g] if g < 2 else later_ref[g - 2]
            p = dot(hid_ref[f], rhs, TN)
            v = p if v is None else v + p
        put(9 + k, v)


def backward_kernel(members, pg_ref, up_ref, dn_ref, w_ref, x_ref, st_ref, ng_ref, o_ref, a_ref, b_ref, c_ref):
    stats = moments(st_ref, members)
    sums = []
    for f in range(2):
        mean, inv = stats[f]

        def put(v, row):
            v = v.astype(F32)
            before, after = shifted(v)
            at = pl.ds(row, 128)
            a_ref[f, at, :] = after.astype(BF16)
            b_ref[f, at, :] = v.astype(BF16)
            c_ref[f, at, :] = before.astype(BF16)

        put(up_ref[f], 0)
        put(dn_ref[f], 9 * 128)

        def line(r, _):
            at = pl.multiple_of(r * 128, 128)
            put(pg_ref[f, pl.ds(at, 128), :], pl.multiple_of(at + 128, 128))
            return 0

        lax.fori_loop(0, 8, line, 0)

        def conv(r, carry):
            at = pl.multiple_of(r * 256, 256)
            v = None
            for i in range(3):
                rows = pl.ds(pl.multiple_of(at + (2 - i) * 128, 128), 256)
                for j, ref in enumerate((a_ref, b_ref, c_ref)):
                    p = dot(ref[f, rows, :], w_ref[i, j], NT)
                    v = p if v is None else v + p
            n = (x_ref[f, pl.ds(at, 256), :].astype(F32) - mean) * inv
            s = sigmoid(n)
            ng = v * (s * (1.0 + n * (1.0 - s)))
            ng_ref[f, pl.ds(at, 256), :] = ng
            return carry[0] + fold(ng), carry[1] + fold(ng * n)

        zero = jnp.zeros((8, 256), F32)
        sums.append(lax.fori_loop(0, 4, conv, (zero, zero)))
    store_stats(o_ref, sums)


def input_grad_kernel(members, x_ref, cot_ref, ng_ref, st_ref, gst_ref, o_ref):
    stats = moments(st_ref, members)
    gstats = group_totals(gst_ref)
    for f in range(2):
        mean, inv = stats[f]
        first, second = gstats[f][0] / members, gstats[f][1] / members

        def part(r, _):
            at = pl.ds(pl.multiple_of(r * 128, 128), 128)
            n = (x_ref[f, at, :].astype(F32) - mean) * inv
            term = inv * (ng_ref[f, at, :] - first - n * second)
            o_ref[f, at, :] = (cot_ref[f, at, :].astype(F32) + term).astype(BF16)
            return 0

        lax.fori_loop(0, 8, part, 0)


def block_kernel(x_ref, hid_ref, prev_ref, w_ref, o_ref):
    for f in range(2):

        def part(r, _):
            at = pl.ds(pl.multiple_of(r * 256, 256), 256)
            v = None
            for k in range(3):
                g = f - 2 + k
                lhs = hid_ref[g, at, :] if g >= 0 else prev_ref[g + 2, at, :]
                p = dot(lhs, w_ref[k])
                v = p if v is None else v + p
            o_ref[f, at, :] = (x_ref[f, at, :].astype(F32) + v).astype(BF16)
            return 0

        lax.fori_loop(0, 4, part, 0)


def coded(v):
    t = v * UNIT
    return (t * jnp.sqrt(jnp.abs(t))).astype(BF16)


def decoded(u):
    u = u.astype(F32)
    size = jnp.abs(u)
    root = jnp.exp(jnp.log(jnp.maximum(size, 1e-37)) * (2.0 / 3.0)) * (1.0 / UNIT)
    return jnp.where(size < 1e-37, 0.0, jnp.where(u < 0, -root, root))


def encode_kernel(a_ref, b_ref, o_ref):
    def part(r, _):
        at = pl.ds(pl.multiple_of(r * 256, 256), 256)
        o_ref[at, :] = coded(a_ref[at, :] + b_ref[at, :])
        return 0

    lax.fori_loop(0, a_ref.shape[0] // 256, part, 0)


def own_kernel(u_ref, o_ref):
    rows = u_ref.shape[0] // 64

    def part(r, acc):
        return acc + decoded(u_ref[pl.ds(pl.multiple_of(r * rows, rows), rows), :])

    acc = lax.fori_loop(0, 64, part, jnp.zeros((rows, 128), F32))
    total = acc[: rows // 2] + acc[rows // 2 :]
    copy = coded(jnp.concatenate([total, total], axis=0))

    def put(r, _):
        o_ref[pl.ds(pl.multiple_of(r * rows, rows), rows), :] = copy
        return 0

    lax.fori_loop(0, 64, put, 0)


def clip_kernel(clip_level, info, own_ref, other_ref, s_ref, t_ref):
    acc = jnp.zeros((8, 128), F32)
    for tap in range(12):
        ref, k = (s_ref, tap) if tap < 9 else (t_ref, tap - 9)
        mine = info[0] == tap // 6
        for lh in range(2):
            at = ((tap % 6) * 2 + lh) * 256
            v = decoded(jnp.where(mine, own_ref[at : at + 256, :], other_ref[at : at + 256, :]))
            ref[k, :, lh * 128 : lh * 128 + 128] = v
            acc = acc + fold(v * v)
    total = jnp.sum(jnp.sum(acc, axis=0, keepdims=True), axis=1, keepdims=True)
    scale = clip_level / jnp.maximum(jnp.sqrt(total), clip_level)

    def finish(k, _):
        s_ref[k] = s_ref[k] * scale
        return 0

    lax.fori_loop(0, 9, finish, 0)
    for k in range(3):
        t_ref[k] = t_ref[k] * scale


def swapped(x, axis):
    return lax.ppermute(x, axis, [(0, 1), (1, 0)])


def moved(x, axes, distance):
    n = lax.axis_size(axes)
    route = [(i, i + distance) for i in range(n) if 0 <= i + distance < n]
    return lax.ppermute(x, axes, route)


def body(video_latents, cotangent, spatial_kernel, temporal_kernel):
    batch, frames, rows, columns, channels = video_latents.shape
    peers = lax.axis_size(HEIGHT)
    members = float(rows * peers * columns * (channels // GROUPS))
    clip_level = (
        channels * rows * peers * columns
        * math.sqrt(batch * lax.axis_size(DP) * frames * lax.axis_size(TM))
        / CLIP_DIVISOR
    )
    z = lax.axis_index(HEIGHT)
    info = jnp.stack([lax.axis_index("core"), z, peers - 1 - z]).astype(jnp.int32)
    pixels = rows * columns
    flat = (2, pixels, 256)
    x = video_latents.reshape(flat)
    cot = cotangent.reshape(flat)
    w9 = spatial_kernel
    w3 = spatial_kernel.reshape(3, 768, 256)
    gflop = 2 * 2048 * 256 * 256

    later = moved(cot, TM, -1)
    small = out((8, 8, 128), F32)
    edge = out((2, columns, 256), BF16)
    st, x_top, x_bot = call(stats_kernel, [small, edge, edge], [x], 1 << 21)
    st = lax.all_to_all(st, HEIGHT, 0, 0, tiled=True)
    up = moved(x_bot, HEIGHT, 1)
    dn = moved(x_top, HEIGHT, -1)
    act, hid, slope = call(
        lambda *refs: forward_kernel(members, *refs),
        [out((2, 1280, 768), BF16), out(flat, BF16), out(flat, F32)],
        [info, x, up, dn, st, w3],
        9 * gflop,
        smem=1,
        loose=(2, 3, 4),
        scratch=[
            pltpu.VMEM(edge.shape, BF16),
            pltpu.VMEM(edge.shape, BF16),
            pltpu.VMEM(small.shape, F32),
            pltpu.SemaphoreType.DMA((3,)),
        ],
    )
    pg, top, bot = call(
        pregrad_kernel, [out(flat, BF16), edge, edge], [cot, later, slope, temporal_kernel], 3 * gflop
    )
    gup = moved(bot, HEIGHT, 1)
    gdn = moved(top, HEIGHT, -1)
    slab = (3072, 128)
    keep, send = call(
        grads_kernel,
        [out(slab, F32), out(slab, F32)],
        [info, act, pg, hid, cot, later],
        12 * gflop,
        smem=1,
    )
    send, gup, gdn = tied((send, gup, gdn))
    (code,) = call(encode_kernel, [out(slab, BF16)], [keep, swapped(send, "core")], 1 << 21)
    code, gup, gdn, hid_sent = tied((code, gup, gdn, hid))
    code = lax.all_to_all(code.reshape(128, 24, 128), CHIPS, 0, 0, tiled=True)
    ng, gst = call(
        lambda *refs: backward_kernel(members, *refs),
        [out(flat, F32), out((1, 8, 128), F32)],
        [pg, gup, gdn, w9, x, st],
        9 * gflop,
        scratch=[pltpu.VMEM((2, 1280, 256), BF16)] * 3,
    )
    for d in (1, 2, 4):
        gst = gst + lax.ppermute(gst, HEIGHT, [(i, i ^ d) for i in range(peers)])
    prev = moved(hid_sent, TM, 1)
    code, ng, gst, prev = tied((code, ng, gst, prev))
    (copies,) = call(own_kernel, [out(slab, BF16)], [code.reshape(slab)], 1 << 21)
    mine = lax.all_to_all(copies.reshape(128, 24, 128), CHIPS, 0, 0, tiled=True)
    (input_grad,) = call(
        lambda *refs: input_grad_kernel(members, *refs), [out(flat, BF16)], [x, cot, ng, st, gst], 1 << 21
    )
    (block_output,) = call(block_kernel, [out(flat, BF16)], [x, hid, prev, temporal_kernel], 3 * gflop)
    mine, input_grad, block_output = tied((mine, input_grad, block_output))
    mine = mine.reshape(slab)
    clipped_spatial, clipped_temporal = call(
        lambda *refs: clip_kernel(clip_level, *refs),
        [out((9, 256, 256), F32), out((3, 256, 256), F32)],
        [info, mine, swapped(mine, "core")],
        1 << 21,
        smem=1,
    )
    return (
        block_output.reshape(video_latents.shape),
        input_grad.reshape(video_latents.shape),
        clipped_spatial.reshape(spatial_kernel.shape),
        clipped_temporal,
    )


def solution(mesh):
    sizes = (mesh.shape["dp"] // 2, 2, mesh.shape[TM], mesh.shape[HEIGHT])
    torus = Mesh(mesh.devices.reshape(sizes), (*DP, TM, HEIGHT))
    field = P(DP, TM, HEIGHT, None, None)
    return jax.shard_map(
        body, mesh=torus, in_specs=(field, field, P(), P()), out_specs=(field, field, P(), P()), check_vma=False
    )
```

```python
import math

import jax
import jax.numpy as jnp
from jax import lax
from jax.experimental import pallas as pl
from jax.experimental.pallas import tpu as pltpu
from jax.sharding import Mesh
from jax.sharding import PartitionSpec as P

GROUPS = 32
tied = lax.optimization_barrier
EPSILON = 1e-05
CLIP_DIVISOR = 20.0
F32 = jnp.float32
BF16 = jnp.bfloat16
DP = ("y", "core")
TM = "tm"
HEIGHT = "height"
UNIT = 2.0**40
VMEM = pl.BlockSpec(memory_space=pltpu.VMEM)
SMEM = pl.BlockSpec(memory_space=pltpu.SMEM)
ANY = pl.BlockSpec(memory_space=pl.ANY)
NT = (((1,), (1,)), ((), ()))
TN = (((0,), (0,)), ((), ()))


def call(kernel, outs, args, flops, scratch=(), smem=0, limit=16, loose=()):
    nbytes = sum(a.size * a.dtype.itemsize for a in (*args, *outs))
    specs = [SMEM] * smem + [ANY if i in loose else VMEM for i in range(smem, len(args))]
    return pl.pallas_call(
        kernel,
        out_shape=tuple(outs),
        in_specs=specs,
        out_specs=tuple(VMEM for _ in outs),
        scratch_shapes=list(scratch),
        compiler_params=pltpu.CompilerParams(vmem_limit_bytes=limit << 20),
        cost_estimate=pl.CostEstimate(flops=flops, bytes_accessed=nbytes, transcendentals=0),
    )(*args)


def out(shape, dtype):
    return jax.ShapeDtypeStruct(shape, dtype)


def dot(a, b, dims=None):
    if dims is None:
        return jnp.dot(a, b, preferred_element_type=F32)
    return lax.dot_general(a, b, dims, preferred_element_type=F32)


def sigmoid(v):
    return 1.0 / (1.0 + jnp.exp(-v))


def store_stats(o_ref, sums):
    rows = []
    for first, second in sums:
        for v in (first, second):
            t = jnp.sum(v, axis=0, keepdims=True)
            rows += [t[:, :128], t[:, 128:]]
    packed = jnp.concatenate(rows, axis=0)
    for peer in range(o_ref.shape[0]):
        o_ref[peer] = packed


def group_totals(st_ref):
    tot = st_ref[0]
    for peer in range(1, st_ref.shape[0]):
        tot = tot + st_ref[peer]
    lane = lax.broadcasted_iota(jnp.int32, tot.shape, 1)
    for d in (1, 2, 4):
        low = (lane & d) == 0
        tot = tot + jnp.where(low, pltpu.roll(tot, 128 - d, 1), pltpu.roll(tot, d, 1))
    res = []
    for f in range(tot.shape[0] // 4):
        r = [tot[4 * f + k : 4 * f + k + 1] for k in range(4)]
        res.append((jnp.concatenate(r[:2], axis=1), jnp.concatenate(r[2:], axis=1)))
    return res


def moments(st_ref, members):
    res = []
    for first, second in group_totals(st_ref):
        mean = first / members
        res.append((mean, lax.rsqrt(second / members - mean * mean + EPSILON)))
    return res


def fetched(*pairs, sems):
    copies = [pltpu.make_async_copy(a, b, sems.at[i]) for i, (a, b) in enumerate(pairs)]
    for c in copies:
        c.start()
    for c in copies:
        c.wait()


def fold(v):
    return jnp.sum(v.reshape(v.shape[0] // 8, 8, v.shape[1]), axis=0)


def stats_kernel(x_ref, o_ref, top_ref, bot_ref):
    sums = []
    for f in range(2):
        top_ref[f] = x_ref[f, 0:128, :]
        bot_ref[f] = x_ref[f, 896:1024, :]

        def step(r, carry):
            v = x_ref[f, pl.ds(pl.multiple_of(r * 128, 128), 128), :].astype(F32)
            return carry[0] + fold(v), carry[1] + fold(v * v)

        zero = jnp.zeros((8, 256), F32)
        sums.append(lax.fori_loop(0, 8, step, (zero, zero)))
    store_stats(o_ref, sums)


def shifted(v):
    row = lax.broadcasted_iota(jnp.int32, v.shape, 0)
    before = jnp.where(row == 0, 0.0, pltpu.roll(v, 1, 0))
    after = jnp.where(row == v.shape[0] - 1, 0.0, pltpu.roll(v, v.shape[0] - 1, 0))
    return before, after


def forward_kernel(
    members, info, x_ref, up_hbm, dn_hbm, st_hbm, w_ref, act_ref, hid_ref, slope_ref, up_ref, dn_ref, st_ref, sems
):
    fetched((st_hbm, st_ref), (up_hbm, up_ref), (dn_hbm, dn_ref), sems=sems)
    keep_up = (info[1] > 0).astype(F32)
    keep_dn = (info[2] > 0).astype(F32)
    stats = moments(st_ref, members)
    for f in range(2):
        mean, inv = stats[f]

        def put(v, row, keep=None):
            n = (v.astype(F32) - mean) * inv
            a = n * sigmoid(n)
            if keep is not None:
                a = a * keep
            before, after = shifted(a)
            at = pl.ds(row, 128)
            act_ref[f, at, 0:256] = before.astype(BF16)
            act_ref[f, at, 256:512] = a.astype(BF16)
            act_ref[f, at, 512:768] = after.astype(BF16)

        put(up_ref[f], 0, keep_up)
        put(dn_ref[f], 9 * 128, keep_dn)

        def line(r, _):
            at = pl.multiple_of(r * 128, 128)
            put(x_ref[f, pl.ds(at, 128), :], pl.multiple_of(at + 128, 128))
            return 0

        lax.fori_loop(0, 8, line, 0)

        def conv(r, _):
            at = pl.multiple_of(r * 256, 256)
            v = None
            for i in range(3):
                lhs = act_ref[f, pl.ds(pl.multiple_of(at + i * 128, 128), 256), :]
                part = dot(lhs, w_ref[i])
                v = part if v is None else v + part
            s = sigmoid(v)
            hid_ref[f, pl.ds(at, 256), :] = (v * s).astype(BF16)
            slope_ref[f, pl.ds(at, 256), :] = s * (1.0 + v * (1.0 - s))
            return 0

        lax.fori_loop(0, 4, conv, 0)


def pregrad_kernel(cot_ref, later_ref, slope_ref, w_ref, pg_ref, top_ref, bot_ref):
    for f in range(2):

        def part(r, _):
            at = pl.ds(pl.multiple_of(r * 256, 256), 256)
            v = None
            for k in range(3):
                g = f + 2 - k
                lhs = cot_ref[g, at, :] if g < 2 else later_ref[g - 2, at, :]
                p = dot(lhs, w_ref[k], NT)
                v = p if v is None else v + p
            pg_ref[f, at, :] = (v * slope_ref[f, at, :]).astype(BF16)
            return 0

        lax.fori_loop(0, 4, part, 0)
        top_ref[f] = pg_ref[f, 0:128, :]
        bot_ref[f] = pg_ref[f, 896:1024, :]


def slab_rows(info, unit, part):
    piece = (unit % 3) * 4 + part
    x, y = (unit // 3 - info[3]) & 3, (piece // 3 - info[4]) & 3
    return pl.multiple_of(x * 768 + y * 192 + (piece % 3) * 64, 64)


def grads_kernel(info, act_ref, pg_ref, hid_ref, cot_ref, later_ref, g_ref):
    def put(tap, v):
        base = ((tap // 6) ^ info[0]) * 3072
        for lh in range(2):
            for part in range(4):
                at = pl.multiple_of(base + slab_rows(info, (tap % 6) * 2 + lh, part), 64)
                g_ref[pl.ds(at, 64), :] = v[part * 64 : part * 64 + 64, lh * 128 : lh * 128 + 128]

    for i in range(3):
        for j in range(3):
            v = None
            for f in range(2):
                lhs = act_ref[f, i * 128 : i * 128 + 1024, j * 256 : j * 256 + 256]
                p = dot(lhs, pg_ref[f], TN)
                v = p if v is None else v + p
            put(3 * i + j, v)
    for k in range(3):
        v = None
        for f in range(2):
            g = f + 2 - k
            rhs = cot_ref[g] if g < 2 else later_ref[g - 2]
            p = dot(hid_ref[f], rhs, TN)
            v = p if v is None else v + p
        put(9 + k, v)


def backward_kernel(members, pg_ref, up_ref, dn_ref, w_ref, x_ref, st_ref, ng_ref, o_ref, a_ref, b_ref, c_ref):
    stats = moments(st_ref, members)
    sums = []
    for f in range(2):
        mean, inv = stats[f]

        def put(v, row):
            v = v.astype(F32)
            before, after = shifted(v)
            at = pl.ds(row, 128)
            a_ref[f, at, :] = after.astype(BF16)
            b_ref[f, at, :] = v.astype(BF16)
            c_ref[f, at, :] = before.astype(BF16)

        put(up_ref[f], 0)
        put(dn_ref[f], 9 * 128)

        def line(r, _):
            at = pl.multiple_of(r * 128, 128)
            put(pg_ref[f, pl.ds(at, 128), :], pl.multiple_of(at + 128, 128))
            return 0

        lax.fori_loop(0, 8, line, 0)

        def conv(r, carry):
            at = pl.multiple_of(r * 256, 256)
            v = None
            for i in range(3):
                rows = pl.ds(pl.multiple_of(at + (2 - i) * 128, 128), 256)
                for j, ref in enumerate((a_ref, b_ref, c_ref)):
                    p = dot(ref[f, rows, :], w_ref[i, j], NT)
                    v = p if v is None else v + p
            n = (x_ref[f, pl.ds(at, 256), :].astype(F32) - mean) * inv
            s = sigmoid(n)
            ng = v * (s * (1.0 + n * (1.0 - s)))
            ng_ref[f, pl.ds(at, 256), :] = ng
            return carry[0] + fold(ng), carry[1] + fold(ng * n)

        zero = jnp.zeros((8, 256), F32)
        sums.append(lax.fori_loop(0, 4, conv, (zero, zero)))
    store_stats(o_ref, sums)


def input_grad_kernel(members, x_ref, cot_ref, ng_ref, st_ref, gst_ref, o_ref):
    stats = moments(st_ref, members)
    gstats = group_totals(gst_ref)
    for f in range(2):
        mean, inv = stats[f]
        first, second = gstats[f][0] / members, gstats[f][1] / members

        def part(r, _):
            at = pl.ds(pl.multiple_of(r * 128, 128), 128)
            n = (x_ref[f, at, :].astype(F32) - mean) * inv
            term = inv * (ng_ref[f, at, :] - first - n * second)
            o_ref[f, at, :] = (cot_ref[f, at, :].astype(F32) + term).astype(BF16)
            return 0

        lax.fori_loop(0, 8, part, 0)


def block_kernel(x_ref, hid_ref, prev_ref, w_ref, o_ref):
    for f in range(2):

        def part(r, _):
            at = pl.ds(pl.multiple_of(r * 256, 256), 256)
            v = None
            for k in range(3):
                g = f - 2 + k
                lhs = hid_ref[g, at, :] if g >= 0 else prev_ref[g + 2, at, :]
                p = dot(lhs, w_ref[k])
                v = p if v is None else v + p
            o_ref[f, at, :] = (x_ref[f, at, :].astype(F32) + v).astype(BF16)
            return 0

        lax.fori_loop(0, 4, part, 0)


def coded(v):
    t = v * UNIT
    return (t * jnp.sqrt(jnp.abs(t))).astype(BF16)


def decoded(u):
    u = u.astype(F32)
    size = jnp.abs(u)
    root = jnp.exp(jnp.log(jnp.maximum(size, 1e-37)) * (2.0 / 3.0)) * (1.0 / UNIT)
    return jnp.where(size < 1e-37, 0.0, jnp.where(u < 0, -root, root))


def pair_kernel(g_ref, got_ref, own_ref, *sent):
    for k in range(4):

        def part(r, _):
            at = pl.multiple_of(r * 128, 128)
            rows = pl.ds(pl.multiple_of(at + k * 768, 128), 128)
            v = g_ref[rows, :] + got_ref[rows, :]
            if k == 0:
                own_ref[pl.ds(at, 128), :] = v
            else:
                sent[k - 1][pl.ds(at, 128), :] = coded(v)
            return 0

        lax.fori_loop(0, 6, part, 0)


def x_kernel(own_ref, a_ref, b_ref, c_ref, mine_ref, *sent):
    for k in range(4):

        def part(r, _):
            at = pl.multiple_of(r * 64, 64)
            rows = pl.ds(pl.multiple_of(at + k * 192, 64), 64)
            v = own_ref[rows, :] + decoded(a_ref[rows, :]) + decoded(b_ref[rows, :]) + decoded(c_ref[rows, :])
            (mine_ref, *sent)[k][pl.ds(at, 64), :] = v
            return 0

        lax.fori_loop(0, 3, part, 0)


def y_kernel(own_ref, a_ref, b_ref, c_ref, gst_ref, o_ref):
    for peer in range(8):
        rows = slice(peer * 24, peer * 24 + 24)
        o_ref[peer, 0:24, :] = own_ref[rows, :] + a_ref[rows, :] + b_ref[rows, :] + c_ref[rows, :]
        o_ref[peer, 24:32, :] = gst_ref[0]


def z_kernel(u_ref, o_ref, gst_ref):
    total = u_ref[0]
    for peer in range(1, 8):
        total = total + u_ref[peer]
    gst_ref[0] = total[24:32]
    mine = coded(total[:24])
    for peer in range(8):
        o_ref[peer] = mine


def clip_kernel(clip_level, info, own_ref, other_ref, s_ref, t_ref):
    acc = jnp.zeros((8, 128), F32)
    for tap in range(12):
        ref, k = (s_ref, tap) if tap < 9 else (t_ref, tap - 9)
        mine = info[0] == tap // 6
        for lh in range(2):
            for part in range(4):
                at = pl.ds(slab_rows(info, (tap % 6) * 2 + lh, part), 64)
                v = decoded(jnp.where(mine, own_ref[at, :], other_ref[at, :]))
                ref[k, part * 64 : part * 64 + 64, lh * 128 : lh * 128 + 128] = v
                acc = acc + fold(v * v)
    total = jnp.sum(jnp.sum(acc, axis=0, keepdims=True), axis=1, keepdims=True)
    scale = clip_level / jnp.maximum(jnp.sqrt(total), clip_level)

    def finish(k, _):
        s_ref[k] = s_ref[k] * scale
        return 0

    lax.fori_loop(0, 9, finish, 0)
    for k in range(3):
        t_ref[k] = t_ref[k] * scale


def in_hbm(x):
    return pltpu.with_memory_space_constraint(x, pltpu.HBM)


def swapped(x, axis):
    return lax.ppermute(x, axis, [(0, 1), (1, 0)])


def moved(x, axes, distance):
    n = lax.axis_size(axes)
    route = [(i, i + distance) for i in range(n) if 0 <= i + distance < n]
    return lax.ppermute(x, axes, route)


def shifts(sent, axis):
    n = lax.axis_size(axis)
    return [
        lax.ppermute(m, axis, [(i, (i + d) % n) for i in range(n)]) for d, m in enumerate(sent, 1)
    ]


def gathered(mine, axis):
    got = tied(shifts([mine] * 3, axis))
    return jnp.concatenate([mine, got[2], got[1], got[0]], axis=0)


def body(video_latents, cotangent, spatial_kernel, temporal_kernel):
    batch, frames, rows, columns, channels = video_latents.shape
    peers = lax.axis_size(HEIGHT)
    members = float(rows * peers * columns * (channels // GROUPS))
    clip_level = (
        channels * rows * peers * columns
        * math.sqrt(batch * lax.axis_size(DP) * frames * lax.axis_size(TM))
        / CLIP_DIVISOR
    )
    z = lax.axis_index(HEIGHT)
    info = jnp.stack(
        [lax.axis_index("core"), z, peers - 1 - z, lax.axis_index(TM), lax.axis_index("y")]
    ).astype(jnp.int32)
    pixels = rows * columns
    flat = (2, pixels, 256)
    x = video_latents.reshape(flat)
    cot = cotangent.reshape(flat)
    w9 = spatial_kernel
    w3 = spatial_kernel.reshape(3, 768, 256)
    gflop = 2 * 2048 * 256 * 256

    later = moved(cot, TM, -1)
    small = out((8, 8, 128), F32)
    edge = out((2, columns, 256), BF16)
    st, x_top, x_bot = call(stats_kernel, [small, edge, edge], [x], 1 << 21)
    st = lax.all_to_all(st, HEIGHT, 0, 0, tiled=True)
    up = moved(x_bot, HEIGHT, 1)
    dn = moved(x_top, HEIGHT, -1)
    act, hid, slope = call(
        lambda *refs: forward_kernel(members, *refs),
        [out((2, 1280, 768), BF16), out(flat, BF16), out(flat, F32)],
        [info, in_hbm(x), in_hbm(up), in_hbm(dn), in_hbm(st), in_hbm(w3)],
        9 * gflop,
        smem=1,
        loose=(2, 3, 4),
        scratch=[
            pltpu.VMEM(edge.shape, BF16),
            pltpu.VMEM(edge.shape, BF16),
            pltpu.VMEM(small.shape, F32),
            pltpu.SemaphoreType.DMA((3,)),
        ],
    )
    pg, top, bot = call(
        pregrad_kernel, [out(flat, BF16), edge, edge], [cot, later, slope, temporal_kernel], 3 * gflop
    )
    (g,) = call(
        grads_kernel, [out((6144, 128), F32)], [info, act, pg, hid, cot, later], 12 * gflop, smem=1
    )
    send, top, bot = tied((g[3072:], top, bot))
    got = swapped(send, "core")
    gup = moved(bot, HEIGHT, 1)
    gdn = moved(top, HEIGHT, -1)
    quarter = out((768, 128), BF16)
    own, *sent = call(
        pair_kernel, [out((768, 128), F32), quarter, quarter, quarter], [g, got], 1 << 21
    )
    own, sent, gup, gdn = tied((own, sent, gup, gdn))
    got = shifts(sent, TM)
    ng, gst = call(
        lambda *refs: backward_kernel(members, *refs),
        [out(flat, F32), out((1, 8, 128), F32)],
        [pg, gup, gdn, w9, x, st],
        9 * gflop,
        scratch=[pltpu.VMEM((2, 1280, 256), BF16)] * 3,
    )
    got, ng, gst = tied((got, ng, gst))
    part = out((192, 128), F32)
    own, *sent = call(x_kernel, [part] * 4, [own, *got], 1 << 21)
    own, sent, hid_sent = tied((own, sent, hid))
    got = tied(shifts(sent, "y"))
    prev = moved(hid_sent, TM, 1)
    (pieces,) = call(y_kernel, [out((8, 32, 128), F32)], [own, *got, gst], 1 << 20)
    pieces = lax.all_to_all(pieces, HEIGHT, 0, 0, tiled=True)
    copies, gst = call(z_kernel, [out((8, 24, 128), BF16), out((1, 8, 128), F32)], [pieces], 1 << 20)
    mine = lax.all_to_all(copies, HEIGHT, 0, 0, tiled=True).reshape(192, 128)
    (input_grad,) = call(
        lambda *refs: input_grad_kernel(members, *refs), [out(flat, BF16)], [x, cot, ng, st, gst], 1 << 21
    )
    mine, input_grad = tied((mine, input_grad))
    mine, prev = tied((gathered(mine, "y"), prev))
    (block_output,) = call(block_kernel, [out(flat, BF16)], [x, hid, prev, temporal_kernel], 3 * gflop)
    mine = gathered(mine, TM)
    mine, block_output = tied((mine, block_output))
    clipped_spatial, clipped_temporal = call(
        lambda *refs: clip_kernel(clip_level, *refs),
        [out((9, 256, 256), F32), out((3, 256, 256), F32)],
        [info, mine, swapped(mine, "core")],
        1 << 21,
        smem=1,
    )
    return (
        block_output.reshape(video_latents.shape),
        input_grad.reshape(video_latents.shape),
        clipped_spatial.reshape(spatial_kernel.shape),
        clipped_temporal,
    )


def solution(mesh):
    sizes = (mesh.shape["dp"] // 2, 2, mesh.shape[TM], mesh.shape[HEIGHT])
    torus = Mesh(mesh.devices.reshape(sizes), (*DP, TM, HEIGHT))
    field = P(DP, TM, HEIGHT, None, None)
    return jax.shard_map(
        body, mesh=torus, in_specs=(field, field, P(), P()), out_specs=(field, field, P(), P()), check_vma=False
    )
```

```python
import math

import jax
import jax.numpy as jnp
from jax import lax
from jax.experimental import pallas as pl
from jax.experimental.pallas import tpu as pltpu
from jax.sharding import Mesh
from jax.sharding import PartitionSpec as P

GROUPS = 32
tied = lax.optimization_barrier
EPSILON = 1e-05
CLIP_DIVISOR = 20.0
F32 = jnp.float32
BF16 = jnp.bfloat16
DP = ("y", "core")
TM = "tm"
HEIGHT = "height"
UNIT = 2.0**40
VMEM = pl.BlockSpec(memory_space=pltpu.VMEM)
SMEM = pl.BlockSpec(memory_space=pltpu.SMEM)
ANY = pl.BlockSpec(memory_space=pl.ANY)
NT = (((1,), (1,)), ((), ()))
TN = (((0,), (0,)), ((), ()))


def call(kernel, outs, args, flops, scratch=(), smem=0, limit=16, loose=(), outside=False):
    nbytes = sum(a.size * a.dtype.itemsize for a in (*args, *outs))
    specs = [SMEM] * smem + [ANY if i in loose else VMEM for i in range(smem, len(args))]
    return pl.pallas_call(
        kernel,
        out_shape=tuple(outs),
        in_specs=specs,
        out_specs=tuple(ANY if outside else VMEM for _ in outs),
        scratch_shapes=list(scratch),
        compiler_params=pltpu.CompilerParams(vmem_limit_bytes=limit << 20),
        cost_estimate=pl.CostEstimate(flops=flops, bytes_accessed=nbytes, transcendentals=0),
    )(*args)


def out(shape, dtype):
    return jax.ShapeDtypeStruct(shape, dtype)


def dot(a, b, dims=None):
    if dims is None:
        return jnp.dot(a, b, preferred_element_type=F32)
    return lax.dot_general(a, b, dims, preferred_element_type=F32)


def sigmoid(v):
    return 0.5 + 0.5 * jnp.tanh(0.5 * v)


def store_stats(o_ref, sums):
    rows = []
    for first, second in sums:
        for v in (first, second):
            t = jnp.sum(v, axis=0, keepdims=True)
            rows += [t[:, :128], t[:, 128:]]
    packed = jnp.concatenate(rows, axis=0)
    for peer in range(o_ref.shape[0]):
        o_ref[peer] = packed


def group_totals(st_ref):
    tot = st_ref[0]
    for peer in range(1, st_ref.shape[0]):
        tot = tot + st_ref[peer]
    lane = lax.broadcasted_iota(jnp.int32, tot.shape, 1)
    for d in (1, 2, 4):
        low = (lane & d) == 0
        tot = tot + jnp.where(low, pltpu.roll(tot, 128 - d, 1), pltpu.roll(tot, d, 1))
    res = []
    for f in range(tot.shape[0] // 4):
        r = [tot[4 * f + k : 4 * f + k + 1] for k in range(4)]
        res.append((jnp.concatenate(r[:2], axis=1), jnp.concatenate(r[2:], axis=1)))
    return res


def moments(st_ref, members):
    res = []
    for first, second in group_totals(st_ref):
        mean = first / members
        res.append((mean, lax.rsqrt(second / members - mean * mean + EPSILON)))
    return res


def fetched(*pairs, sems):
    copies = [pltpu.make_async_copy(a, b, sems.at[i]) for i, (a, b) in enumerate(pairs)]
    for c in copies:
        c.start()
    for c in copies:
        c.wait()


def fold(v):
    return jnp.sum(v.reshape(v.shape[0] // 8, 8, v.shape[1]), axis=0)


def stats_kernel(x_ref, o_ref, top_ref, bot_ref):
    sums = []
    for f in range(2):
        top_ref[f] = x_ref[f, 0:128, :]
        bot_ref[f] = x_ref[f, 896:1024, :]

        def step(r, carry):
            v = x_ref[f, pl.ds(pl.multiple_of(r * 128, 128), 128), :].astype(F32)
            return carry[0] + fold(v), carry[1] + fold(v * v)

        zero = jnp.zeros((8, 256), F32)
        sums.append(lax.fori_loop(0, 8, step, (zero, zero)))
    store_stats(o_ref, sums)


def shifted(v):
    row = lax.broadcasted_iota(jnp.int32, v.shape, 0)
    before = jnp.where(row == 0, 0.0, pltpu.roll(v, 1, 0))
    after = jnp.where(row == v.shape[0] - 1, 0.0, pltpu.roll(v, v.shape[0] - 1, 0))
    return before, after


def forward_kernel(
    members, info, x_ref, up_hbm, dn_hbm, st_hbm, w_ref, act_ref, hid_ref, slope_ref, up_ref, dn_ref, st_ref, sems
):
    fetched((st_hbm, st_ref), (up_hbm, up_ref), (dn_hbm, dn_ref), sems=sems)
    keep_up = (info[1] > 0).astype(F32)
    keep_dn = (info[2] > 0).astype(F32)
    stats = moments(st_ref, members)
    for f in range(2):
        mean, inv = stats[f]

        def put(v, row, keep=None):
            n = (v.astype(F32) - mean) * inv
            a = n * sigmoid(n)
            if keep is not None:
                a = a * keep
            before, after = shifted(a)
            at = pl.ds(row, 128)
            act_ref[f, at, 0:256] = before.astype(BF16)
            act_ref[f, at, 256:512] = a.astype(BF16)
            act_ref[f, at, 512:768] = after.astype(BF16)

        put(up_ref[f], 0, keep_up)
        put(dn_ref[f], 9 * 128, keep_dn)

        def line(r, _):
            at = pl.multiple_of(r * 128, 128)
            put(x_ref[f, pl.ds(at, 128), :], pl.multiple_of(at + 128, 128))
            return 0

        lax.fori_loop(0, 8, line, 0)

        def conv(r, _):
            at = pl.multiple_of(r * 512, 512)
            v = None
            for i in range(3):
                lhs = act_ref[f, pl.ds(pl.multiple_of(at + i * 128, 128), 512), :]
                part = dot(lhs, w_ref[i])
                v = part if v is None else v + part
            s = sigmoid(v)
            hid_ref[f, pl.ds(at, 512), :] = (v * s).astype(BF16)
            slope_ref[f, pl.ds(at, 512), :] = s * (1.0 + v * (1.0 - s))
            return 0

        lax.fori_loop(0, 2, conv, 0)


def pregrad_kernel(cot_ref, later_ref, slope_ref, w_ref, pg_ref, top_ref, bot_ref):
    for f in range(2):

        def part(r, _):
            at = pl.ds(pl.multiple_of(r * 512, 512), 512)
            v = None
            for k in range(3):
                g = f + 2 - k
                lhs = cot_ref[g, at, :] if g < 2 else later_ref[g - 2, at, :]
                p = dot(lhs, w_ref[k], NT)
                v = p if v is None else v + p
            pg_ref[f, at, :] = (v * slope_ref[f, at, :]).astype(BF16)
            return 0

        lax.fori_loop(0, 2, part, 0)
        top_ref[f] = pg_ref[f, 0:128, :]
        bot_ref[f] = pg_ref[f, 896:1024, :]


def slab_rows(info, unit, part):
    piece = (unit % 3) * 4 + part
    x, y = (unit // 3 - info[3]) & 3, (piece // 3 - info[4]) & 3
    return pl.multiple_of(x * 768 + y * 192 + (piece % 3) * 64, 64)


def grads_kernel(info, act_ref, pg_ref, hid_ref, cot_ref, later_ref, g_ref):
    def put(tap, v):
        base = ((tap // 6) ^ info[0]) * 3072
        for lh in range(2):
            for part in range(4):
                at = pl.multiple_of(base + slab_rows(info, (tap % 6) * 2 + lh, part), 64)
                g_ref[pl.ds(at, 64), :] = v[part * 64 : part * 64 + 64, lh * 128 : lh * 128 + 128]

    for i in range(3):
        for j in range(3):
            v = None
            for f in range(2):
                lhs = act_ref[f, i * 128 : i * 128 + 1024, j * 256 : j * 256 + 256]
                p = dot(lhs, pg_ref[f], TN)
                v = p if v is None else v + p
            put(3 * i + j, v)
    for k in range(3):
        v = None
        for f in range(2):
            g = f + 2 - k
            rhs = cot_ref[g] if g < 2 else later_ref[g - 2]
            p = dot(hid_ref[f], rhs, TN)
            v = p if v is None else v + p
        put(9 + k, v)


def backward_kernel(members, pg_ref, up_ref, dn_ref, w_ref, x_ref, st_ref, ng_ref, o_ref, a_ref, b_ref, c_ref):
    stats = moments(st_ref, members)
    sums = []
    for f in range(2):
        mean, inv = stats[f]

        def put(v, row):
            v = v.astype(F32)
            before, after = shifted(v)
            at = pl.ds(row, 128)
            a_ref[f, at, :] = after.astype(BF16)
            b_ref[f, at, :] = v.astype(BF16)
            c_ref[f, at, :] = before.astype(BF16)

        put(up_ref[f], 0)
        put(dn_ref[f], 9 * 128)

        def line(r, _):
            at = pl.multiple_of(r * 128, 128)
            put(pg_ref[f, pl.ds(at, 128), :], pl.multiple_of(at + 128, 128))
            return 0

        lax.fori_loop(0, 8, line, 0)

        def conv(r, carry):
            at = pl.multiple_of(r * 512, 512)
            v = None
            for i in range(3):
                rows = pl.ds(pl.multiple_of(at + (2 - i) * 128, 128), 512)
                for j, ref in enumerate((a_ref, b_ref, c_ref)):
                    p = dot(ref[f, rows, :], w_ref[i, j], NT)
                    v = p if v is None else v + p
            n = (x_ref[f, pl.ds(at, 512), :].astype(F32) - mean) * inv
            s = sigmoid(n)
            ng = v * (s * (1.0 + n * (1.0 - s)))
            ng_ref[f, pl.ds(at, 512), :] = ng
            return carry[0] + fold(ng), carry[1] + fold(ng * n)

        zero = jnp.zeros((8, 256), F32)
        sums.append(lax.fori_loop(0, 2, conv, (zero, zero)))
    store_stats(o_ref, sums)


def input_grad_kernel(members, x_ref, cot_ref, ng_ref, st_ref, gst_ref, o_ref):
    stats = moments(st_ref, members)
    gstats = group_totals(gst_ref)
    for f in range(2):
        mean, inv = stats[f]
        first, second = gstats[f][0] / members, gstats[f][1] / members

        def part(r, _):
            at = pl.ds(pl.multiple_of(r * 128, 128), 128)
            n = (x_ref[f, at, :].astype(F32) - mean) * inv
            term = inv * (ng_ref[f, at, :] - first - n * second)
            o_ref[f, at, :] = (cot_ref[f, at, :].astype(F32) + term).astype(BF16)
            return 0

        lax.fori_loop(0, 8, part, 0)


def block_kernel(x_ref, hid_ref, prev_ref, w_ref, o_ref):
    for f in range(2):

        def part(r, _):
            at = pl.ds(pl.multiple_of(r * 512, 512), 512)
            v = None
            for k in range(3):
                g = f - 2 + k
                lhs = hid_ref[g, at, :] if g >= 0 else prev_ref[g + 2, at, :]
                p = dot(lhs, w_ref[k])
                v = p if v is None else v + p
            o_ref[f, at, :] = (x_ref[f, at, :].astype(F32) + v).astype(BF16)
            return 0

        lax.fori_loop(0, 2, part, 0)


def coded(v):
    t = v * UNIT
    return (t * jnp.sqrt(jnp.abs(t))).astype(BF16)


def decoded(u):
    u = u.astype(F32)
    size = jnp.abs(u)
    root = jnp.exp(jnp.log(jnp.maximum(size, 1e-37)) * (2.0 / 3.0)) * (1.0 / UNIT)
    return jnp.where(size < 1e-37, 0.0, jnp.where(u < 0, -root, root))


def pair_kernel(g_ref, got_ref, own_ref, *sent):
    for k in range(4):

        def part(r, _):
            at = pl.multiple_of(r * 128, 128)
            rows = pl.ds(pl.multiple_of(at + k * 768, 128), 128)
            v = g_ref[rows, :] + got_ref[rows, :]
            if k == 0:
                own_ref[pl.ds(at, 128), :] = v
            else:
                sent[k - 1][pl.ds(at, 128), :] = coded(v)
            return 0

        lax.fori_loop(0, 6, part, 0)


def x_kernel(own_ref, a_ref, b_ref, c_ref, mine_ref, *sent):
    for k in range(4):

        def part(r, _):
            at = pl.multiple_of(r * 64, 64)
            rows = pl.ds(pl.multiple_of(at + k * 192, 64), 64)
            v = own_ref[rows, :] + decoded(a_ref[rows, :]) + decoded(b_ref[rows, :]) + decoded(c_ref[rows, :])
            (mine_ref, *sent)[k][pl.ds(at, 64), :] = v
            return 0

        lax.fori_loop(0, 3, part, 0)


def y_kernel(own_ref, a_ref, b_ref, c_ref, o_ref):
    for peer in range(8):
        rows = slice(peer * 24, peer * 24 + 24)
        o_ref[peer] = own_ref[rows, :] + a_ref[rows, :] + b_ref[rows, :] + c_ref[rows, :]


def z_kernel(u_ref, gst_ref, o_ref):
    total = u_ref[0]
    for peer in range(1, 8):
        total = total + u_ref[peer]
    for peer in range(8):
        o_ref[peer, 0:24, :] = total
        o_ref[peer, 24:32, :] = gst_ref[0]


def code_kernel(u_ref, o_ref, gst_ref):
    for peer in range(0, 8, 2):
        pair = jnp.concatenate([u_ref[peer, 0:24, :], u_ref[peer + 1, 0:24, :]], axis=0)
        o_ref[peer * 24 : peer * 24 + 48, :] = coded(pair)
    total = u_ref[0, 24:32, :]
    for peer in range(1, 8):
        total = total + u_ref[peer, 24:32, :]
    gst_ref[0] = total


def clip_kernel(clip_level, info, own_ref, other_ref, s_ref, t_ref, w_ref, sems):
    acc = jnp.zeros((8, 128), F32)
    for tap in range(12):
        mine = info[0] == tap // 6
        for lh in range(2):
            for part in range(4):
                at = pl.ds(slab_rows(info, (tap % 6) * 2 + lh, part), 64)
                v = decoded(jnp.where(mine, own_ref[at, :], other_ref[at, :]))
                w_ref[tap, part * 64 : part * 64 + 64, lh * 128 : lh * 128 + 128] = v
                acc = acc + fold(v * v)
    total = jnp.sum(jnp.sum(acc, axis=0, keepdims=True), axis=1, keepdims=True)
    scale = clip_level / jnp.maximum(jnp.sqrt(total), clip_level)
    copies = []
    for tap in range(12):
        w_ref[tap] = w_ref[tap] * scale
        target = s_ref.at[tap] if tap < 9 else t_ref.at[tap - 9]
        copies.append(pltpu.make_async_copy(w_ref.at[tap], target, sems.at[tap]))
        copies[-1].start()
    for c in copies:
        c.wait()


def in_hbm(x):
    return pltpu.with_memory_space_constraint(x, pltpu.HBM)


def swapped(x, axis):
    return lax.ppermute(x, axis, [(0, 1), (1, 0)])


def moved(x, axes, distance):
    n = lax.axis_size(axes)
    route = [(i, i + distance) for i in range(n) if 0 <= i + distance < n]
    return lax.ppermute(x, axes, route)


def shifts(sent, axis):
    n = lax.axis_size(axis)
    return [
        lax.ppermute(m, axis, [(i, (i + d) % n) for i in range(n)]) for d, m in enumerate(sent, 1)
    ]


def gathered(mine, axis):
    got = tied(shifts([mine] * 3, axis))
    return jnp.concatenate([mine, got[2], got[1], got[0]], axis=0)


def body(video_latents, cotangent, spatial_kernel, temporal_kernel):
    batch, frames, rows, columns, channels = video_latents.shape
    peers = lax.axis_size(HEIGHT)
    members = float(rows * peers * columns * (channels // GROUPS))
    clip_level = (
        channels * rows * peers * columns
        * math.sqrt(batch * lax.axis_size(DP) * frames * lax.axis_size(TM))
        / CLIP_DIVISOR
    )
    z = lax.axis_index(HEIGHT)
    info = jnp.stack(
        [lax.axis_index("core"), z, peers - 1 - z, lax.axis_index(TM), lax.axis_index("y")]
    ).astype(jnp.int32)
    pixels = rows * columns
    flat = (2, pixels, 256)
    x = video_latents.reshape(flat)
    cot = cotangent.reshape(flat)
    w9 = spatial_kernel
    w3 = spatial_kernel.reshape(3, 768, 256)
    gflop = 2 * 2048 * 256 * 256

    later = moved(cot, TM, -1)
    small = out((8, 8, 128), F32)
    edge = out((2, columns, 256), BF16)
    st, x_top, x_bot = call(stats_kernel, [small, edge, edge], [x], 1 << 21)
    st = lax.all_to_all(st, HEIGHT, 0, 0, tiled=True)
    up = moved(x_bot, HEIGHT, 1)
    dn = moved(x_top, HEIGHT, -1)
    act, hid, slope = call(
        lambda *refs: forward_kernel(members, *refs),
        [out((2, 1280, 768), BF16), out(flat, BF16), out(flat, F32)],
        [info, in_hbm(x), in_hbm(up), in_hbm(dn), in_hbm(st), in_hbm(w3)],
        9 * gflop,
        smem=1,
        loose=(2, 3, 4),
        scratch=[
            pltpu.VMEM(edge.shape, BF16),
            pltpu.VMEM(edge.shape, BF16),
            pltpu.VMEM(small.shape, F32),
            pltpu.SemaphoreType.DMA((3,)),
        ],
    )
    pg, top, bot = call(
        pregrad_kernel, [out(flat, BF16), edge, edge], [cot, later, slope, temporal_kernel], 3 * gflop
    )
    (g,) = call(
        grads_kernel, [out((6144, 128), F32)], [info, act, pg, hid, cot, later], 12 * gflop, smem=1
    )
    send, top, bot = tied((g[3072:], top, bot))
    got = swapped(send, "core")
    gup = moved(bot, HEIGHT, 1)
    gdn = moved(top, HEIGHT, -1)
    quarter = out((768, 128), BF16)
    own, *sent = call(
        pair_kernel, [out((768, 128), F32), quarter, quarter, quarter], [g, got], 1 << 21
    )
    got = tied(shifts(sent, TM))
    part = out((192, 128), F32)
    own, *sent = call(x_kernel, [part] * 4, [own, *got], 1 << 21)
    got = tied(shifts(sent, "y"))
    (pieces,) = call(y_kernel, [out((8, 24, 128), F32)], [own, *got], 1 << 20)
    pieces, gup, gdn, hid_sent = tied((pieces, gup, gdn, hid))
    pieces = lax.all_to_all(pieces, HEIGHT, 0, 0, tiled=True)
    prev = moved(hid_sent, TM, 1)
    ng, gst = call(
        lambda *refs: backward_kernel(members, *refs),
        [out(flat, F32), out((1, 8, 128), F32)],
        [in_hbm(a) for a in (pg, gup, gdn, w9, x, st)],
        9 * gflop,
        scratch=[pltpu.VMEM((2, 1280, 256), BF16)] * 3,
    )
    pieces, ng, gst = tied((pieces, in_hbm(ng), gst))
    (copies,) = call(z_kernel, [out((8, 32, 128), F32)], [pieces, gst], 1 << 20)
    copies = lax.all_to_all(copies, HEIGHT, 0, 0, tiled=True)
    mine, gst = call(code_kernel, [out((192, 128), BF16), out((1, 8, 128), F32)], [copies], 1 << 20)
    mine, prev, gst = tied((mine, prev, gst))
    (input_grad,) = call(
        lambda *refs: input_grad_kernel(members, *refs), [out(flat, BF16)], [x, cot, in_hbm(ng), in_hbm(st), gst], 1 << 21
    )
    mine = gathered(mine, "y")
    mine, input_grad = tied((mine, input_grad))
    (block_output,) = call(block_kernel, [out(flat, BF16)], [x, hid, prev, temporal_kernel], 3 * gflop)
    mine = gathered(mine, TM)
    mine, block_output = tied((mine, block_output))
    clipped_spatial, clipped_temporal = call(
        lambda *refs: clip_kernel(clip_level, *refs),
        [out((9, 256, 256), F32), out((3, 256, 256), F32)],
        [info, mine, swapped(mine, "core")],
        1 << 21,
        smem=1,
        outside=True,
        scratch=[pltpu.VMEM((12, 256, 256), F32), pltpu.SemaphoreType.DMA((12,))],
    )
    return (
        block_output.reshape(video_latents.shape),
        input_grad.reshape(video_latents.shape),
        clipped_spatial.reshape(spatial_kernel.shape),
        clipped_temporal,
    )


def solution(mesh):
    sizes = (mesh.shape["dp"] // 2, 2, mesh.shape[TM], mesh.shape[HEIGHT])
    torus = Mesh(mesh.devices.reshape(sizes), (*DP, TM, HEIGHT))
    field = P(DP, TM, HEIGHT, None, None)
    return jax.shard_map(
        body, mesh=torus, in_specs=(field, field, P(), P()), out_specs=(field, field, P(), P()), check_vma=False
    )
```

```python
import math

import jax
import jax.numpy as jnp
from jax import lax
from jax.experimental import pallas as pl
from jax.experimental.pallas import tpu as pltpu
from jax.sharding import Mesh
from jax.sharding import PartitionSpec as P


GROUPS = 32
tied = lax.optimization_barrier
EPSILON = 1e-05
CLIP_DIVISOR = 20.0
F32 = jnp.float32
BF16 = jnp.bfloat16
DP = ("y", "core")
TM = "tm"
HEIGHT = "height"
UNIT = 2.0**40
VMEM = pl.BlockSpec(memory_space=pltpu.VMEM)
SMEM = pl.BlockSpec(memory_space=pltpu.SMEM)
ANY = pl.BlockSpec(memory_space=pl.ANY)
NT = (((1,), (1,)), ((), ()))
TN = (((0,), (0,)), ((), ()))


def call(kernel, outs, args, flops, scratch=(), smem=0, limit=16, loose=(), outside=False):
    nbytes = sum(a.size * a.dtype.itemsize for a in (*args, *outs))
    specs = [SMEM] * smem + [ANY if i in loose else VMEM for i in range(smem, len(args))]
    return pl.pallas_call(
        kernel,
        out_shape=tuple(outs),
        in_specs=specs,
        out_specs=tuple(ANY if outside else VMEM for _ in outs),
        scratch_shapes=list(scratch),
        compiler_params=pltpu.CompilerParams(vmem_limit_bytes=limit << 20),
        cost_estimate=pl.CostEstimate(flops=flops, bytes_accessed=nbytes, transcendentals=0),
    )(*args)


def out(shape, dtype):
    return jax.ShapeDtypeStruct(shape, dtype)


def dot(a, b, dims=None):
    if dims is None:
        return jnp.dot(a, b, preferred_element_type=F32)
    return lax.dot_general(a, b, dims, preferred_element_type=F32)


def sigmoid(v):
    return 0.5 + 0.5 * jnp.tanh(0.5 * v)


def store_stats(o_ref, sums):
    rows = []
    for first, second in sums:
        for v in (first, second):
            t = jnp.sum(v, axis=0, keepdims=True)
            rows += [t[:, :128], t[:, 128:]]
    packed = jnp.concatenate(rows, axis=0)
    for peer in range(o_ref.shape[0]):
        o_ref[peer] = packed


def group_totals(st_ref):
    tot = st_ref[0]
    for peer in range(1, st_ref.shape[0]):
        tot = tot + st_ref[peer]
    lane = lax.broadcasted_iota(jnp.int32, tot.shape, 1)
    for d in (1, 2, 4):
        low = (lane & d) == 0
        tot = tot + jnp.where(low, pltpu.roll(tot, 128 - d, 1), pltpu.roll(tot, d, 1))
    res = []
    for f in range(tot.shape[0] // 4):
        r = [tot[4 * f + k : 4 * f + k + 1] for k in range(4)]
        res.append((jnp.concatenate(r[:2], axis=1), jnp.concatenate(r[2:], axis=1)))
    return res


def moments(st_ref, members):
    res = []
    for first, second in group_totals(st_ref):
        mean = first / members
        res.append((mean, lax.rsqrt(second / members - mean * mean + EPSILON)))
    return res


def fetched(*pairs, sems):
    copies = [pltpu.make_async_copy(a, b, sems.at[i]) for i, (a, b) in enumerate(pairs)]
    for c in copies:
        c.start()
    for c in copies:
        c.wait()


def fold(v):
    return jnp.sum(v.reshape(v.shape[0] // 8, 8, v.shape[1]), axis=0)


def stats_kernel(x_ref, o_ref, top_ref, bot_ref):
    sums = []
    for f in range(2):
        top_ref[f] = x_ref[f, 0:128, :]
        bot_ref[f] = x_ref[f, 896:1024, :]

        def step(r, carry):
            v = x_ref[f, pl.ds(pl.multiple_of(r * 128, 128), 128), :].astype(F32)
            return carry[0] + fold(v), carry[1] + fold(v * v)

        zero = jnp.zeros((8, 256), F32)
        sums.append(lax.fori_loop(0, 8, step, (zero, zero)))
    store_stats(o_ref, sums)


def shifted(v):
    row = lax.broadcasted_iota(jnp.int32, v.shape, 0)
    before = jnp.where(row == 0, 0.0, pltpu.roll(v, 1, 0))
    after = jnp.where(row == v.shape[0] - 1, 0.0, pltpu.roll(v, v.shape[0] - 1, 0))
    return before, after


def forward_kernel(
    members, info, x_ref, up_hbm, dn_hbm, st_hbm, w_ref, act_ref, hid_ref, slope_ref, up_ref, dn_ref, st_ref, sems
):
    fetched((st_hbm, st_ref), (up_hbm, up_ref), (dn_hbm, dn_ref), sems=sems)
    keep_up = (info[1] > 0).astype(F32)
    keep_dn = (info[2] > 0).astype(F32)
    stats = moments(st_ref, members)
    for f in range(2):
        mean, inv = stats[f]

        def put(v, row, keep=None):
            n = (v.astype(F32) - mean) * inv
            a = n * sigmoid(n)
            if keep is not None:
                a = a * keep
            before, after = shifted(a)
            at = pl.ds(row, 128)
            act_ref[f, at, 0:256] = before.astype(BF16)
            act_ref[f, at, 256:512] = a.astype(BF16)
            act_ref[f, at, 512:768] = after.astype(BF16)

        put(up_ref[f], 0, keep_up)
        put(dn_ref[f], 9 * 128, keep_dn)

        def line(r, _):
            at = pl.multiple_of(r * 128, 128)
            put(x_ref[f, pl.ds(at, 128), :], pl.multiple_of(at + 128, 128))
            return 0

        lax.fori_loop(0, 8, line, 0)

        def conv(r, _):
            at = pl.multiple_of(r * 512, 512)
            v = None
            for i in range(3):
                lhs = act_ref[f, pl.ds(pl.multiple_of(at + i * 128, 128), 512), :]
                part = dot(lhs, w_ref[i])
                v = part if v is None else v + part
            s = sigmoid(v)
            hid_ref[f, pl.ds(at, 512), :] = (v * s).astype(BF16)
            slope_ref[f, pl.ds(at, 512), :] = s * (1.0 + v * (1.0 - s))
            return 0

        lax.fori_loop(0, 2, conv, 0)


def pregrad_kernel(cot_ref, later_ref, slope_ref, w_ref, pg_ref, top_ref, bot_ref):
    for f in range(2):

        def part(r, _):
            at = pl.ds(pl.multiple_of(r * 512, 512), 512)
            v = None
            for k in range(3):
                g = f + 2 - k
                lhs = cot_ref[g, at, :] if g < 2 else later_ref[g - 2, at, :]
                p = dot(lhs, w_ref[k], NT)
                v = p if v is None else v + p
            pg_ref[f, at, :] = (v * slope_ref[f, at, :]).astype(BF16)
            return 0

        lax.fori_loop(0, 2, part, 0)
        top_ref[f] = pg_ref[f, 0:128, :]
        bot_ref[f] = pg_ref[f, 896:1024, :]


def slab_rows(info, unit, part):
    piece = (unit % 3) * 4 + part
    x, y = (unit // 3 - info[3]) & 3, (piece // 3 - info[4]) & 3
    return pl.multiple_of(x * 768 + y * 192 + (piece % 3) * 64, 64)


def grads_kernel(info, act_ref, pg_ref, hid_ref, cot_ref, later_ref, g_ref):
    def put(tap, v):
        base = ((tap // 6) ^ info[0]) * 3072
        for lh in range(2):
            for part in range(4):
                at = pl.multiple_of(base + slab_rows(info, (tap % 6) * 2 + lh, part), 64)
                g_ref[pl.ds(at, 64), :] = v[part * 64 : part * 64 + 64, lh * 128 : lh * 128 + 128]

    for i in range(3):
        for j in range(3):
            v = None
            for f in range(2):
                lhs = act_ref[f, i * 128 : i * 128 + 1024, j * 256 : j * 256 + 256]
                p = dot(lhs, pg_ref[f], TN)
                v = p if v is None else v + p
            put(3 * i + j, v)
    for k in range(3):
        v = None
        for f in range(2):
            g = f + 2 - k
            rhs = cot_ref[g] if g < 2 else later_ref[g - 2]
            p = dot(hid_ref[f], rhs, TN)
            v = p if v is None else v + p
        put(9 + k, v)


def backward_kernel(members, pg_ref, up_ref, dn_ref, w_ref, x_ref, st_ref, ng_ref, o_ref, a_ref, b_ref, c_ref):
    stats = moments(st_ref, members)
    sums = []
    for f in range(2):
        mean, inv = stats[f]

        def put(v, row):
            v = v.astype(F32)
            before, after = shifted(v)
            at = pl.ds(row, 128)
            a_ref[f, at, :] = after.astype(BF16)
            b_ref[f, at, :] = v.astype(BF16)
            c_ref[f, at, :] = before.astype(BF16)

        put(up_ref[f], 0)
        put(dn_ref[f], 9 * 128)

        def line(r, _):
            at = pl.multiple_of(r * 128, 128)
            put(pg_ref[f, pl.ds(at, 128), :], pl.multiple_of(at + 128, 128))
            return 0

        lax.fori_loop(0, 8, line, 0)

        def conv(r, carry):
            at = pl.multiple_of(r * 512, 512)
            v = None
            for i in range(3):
                rows = pl.ds(pl.multiple_of(at + (2 - i) * 128, 128), 512)
                for j, ref in enumerate((a_ref, b_ref, c_ref)):
                    p = dot(ref[f, rows, :], w_ref[i, j], NT)
                    v = p if v is None else v + p
            n = (x_ref[f, pl.ds(at, 512), :].astype(F32) - mean) * inv
            s = sigmoid(n)
            ng = v * (s * (1.0 + n * (1.0 - s)))
            ng_ref[f, pl.ds(at, 512), :] = ng
            return carry[0] + fold(ng), carry[1] + fold(ng * n)

        zero = jnp.zeros((8, 256), F32)
        sums.append(lax.fori_loop(0, 2, conv, (zero, zero)))
    store_stats(o_ref, sums)


def input_grad_kernel(members, x_ref, cot_ref, ng_ref, st_ref, gst_ref, o_ref):
    stats = moments(st_ref, members)
    gstats = group_totals(gst_ref)
    for f in range(2):
        mean, inv = stats[f]
        first, second = gstats[f][0] / members, gstats[f][1] / members

        def part(r, _):
            at = pl.ds(pl.multiple_of(r * 128, 128), 128)
            n = (x_ref[f, at, :].astype(F32) - mean) * inv
            term = inv * (ng_ref[f, at, :] - first - n * second)
            o_ref[f, at, :] = (cot_ref[f, at, :].astype(F32) + term).astype(BF16)
            return 0

        lax.fori_loop(0, 8, part, 0)


def block_kernel(x_ref, hid_ref, prev_ref, w_ref, o_ref):
    for f in range(2):

        def part(r, _):
            at = pl.ds(pl.multiple_of(r * 512, 512), 512)
            v = None
            for k in range(3):
                g = f - 2 + k
                lhs = hid_ref[g, at, :] if g >= 0 else prev_ref[g + 2, at, :]
                p = dot(lhs, w_ref[k])
                v = p if v is None else v + p
            o_ref[f, at, :] = (x_ref[f, at, :].astype(F32) + v).astype(BF16)
            return 0

        lax.fori_loop(0, 2, part, 0)


def coded(v):
    t = v * UNIT
    return (t * jnp.sqrt(jnp.abs(t))).astype(BF16)


def decoded(u):
    u = u.astype(F32)
    size = jnp.abs(u)
    root = jnp.exp(jnp.log(jnp.maximum(size, 1e-37)) * (2.0 / 3.0)) * (1.0 / UNIT)
    return jnp.where(size < 1e-37, 0.0, jnp.where(u < 0, -root, root))


def pair_kernel(g_ref, got_ref, own_ref, *sent):
    for k in range(4):

        def part(r, _):
            at = pl.multiple_of(r * 128, 128)
            rows = pl.ds(pl.multiple_of(at + k * 768, 128), 128)
            v = g_ref[rows, :] + got_ref[rows, :]
            if k == 0:
                own_ref[pl.ds(at, 128), :] = v
            else:
                sent[k - 1][pl.ds(at, 128), :] = coded(v)
            return 0

        lax.fori_loop(0, 6, part, 0)


def x_kernel(own_ref, a_ref, b_ref, c_ref, mine_ref, *sent):
    for k in range(4):

        def part(r, _):
            at = pl.multiple_of(r * 64, 64)
            rows = pl.ds(pl.multiple_of(at + k * 192, 64), 64)
            v = own_ref[rows, :] + decoded(a_ref[rows, :]) + decoded(b_ref[rows, :]) + decoded(c_ref[rows, :])
            (mine_ref, *sent)[k][pl.ds(at, 64), :] = v
            return 0

        lax.fori_loop(0, 3, part, 0)


def y_kernel(own_ref, a_ref, b_ref, c_ref, gst_ref, o_ref):
    code = coded(own_ref[...] + a_ref[...] + b_ref[...] + c_ref[...])
    rest, pieces = gst_ref[0], []
    for _ in range(3):
        piece = rest.astype(BF16).astype(F32)
        pieces.append(piece)
        rest = rest - piece
    sums = jnp.concatenate([*pieces, jnp.zeros_like(rest)], axis=0).astype(BF16)
    for peer in range(8):
        o_ref[peer, 0:192, :] = code
        o_ref[peer, 192:224, :] = sums


def z_kernel(u_ref, o_ref, gst_ref):
    def part(r, _):
        rows = pl.ds(pl.multiple_of(r * 64, 64), 64)
        total = decoded(u_ref[0, rows, :])
        for peer in range(1, 8):
            total = total + decoded(u_ref[peer, rows, :])
        o_ref[rows, :] = coded(total)
        return 0

    lax.fori_loop(0, 3, part, 0)
    sums = jnp.zeros((8, 128), F32)
    for peer in range(8):
        v = u_ref[peer, 192:224, :].astype(F32)
        sums = sums + ((v[0:8] + v[8:16]) + v[16:24])
    gst_ref[0] = sums


def half_kernel(info, u_ref, w_ref, acc_ref):
    acc = jnp.zeros((8, 128), F32)
    for unit in range(12):
        for part in range(4):
            v = decoded(u_ref[pl.ds(slab_rows(info, unit, part), 64), :])
            w_ref[unit * 256 + part * 64 : unit * 256 + part * 64 + 64, :] = v
            acc = acc + fold(v * v)
    acc_ref[...] = acc


def clip_kernel(clip_level, info, own_ref, acc_ref, other_ref, s_ref, t_ref, w_ref, b_ref, oacc_ref, sems):
    half_kernel(info, other_ref, b_ref, oacc_ref)
    acc = acc_ref[...] + oacc_ref[...]
    total = jnp.sum(jnp.sum(acc, axis=0, keepdims=True), axis=1, keepdims=True)
    scale = clip_level / jnp.maximum(jnp.sqrt(total), clip_level)
    copies = []
    for tap in range(12):
        mine = info[0] == tap // 6
        for lh in range(2):
            at = pl.ds(((tap % 6) * 2 + lh) * 256, 256)
            v = jnp.where(mine, own_ref[at, :], b_ref[at, :])
            w_ref[tap, :, lh * 128 : lh * 128 + 128] = v * scale
        target = s_ref.at[tap] if tap < 9 else t_ref.at[tap - 9]
        copies.append(pltpu.make_async_copy(w_ref.at[tap], target, sems.at[tap]))
        copies[-1].start()
    for c in copies:
        c.wait()


def in_hbm(x):
    return pltpu.with_memory_space_constraint(x, pltpu.HBM)


def swapped(x, axis):
    return lax.ppermute(x, axis, [(0, 1), (1, 0)])


def moved(x, axes, distance):
    n = lax.axis_size(axes)
    route = [(i, i + distance) for i in range(n) if 0 <= i + distance < n]
    return lax.ppermute(x, axes, route)


def shifts(sent, axis):
    n = lax.axis_size(axis)
    return [
        lax.ppermute(m, axis, [(i, (i + d) % n) for i in range(n)]) for d, m in enumerate(sent, 1)
    ]


def gathered(mine, axis):
    got = tied(shifts([mine] * 3, axis))
    return jnp.concatenate([mine, got[2], got[1], got[0]], axis=0)


def body(video_latents, cotangent, spatial_kernel, temporal_kernel):
    batch, frames, rows, columns, channels = video_latents.shape
    peers = lax.axis_size(HEIGHT)
    members = float(rows * peers * columns * (channels // GROUPS))
    clip_level = (
        channels * rows * peers * columns
        * math.sqrt(batch * lax.axis_size(DP) * frames * lax.axis_size(TM))
        / CLIP_DIVISOR
    )
    z = lax.axis_index(HEIGHT)
    info = jnp.stack(
        [lax.axis_index("core"), z, peers - 1 - z, lax.axis_index(TM), lax.axis_index("y")]
    ).astype(jnp.int32)
    pixels = rows * columns
    flat = (2, pixels, 256)
    x = video_latents.reshape(flat)
    cot = cotangent.reshape(flat)
    w9 = spatial_kernel
    w3 = spatial_kernel.reshape(3, 768, 256)
    gflop = 2 * 2048 * 256 * 256

    small = out((8, 8, 128), F32)
    edge = out((2, columns, 256), BF16)
    st, x_top, x_bot = call(stats_kernel, [small, edge, edge], [in_hbm(x)], 1 << 21)
    st = in_hbm(lax.all_to_all(st, HEIGHT, 0, 0, tiled=True))
    later = moved(cot, TM, -1)
    up = in_hbm(moved(x_bot, HEIGHT, 1))
    dn = in_hbm(moved(x_top, HEIGHT, -1))
    act, hid, slope = call(
        lambda *refs: forward_kernel(members, *refs),
        [out((2, 1280, 768), BF16), out(flat, BF16), out(flat, F32)],
        [info, in_hbm(x), up, dn, st, in_hbm(w3)],
        9 * gflop,
        smem=1,
        loose=(2, 3, 4),
        scratch=[
            pltpu.VMEM(edge.shape, BF16),
            pltpu.VMEM(edge.shape, BF16),
            pltpu.VMEM(small.shape, F32),
            pltpu.SemaphoreType.DMA((3,)),
        ],
    )
    pg, top, bot = call(
        pregrad_kernel, [out(flat, BF16), edge, edge], [cot, later, slope, temporal_kernel], 3 * gflop
    )
    (g,) = call(
        grads_kernel, [out((6144, 128), F32)], [info, act, pg, hid, cot, later], 12 * gflop, smem=1
    )
    send, top, bot = tied((g[3072:], top, bot))
    got = swapped(send, "core")
    gup = moved(bot, HEIGHT, 1)
    gdn = moved(top, HEIGHT, -1)
    quarter = out((768, 128), BF16)
    own, *sent = call(
        pair_kernel, [out((768, 128), F32), quarter, quarter, quarter], [g, got], 1 << 21
    )
    got = shifts(sent, TM)
    ng, gst = call(
        lambda *refs: backward_kernel(members, *refs),
        [out(flat, F32), out((1, 8, 128), F32)],
        [pg, gup, gdn, in_hbm(w9), in_hbm(x), in_hbm(st)],
        9 * gflop,
        scratch=[pltpu.VMEM((2, 1280, 256), BF16)] * 3,
    )
    got, gst = tied((got, gst))
    part = out((192, 128), F32)
    own, *sent = call(x_kernel, [part] * 4, [own, *got], 1 << 21)
    got = tied(shifts(sent, "y"))
    (pieces,) = call(y_kernel, [out((8, 224, 128), BF16)], [own, *got, gst], 1 << 20)
    pieces, hid_sent = tied((pieces, hid))
    pieces = lax.all_to_all(pieces, HEIGHT, 0, 0, tiled=True)
    prev = moved(hid_sent, TM, 1)
    mine, gst = call(z_kernel, [out((192, 128), BF16), out((1, 8, 128), F32)], [pieces], 1 << 20)
    (input_grad,) = call(
        lambda *refs: input_grad_kernel(members, *refs),
        [out(flat, BF16)],
        [x, cot, in_hbm(ng), in_hbm(st), gst],
        1 << 21,
    )
    mine = gathered(mine, "y")
    mine, prev, input_grad = tied((mine, prev, input_grad))
    (block_output,) = call(block_kernel, [out(flat, BF16)], [x, hid, prev, temporal_kernel], 3 * gflop)
    mine = gathered(mine, TM)
    mine, block_output = tied((mine, block_output))
    slab = (3072, 128)
    tile = out((8, 128), F32)
    own, acc = call(half_kernel, [out(slab, F32), tile], [info, mine], 1 << 21, smem=1)
    clipped_spatial, clipped_temporal = call(
        lambda *refs: clip_kernel(clip_level, *refs),
        [out((9, 256, 256), F32), out((3, 256, 256), F32)],
        [info, own, acc, swapped(mine, "core")],
        1 << 21,
        smem=1,
        outside=True,
        scratch=[
            pltpu.VMEM((12, 256, 256), F32),
            pltpu.VMEM(slab, F32),
            pltpu.VMEM(tile.shape, F32),
            pltpu.SemaphoreType.DMA((12,)),
        ],
    )
    return (
        block_output.reshape(video_latents.shape),
        input_grad.reshape(video_latents.shape),
        clipped_spatial.reshape(spatial_kernel.shape),
        clipped_temporal,
    )


def solution(mesh):
    sizes = (mesh.shape["dp"] // 2, 2, mesh.shape[TM], mesh.shape[HEIGHT])
    torus = Mesh(mesh.devices.reshape(sizes), (*DP, TM, HEIGHT))
    field = P(DP, TM, HEIGHT, None, None)
    return jax.shard_map(
        body, mesh=torus, in_specs=(field, field, P(), P()), out_specs=(field, field, P(), P()), check_vma=False
    )
```

```python
import math

import jax
import jax.numpy as jnp
from jax import lax
from jax.experimental import pallas as pl
from jax.experimental.pallas import tpu as pltpu
from jax.sharding import Mesh
from jax.sharding import PartitionSpec as P


GROUPS = 32
tied = lax.optimization_barrier
EPSILON = 1e-05
CLIP_DIVISOR = 20.0
F32 = jnp.float32
BF16 = jnp.bfloat16
DP = ("y", "core")
TM = "tm"
HEIGHT = "height"
UNIT = 2.0**40
VMEM = pl.BlockSpec(memory_space=pltpu.VMEM)
SMEM = pl.BlockSpec(memory_space=pltpu.SMEM)
ANY = pl.BlockSpec(memory_space=pl.ANY)
HBM = pl.BlockSpec(memory_space=pltpu.HBM)
NT = (((1,), (1,)), ((), ()))
TN = (((0,), (0,)), ((), ()))


def call(kernel, outs, args, flops, scratch=(), smem=0, limit=16, loose=(), outside=()):
    nbytes = sum(a.size * a.dtype.itemsize for a in (*args, *outs))
    specs = [SMEM] * smem + [ANY if i in loose else VMEM for i in range(smem, len(args))]
    return pl.pallas_call(
        kernel,
        out_shape=tuple(pltpu.HBM(o.shape, o.dtype) if i in outside else o for i, o in enumerate(outs)),
        in_specs=specs,
        out_specs=tuple(HBM if i in outside else VMEM for i in range(len(outs))),
        scratch_shapes=list(scratch),
        compiler_params=pltpu.CompilerParams(vmem_limit_bytes=limit << 20),
        cost_estimate=pl.CostEstimate(flops=flops, bytes_accessed=nbytes, transcendentals=0),
    )(*args)


def out(shape, dtype):
    return jax.ShapeDtypeStruct(shape, dtype)


def dot(a, b, dims=None):
    if dims is None:
        return jnp.dot(a, b, preferred_element_type=F32)
    return lax.dot_general(a, b, dims, preferred_element_type=F32)


def sigmoid(v):
    return 0.5 + 0.5 * jnp.tanh(0.5 * v)


def store_stats(o_ref, sums):
    rows = []
    for first, second in sums:
        for v in (first, second):
            t = jnp.sum(v, axis=0, keepdims=True)
            rows += [t[:, :128], t[:, 128:]]
    packed = jnp.concatenate(rows, axis=0)
    for peer in range(o_ref.shape[0]):
        o_ref[peer] = packed


def group_totals(st_ref):
    tot = st_ref[0]
    for peer in range(1, st_ref.shape[0]):
        tot = tot + st_ref[peer]
    lane = lax.broadcasted_iota(jnp.int32, tot.shape, 1)
    for d in (1, 2, 4):
        low = (lane & d) == 0
        tot = tot + jnp.where(low, pltpu.roll(tot, 128 - d, 1), pltpu.roll(tot, d, 1))
    res = []
    for f in range(tot.shape[0] // 4):
        r = [tot[4 * f + k : 4 * f + k + 1] for k in range(4)]
        res.append((jnp.concatenate(r[:2], axis=1), jnp.concatenate(r[2:], axis=1)))
    return res


def moments(st_ref, members):
    res = []
    for first, second in group_totals(st_ref):
        mean = first / members
        res.append((mean, lax.rsqrt(second / members - mean * mean + EPSILON)))
    return res


def fetched(*pairs, sems):
    copies = [pltpu.make_async_copy(a, b, sems.at[i]) for i, (a, b) in enumerate(pairs)]
    for c in copies:
        c.start()
    for c in copies:
        c.wait()


def fold(v):
    return jnp.sum(v.reshape(v.shape[0] // 8, 8, v.shape[1]), axis=0)


def stats_kernel(x_ref, o_ref, top_ref, bot_ref):
    sums = []
    for f in range(2):
        top_ref[f] = x_ref[f, 0:128, :]
        bot_ref[f] = x_ref[f, 896:1024, :]

        def step(r, carry):
            v = x_ref[f, pl.ds(pl.multiple_of(r * 128, 128), 128), :].astype(F32)
            return carry[0] + fold(v), carry[1] + fold(v * v)

        zero = jnp.zeros((8, 256), F32)
        sums.append(lax.fori_loop(0, 8, step, (zero, zero)))
    store_stats(o_ref, sums)


def shifted(v):
    row = lax.broadcasted_iota(jnp.int32, v.shape, 0)
    before = jnp.where(row == 0, 0.0, pltpu.roll(v, 1, 0))
    after = jnp.where(row == v.shape[0] - 1, 0.0, pltpu.roll(v, v.shape[0] - 1, 0))
    return before, after


def forward_kernel(
    members, info, x_ref, up_hbm, dn_hbm, st_hbm, w_hbm, act_ref, hid_ref, slope_ref,
    up_ref, dn_ref, st_ref, w_ref, sems,
):
    weights = pltpu.make_async_copy(w_hbm, w_ref, sems.at[3])
    weights.start()
    fetched((st_hbm, st_ref), (up_hbm, up_ref), (dn_hbm, dn_ref), sems=sems)
    keep_up = (info[1] > 0).astype(F32)
    keep_dn = (info[2] > 0).astype(F32)
    stats = moments(st_ref, members)
    for f in range(2):
        mean, inv = stats[f]

        def put(v, row, keep=None):
            n = (v.astype(F32) - mean) * inv
            a = n * sigmoid(n)
            if keep is not None:
                a = a * keep
            before, after = shifted(a)
            at = pl.ds(row, 128)
            act_ref[f, at, 0:256] = before.astype(BF16)
            act_ref[f, at, 256:512] = a.astype(BF16)
            act_ref[f, at, 512:768] = after.astype(BF16)

        put(up_ref[f], 0, keep_up)
        put(dn_ref[f], 9 * 128, keep_dn)

        def line(r, _):
            at = pl.multiple_of(r * 128, 128)
            put(x_ref[f, pl.ds(at, 128), :], pl.multiple_of(at + 128, 128))
            return 0

        lax.fori_loop(0, 8, line, 0)
        if f == 0:
            weights.wait()

        def conv(r, _):
            at = pl.multiple_of(r * 512, 512)
            v = None
            for i in range(3):
                lhs = act_ref[f, pl.ds(pl.multiple_of(at + i * 128, 128), 512), :]
                part = dot(lhs, w_ref[i])
                v = part if v is None else v + part
            s = sigmoid(v)
            hid_ref[f, pl.ds(at, 512), :] = (v * s).astype(BF16)
            slope_ref[f, pl.ds(at, 512), :] = s * (1.0 + v * (1.0 - s))
            return 0

        lax.fori_loop(0, 2, conv, 0)


def pregrad_kernel(cot_ref, later_ref, slope_ref, w_ref, pg_ref, top_ref, bot_ref):
    for f in range(2):

        def part(r, _):
            at = pl.ds(pl.multiple_of(r * 512, 512), 512)
            v = None
            for k in range(3):
                g = f + 2 - k
                lhs = cot_ref[g, at, :] if g < 2 else later_ref[g - 2, at, :]
                p = dot(lhs, w_ref[k], NT)
                v = p if v is None else v + p
            pg_ref[f, at, :] = (v * slope_ref[f, at, :]).astype(BF16)
            return 0

        lax.fori_loop(0, 2, part, 0)
        top_ref[f] = pg_ref[f, 0:128, :]
        bot_ref[f] = pg_ref[f, 896:1024, :]


def slab_rows(info, unit, part):
    piece = (unit % 3) * 4 + part
    x, y = (unit // 3 - info[3]) & 3, (piece // 3 - info[4]) & 3
    return pl.multiple_of(x * 768 + y * 192 + (piece % 3) * 64, 64)


def grads_kernel(info, act_ref, pg_ref, hid_ref, cot_ref, later_ref, g_ref):
    def put(tap, v):
        base = ((tap // 6) ^ info[0]) * 3072
        for lh in range(2):
            for part in range(4):
                at = pl.multiple_of(base + slab_rows(info, (tap % 6) * 2 + lh, part), 64)
                g_ref[pl.ds(at, 64), :] = v[part * 64 : part * 64 + 64, lh * 128 : lh * 128 + 128]

    for i in range(3):
        for j in range(3):
            v = None
            for f in range(2):
                lhs = act_ref[f, i * 128 : i * 128 + 1024, j * 256 : j * 256 + 256]
                p = dot(lhs, pg_ref[f], TN)
                v = p if v is None else v + p
            put(3 * i + j, v)
    for k in range(3):
        v = None
        for f in range(2):
            g = f + 2 - k
            rhs = cot_ref[g] if g < 2 else later_ref[g - 2]
            p = dot(hid_ref[f], rhs, TN)
            v = p if v is None else v + p
        put(9 + k, v)


def backward_kernel(
    members, pg_ref, up_ref, dn_ref, w_hbm, x_hbm, st_hbm, ng_hbm, o_ref,
    a_ref, b_ref, c_ref, w_ref, x_ref, st_ref, ng_ref, sems,
):
    loads = [(w_hbm, w_ref), (x_hbm, x_ref), (st_hbm, st_ref)]
    loads = [pltpu.make_async_copy(a, b, sems.at[i]) for i, (a, b) in enumerate(loads)]
    for c in loads:
        c.start()
    stats = None
    stores = []
    sums = []
    for f in range(2):

        def put(v, row):
            v = v.astype(F32)
            before, after = shifted(v)
            at = pl.ds(row, 128)
            a_ref[f, at, :] = after.astype(BF16)
            b_ref[f, at, :] = v.astype(BF16)
            c_ref[f, at, :] = before.astype(BF16)

        put(up_ref[f], 0)
        put(dn_ref[f], 9 * 128)

        def line(r, _):
            at = pl.multiple_of(r * 128, 128)
            put(pg_ref[f, pl.ds(at, 128), :], pl.multiple_of(at + 128, 128))
            return 0

        lax.fori_loop(0, 8, line, 0)
        if f == 0:
            for c in loads:
                c.wait()
            stats = moments(st_ref, members)
        mean, inv = stats[f]

        def conv(r, carry):
            at = pl.multiple_of(r * 512, 512)
            v = None
            for i in range(3):
                rows = pl.ds(pl.multiple_of(at + (2 - i) * 128, 128), 512)
                for j, ref in enumerate((a_ref, b_ref, c_ref)):
                    p = dot(ref[f, rows, :], w_ref[i, j], NT)
                    v = p if v is None else v + p
            n = (x_ref[f, pl.ds(at, 512), :].astype(F32) - mean) * inv
            s = sigmoid(n)
            ng = v * (s * (1.0 + n * (1.0 - s)))
            ng_ref[f, pl.ds(at, 512), :] = ng
            return carry[0] + fold(ng), carry[1] + fold(ng * n)

        zero = jnp.zeros((8, 256), F32)
        sums.append(lax.fori_loop(0, 2, conv, (zero, zero)))
        stores.append(pltpu.make_async_copy(ng_ref.at[f], ng_hbm.at[f], sems.at[3 + f]))
        stores[-1].start()
    store_stats(o_ref, sums)
    for c in stores:
        c.wait()


def input_grad_kernel(members, x_ref, cot_ref, ng_ref, st_ref, gst_ref, o_ref):
    stats = moments(st_ref, members)
    gstats = group_totals(gst_ref)
    for f in range(2):
        mean, inv = stats[f]
        first, second = gstats[f][0] / members, gstats[f][1] / members

        def part(r, _):
            at = pl.ds(pl.multiple_of(r * 128, 128), 128)
            n = (x_ref[f, at, :].astype(F32) - mean) * inv
            term = inv * (ng_ref[f, at, :] - first - n * second)
            o_ref[f, at, :] = (cot_ref[f, at, :].astype(F32) + term).astype(BF16)
            return 0

        lax.fori_loop(0, 8, part, 0)


def block_kernel(x_ref, hid_ref, prev_ref, w_ref, o_ref):
    for f in range(2):

        def part(r, _):
            at = pl.ds(pl.multiple_of(r * 512, 512), 512)
            v = None
            for k in range(3):
                g = f - 2 + k
                lhs = hid_ref[g, at, :] if g >= 0 else prev_ref[g + 2, at, :]
                p = dot(lhs, w_ref[k])
                v = p if v is None else v + p
            o_ref[f, at, :] = (x_ref[f, at, :].astype(F32) + v).astype(BF16)
            return 0

        lax.fori_loop(0, 2, part, 0)


def coded(v):
    t = v * UNIT
    return (t * jnp.sqrt(jnp.abs(t))).astype(BF16)


def decoded(u):
    u = u.astype(F32)
    size = jnp.abs(u)
    root = jnp.exp(jnp.log(jnp.maximum(size, 1e-37)) * (2.0 / 3.0)) * (1.0 / UNIT)
    return jnp.where(size < 1e-37, 0.0, jnp.where(u < 0, -root, root))


def pair_kernel(g_ref, got_ref, own_ref, *sent):
    for k in range(4):

        def part(r, _):
            at = pl.multiple_of(r * 128, 128)
            rows = pl.ds(pl.multiple_of(at + k * 768, 128), 128)
            v = g_ref[rows, :] + got_ref[rows, :]
            if k == 0:
                own_ref[pl.ds(at, 128), :] = v
            else:
                sent[k - 1][pl.ds(at, 128), :] = coded(v)
            return 0

        lax.fori_loop(0, 6, part, 0)


def x_kernel(own_ref, a_ref, b_ref, c_ref, mine_ref, *sent):
    for k in range(4):

        def part(r, _):
            at = pl.multiple_of(r * 64, 64)
            rows = pl.ds(pl.multiple_of(at + k * 192, 64), 64)
            v = own_ref[rows, :] + decoded(a_ref[rows, :]) + decoded(b_ref[rows, :]) + decoded(c_ref[rows, :])
            (mine_ref, *sent)[k][pl.ds(at, 64), :] = v
            return 0

        lax.fori_loop(0, 3, part, 0)


def y_kernel(own_ref, a_ref, b_ref, c_ref, gst_ref, o_ref):
    code = coded(own_ref[...] + a_ref[...] + b_ref[...] + c_ref[...])
    rest, pieces = gst_ref[0], []
    for _ in range(3):
        piece = rest.astype(BF16).astype(F32)
        pieces.append(piece)
        rest = rest - piece
    sums = jnp.concatenate([*pieces, jnp.zeros_like(rest)], axis=0).astype(BF16)
    for peer in range(8):
        o_ref[peer, 0:192, :] = code
        o_ref[peer, 192:224, :] = sums


def z_kernel(u_ref, o_ref, gst_ref):
    def part(r, _):
        rows = pl.ds(pl.multiple_of(r * 64, 64), 64)
        total = decoded(u_ref[0, rows, :])
        for peer in range(1, 8):
            total = total + decoded(u_ref[peer, rows, :])
        o_ref[rows, :] = coded(total)
        return 0

    lax.fori_loop(0, 3, part, 0)
    sums = jnp.zeros((8, 128), F32)
    for peer in range(8):
        v = u_ref[peer, 192:224, :].astype(F32)
        sums = sums + ((v[0:8] + v[8:16]) + v[16:24])
    gst_ref[0] = sums


def half_kernel(info, u_ref, w_ref, acc_ref):
    acc = jnp.zeros((8, 128), F32)
    for unit in range(12):
        for part in range(4):
            v = decoded(u_ref[pl.ds(slab_rows(info, unit, part), 64), :])
            w_ref[unit * 256 + part * 64 : unit * 256 + part * 64 + 64, :] = v
            acc = acc + fold(v * v)
    acc_ref[...] = acc


def clip_kernel(clip_level, info, own_ref, acc_ref, other_ref, s_ref, t_ref, w_ref, b_ref, oacc_ref, sems):
    half_kernel(info, other_ref, b_ref, oacc_ref)
    acc = acc_ref[...] + oacc_ref[...]
    total = jnp.sum(jnp.sum(acc, axis=0, keepdims=True), axis=1, keepdims=True)
    scale = clip_level / jnp.maximum(jnp.sqrt(total), clip_level)
    copies = []
    for tap in range(12):
        mine = info[0] == tap // 6
        for lh in range(2):
            at = pl.ds(((tap % 6) * 2 + lh) * 256, 256)
            v = jnp.where(mine, own_ref[at, :], b_ref[at, :])
            w_ref[tap, :, lh * 128 : lh * 128 + 128] = v * scale
        target = s_ref.at[tap] if tap < 9 else t_ref.at[tap - 9]
        copies.append(pltpu.make_async_copy(w_ref.at[tap], target, sems.at[tap]))
        copies[-1].start()
    for c in copies:
        c.wait()


def in_hbm(x):
    return pltpu.with_memory_space_constraint(x, pltpu.HBM)


def swapped(x, axis):
    return lax.ppermute(x, axis, [(0, 1), (1, 0)])


def moved(x, axes, distance):
    n = lax.axis_size(axes)
    route = [(i, i + distance) for i in range(n) if 0 <= i + distance < n]
    return lax.ppermute(x, axes, route)


def shifts(sent, axis):
    n = lax.axis_size(axis)
    return [
        lax.ppermute(m, axis, [(i, (i + d) % n) for i in range(n)]) for d, m in enumerate(sent, 1)
    ]


def gathered(mine, axis):
    got = tied(shifts([mine] * 3, axis))
    return jnp.concatenate([mine, got[2], got[1], got[0]], axis=0)


def body(video_latents, cotangent, spatial_kernel, temporal_kernel):
    batch, frames, rows, columns, channels = video_latents.shape
    peers = lax.axis_size(HEIGHT)
    members = float(rows * peers * columns * (channels // GROUPS))
    clip_level = (
        channels * rows * peers * columns
        * math.sqrt(batch * lax.axis_size(DP) * frames * lax.axis_size(TM))
        / CLIP_DIVISOR
    )
    z = lax.axis_index(HEIGHT)
    info = jnp.stack(
        [lax.axis_index("core"), z, peers - 1 - z, lax.axis_index(TM), lax.axis_index("y")]
    ).astype(jnp.int32)
    pixels = rows * columns
    flat = (2, pixels, 256)
    x = video_latents.reshape(flat)
    cot = cotangent.reshape(flat)
    w9 = spatial_kernel
    w3 = spatial_kernel.reshape(3, 768, 256)
    gflop = 2 * 2048 * 256 * 256

    small = out((8, 8, 128), F32)
    edge = out((2, columns, 256), BF16)
    st, x_top, x_bot = call(stats_kernel, [small, edge, edge], [in_hbm(x)], 1 << 21)
    st = in_hbm(lax.all_to_all(st, HEIGHT, 0, 0, tiled=True))
    later = moved(cot, TM, -1)
    up = in_hbm(moved(x_bot, HEIGHT, 1))
    dn = in_hbm(moved(x_top, HEIGHT, -1))
    act, hid, slope = call(
        lambda *refs: forward_kernel(members, *refs),
        [out((2, 1280, 768), BF16), out(flat, BF16), out(flat, F32)],
        [info, in_hbm(x), up, dn, st, in_hbm(w3)],
        9 * gflop,
        smem=1,
        loose=(2, 3, 4, 5),
        scratch=[
            pltpu.VMEM(edge.shape, BF16),
            pltpu.VMEM(edge.shape, BF16),
            pltpu.VMEM(small.shape, F32),
            pltpu.VMEM(w3.shape, BF16),
            pltpu.SemaphoreType.DMA((4,)),
        ],
    )
    pg, top, bot = call(
        pregrad_kernel, [out(flat, BF16), edge, edge], [cot, later, slope, temporal_kernel], 3 * gflop
    )
    (g,) = call(
        grads_kernel, [out((6144, 128), F32)], [info, act, pg, hid, cot, later], 12 * gflop, smem=1
    )
    send, top, bot = tied((g[3072:], top, bot))
    got = swapped(send, "core")
    gup = moved(bot, HEIGHT, 1)
    gdn = moved(top, HEIGHT, -1)
    quarter = out((768, 128), BF16)
    own, *sent = call(
        pair_kernel, [out((768, 128), F32), quarter, quarter, quarter], [g, got], 1 << 21
    )
    got = shifts(sent, TM)
    ng, gst = call(
        lambda *refs: backward_kernel(members, *refs),
        [out(flat, F32), out((1, 8, 128), F32)],
        [pg, gup, gdn, in_hbm(w9), in_hbm(x), st],
        9 * gflop,
        loose=(3, 4, 5),
        outside=(0,),
        scratch=[pltpu.VMEM((2, 1280, 256), BF16)] * 3
        + [
            pltpu.VMEM(w9.shape, BF16),
            pltpu.VMEM(flat, BF16),
            pltpu.VMEM(small.shape, F32),
            pltpu.VMEM(flat, F32),
            pltpu.SemaphoreType.DMA((5,)),
        ],
    )
    got, gst = tied((got, gst))
    part = out((192, 128), F32)
    own, *sent = call(x_kernel, [part] * 4, [own, *got], 1 << 21)
    own, sent, hid_sent = tied((own, sent, hid))
    prev = moved(hid_sent, TM, 1)
    got = shifts(sent, "y")
    got = tied(got)
    (pieces,) = call(y_kernel, [out((8, 224, 128), BF16)], [own, *got, gst], 1 << 20)
    pieces = lax.all_to_all(pieces, HEIGHT, 0, 0, tiled=True)
    mine, gst = call(z_kernel, [out((192, 128), BF16), out((1, 8, 128), F32)], [pieces], 1 << 20)
    (input_grad,) = call(
        lambda *refs: input_grad_kernel(members, *refs),
        [out(flat, BF16)],
        [x, cot, in_hbm(ng), in_hbm(st), gst],
        1 << 21,
    )
    mine = gathered(mine, "y")
    mine, prev, input_grad = tied((mine, prev, input_grad))
    (block_output,) = call(block_kernel, [out(flat, BF16)], [x, hid, prev, temporal_kernel], 3 * gflop)
    mine = gathered(mine, TM)
    mine, block_output = tied((mine, block_output))
    slab = (3072, 128)
    tile = out((8, 128), F32)
    own, acc = call(half_kernel, [out(slab, F32), tile], [info, mine], 1 << 21, smem=1)
    clipped_spatial, clipped_temporal = call(
        lambda *refs: clip_kernel(clip_level, *refs),
        [out((9, 256, 256), F32), out((3, 256, 256), F32)],
        [info, own, acc, swapped(mine, "core")],
        1 << 21,
        smem=1,
        outside=(0, 1),
        scratch=[
            pltpu.VMEM((12, 256, 256), F32),
            pltpu.VMEM(slab, F32),
            pltpu.VMEM(tile.shape, F32),
            pltpu.SemaphoreType.DMA((12,)),
        ],
    )
    return (
        block_output.reshape(video_latents.shape),
        input_grad.reshape(video_latents.shape),
        clipped_spatial.reshape(spatial_kernel.shape),
        clipped_temporal,
    )


def solution(mesh):
    sizes = (mesh.shape["dp"] // 2, 2, mesh.shape[TM], mesh.shape[HEIGHT])
    torus = Mesh(mesh.devices.reshape(sizes), (*DP, TM, HEIGHT))
    field = P(DP, TM, HEIGHT, None, None)
    return jax.shard_map(
        body, mesh=torus, in_specs=(field, field, P(), P()), out_specs=(field, field, P(), P()), check_vma=False
    )
```

```python
import math

import jax
import jax.numpy as jnp
from jax import lax
from jax.experimental import pallas as pl
from jax.experimental.pallas import tpu as pltpu
from jax.sharding import Mesh
from jax.sharding import PartitionSpec as P


GROUPS = 32
tied = lax.optimization_barrier
EPSILON = 1e-05
CLIP_DIVISOR = 20.0
F32 = jnp.float32
BF16 = jnp.bfloat16
DP = ("y", "core")
TM = "tm"
HEIGHT = "height"
UNIT = 2.0**40
VMEM = pl.BlockSpec(memory_space=pltpu.VMEM)
SMEM = pl.BlockSpec(memory_space=pltpu.SMEM)
ANY = pl.BlockSpec(memory_space=pl.ANY)
HBM = pl.BlockSpec(memory_space=pltpu.HBM)
NT = (((1,), (1,)), ((), ()))
TN = (((0,), (0,)), ((), ()))


def call(kernel, outs, args, flops, scratch=(), smem=0, limit=16, loose=(), outside=()):
    nbytes = sum(a.size * a.dtype.itemsize for a in (*args, *outs))
    specs = [SMEM] * smem + [ANY if i in loose else VMEM for i in range(smem, len(args))]
    return pl.pallas_call(
        kernel,
        out_shape=tuple(pltpu.HBM(o.shape, o.dtype) if i in outside else o for i, o in enumerate(outs)),
        in_specs=specs,
        out_specs=tuple(HBM if i in outside else VMEM for i in range(len(outs))),
        scratch_shapes=list(scratch),
        compiler_params=pltpu.CompilerParams(vmem_limit_bytes=limit << 20),
        cost_estimate=pl.CostEstimate(flops=flops, bytes_accessed=nbytes, transcendentals=0),
    )(*args)


def out(shape, dtype):
    return jax.ShapeDtypeStruct(shape, dtype)


def dot(a, b, dims=None):
    if dims is None:
        return jnp.dot(a, b, preferred_element_type=F32)
    return lax.dot_general(a, b, dims, preferred_element_type=F32)


def sigmoid(v):
    return 0.5 + 0.5 * jnp.tanh(0.5 * v)


def store_stats(o_ref, sums):
    rows = []
    for first, second in sums:
        for v in (first, second):
            t = jnp.sum(v, axis=0, keepdims=True)
            rows += [t[:, :128], t[:, 128:]]
    packed = jnp.concatenate(rows, axis=0)
    for peer in range(o_ref.shape[0]):
        o_ref[peer] = packed


def group_totals(st_ref):
    tot = st_ref[0]
    for peer in range(1, st_ref.shape[0]):
        tot = tot + st_ref[peer]
    lane = lax.broadcasted_iota(jnp.int32, tot.shape, 1)
    for d in (1, 2, 4):
        low = (lane & d) == 0
        tot = tot + jnp.where(low, pltpu.roll(tot, 128 - d, 1), pltpu.roll(tot, d, 1))
    res = []
    for f in range(tot.shape[0] // 4):
        r = [tot[4 * f + k : 4 * f + k + 1] for k in range(4)]
        res.append((jnp.concatenate(r[:2], axis=1), jnp.concatenate(r[2:], axis=1)))
    return res


def moments(st_ref, members):
    res = []
    for first, second in group_totals(st_ref):
        mean = first / members
        res.append((mean, lax.rsqrt(second / members - mean * mean + EPSILON)))
    return res


CHUNK = 256


def woven(put, conv, ready):
    chunks = 1024 // CHUNK
    for line in range(10):
        put(0, line)
    ready()
    done = 0
    for c in range(chunks):
        conv(0, c * CHUNK)
        upto = 10 * (c + 1) // chunks
        for line in range(done, upto):
            put(1, line)
        done = upto
    for c in range(chunks):
        conv(1, c * CHUNK)


def fetched(*pairs, sems):
    copies = [pltpu.make_async_copy(a, b, sems.at[i]) for i, (a, b) in enumerate(pairs)]
    for c in copies:
        c.start()
    for c in copies:
        c.wait()


def fold(v):
    return jnp.sum(v.reshape(v.shape[0] // 8, 8, v.shape[1]), axis=0)


def stats_kernel(x_ref, o_ref, top_ref, bot_ref):
    sums = []
    for f in range(2):
        top_ref[f] = x_ref[f, 0:128, :]
        bot_ref[f] = x_ref[f, 896:1024, :]

        def step(r, carry):
            v = x_ref[f, pl.ds(pl.multiple_of(r * 128, 128), 128), :].astype(F32)
            return carry[0] + fold(v), carry[1] + fold(v * v)

        zero = jnp.zeros((8, 256), F32)
        sums.append(lax.fori_loop(0, 8, step, (zero, zero)))
    store_stats(o_ref, sums)


def shifted(v):
    row = lax.broadcasted_iota(jnp.int32, v.shape, 0)
    before = jnp.where(row == 0, 0.0, pltpu.roll(v, 1, 0))
    after = jnp.where(row == v.shape[0] - 1, 0.0, pltpu.roll(v, v.shape[0] - 1, 0))
    return before, after


def forward_kernel(
    members, info, x_ref, up_hbm, dn_hbm, st_hbm, w_hbm, act_ref, hid_ref, slope_ref,
    up_ref, dn_ref, st_ref, w_ref, sems,
):
    weights = pltpu.make_async_copy(w_hbm, w_ref, sems.at[3])
    weights.start()
    fetched((st_hbm, st_ref), (up_hbm, up_ref), (dn_hbm, dn_ref), sems=sems)
    keep_up = (info[1] > 0).astype(F32)
    keep_dn = (info[2] > 0).astype(F32)
    stats = moments(st_ref, members)

    def put(f, line):
        mean, inv = stats[f]
        v = up_ref[f] if line == 0 else dn_ref[f] if line == 9 else x_ref[f, line * 128 - 128 : line * 128, :]
        n = (v.astype(F32) - mean) * inv
        a = n * sigmoid(n)
        if line == 0:
            a = a * keep_up
        if line == 9:
            a = a * keep_dn
        before, after = shifted(a)
        rows = slice(line * 128, line * 128 + 128)
        act_ref[f, rows, 0:256] = before.astype(BF16)
        act_ref[f, rows, 256:512] = a.astype(BF16)
        act_ref[f, rows, 512:768] = after.astype(BF16)

    def conv(f, at):
        v = None
        for i in range(3):
            part = dot(act_ref[f, at + i * 128 : at + i * 128 + CHUNK, :], w_ref[i])
            v = part if v is None else v + part
        s = sigmoid(v)
        hid_ref[f, at : at + CHUNK, :] = (v * s).astype(BF16)
        slope_ref[f, at : at + CHUNK, :] = s * (1.0 + v * (1.0 - s))

    woven(put, conv, weights.wait)


def pregrad_kernel(cot_ref, later_ref, slope_ref, w_ref, pg_ref, top_ref, bot_ref):
    for f in range(2):

        def part(r, _):
            at = pl.ds(pl.multiple_of(r * 512, 512), 512)
            v = None
            for k in range(3):
                g = f + 2 - k
                lhs = cot_ref[g, at, :] if g < 2 else later_ref[g - 2, at, :]
                p = dot(lhs, w_ref[k], NT)
                v = p if v is None else v + p
            pg_ref[f, at, :] = (v * slope_ref[f, at, :]).astype(BF16)
            return 0

        lax.fori_loop(0, 2, part, 0)
        top_ref[f] = pg_ref[f, 0:128, :]
        bot_ref[f] = pg_ref[f, 896:1024, :]


def slab_rows(info, unit, part):
    piece = (unit % 3) * 4 + part
    x, y = (unit // 3 - info[3]) & 3, (piece // 3 - info[4]) & 3
    return pl.multiple_of(x * 768 + y * 192 + (piece % 3) * 64, 64)


def grads_kernel(info, act_ref, pg_ref, hid_ref, cot_ref, later_ref, g_ref):
    def put(tap, v):
        base = ((tap // 6) ^ info[0]) * 3072
        for lh in range(2):
            for part in range(4):
                at = pl.multiple_of(base + slab_rows(info, (tap % 6) * 2 + lh, part), 64)
                g_ref[pl.ds(at, 64), :] = v[part * 64 : part * 64 + 64, lh * 128 : lh * 128 + 128]

    for i in range(3):
        for j in range(3):
            v = None
            for f in range(2):
                lhs = act_ref[f, i * 128 : i * 128 + 1024, j * 256 : j * 256 + 256]
                p = dot(lhs, pg_ref[f], TN)
                v = p if v is None else v + p
            put(3 * i + j, v)
    for k in range(3):
        v = None
        for f in range(2):
            g = f + 2 - k
            rhs = cot_ref[g] if g < 2 else later_ref[g - 2]
            p = dot(hid_ref[f], rhs, TN)
            v = p if v is None else v + p
        put(9 + k, v)


def backward_kernel(
    members, pg_ref, up_ref, dn_ref, w_hbm, x_hbm, st_hbm, ng_hbm, o_ref,
    g_ref, w_ref, x_ref, st_ref, ng_ref, sems,
):
    loads = [(x_hbm, x_ref), (st_hbm, st_ref)]
    for i in range(3):
        for j in range(3):
            loads.append((w_hbm.at[i, j], w_ref.at[i, :, j * 256 : j * 256 + 256]))
    loads = [pltpu.make_async_copy(a, b, sems.at[i]) for i, (a, b) in enumerate(loads)]
    for c in loads:
        c.start()
    state = []
    sums = [[jnp.zeros((8, 256), F32)] * 2 for _ in range(2)]

    def ready():
        for c in loads:
            c.wait()
        state.extend(moments(st_ref, members))

    def put(f, line):
        v = up_ref[f] if line == 0 else dn_ref[f] if line == 9 else pg_ref[f, line * 128 - 128 : line * 128, :]
        before, after = shifted(v.astype(F32))
        rows = slice(line * 128, line * 128 + 128)
        g_ref[f, rows, 0:256] = after.astype(BF16)
        g_ref[f, rows, 256:512] = v
        g_ref[f, rows, 512:768] = before.astype(BF16)

    def conv(f, at):
        mean, inv = state[f]
        v = None
        for i in range(3):
            start = at + (2 - i) * 128
            p = dot(g_ref[f, start : start + CHUNK, :], w_ref[i], NT)
            v = p if v is None else v + p
        n = (x_ref[f, at : at + CHUNK, :].astype(F32) - mean) * inv
        s = sigmoid(n)
        ng = v * (s * (1.0 + n * (1.0 - s)))
        ng_ref[f, at : at + CHUNK, :] = ng
        sums[f] = [sums[f][0] + fold(ng), sums[f][1] + fold(ng * n)]

    woven(put, conv, ready)
    store_stats(o_ref, sums)
    store = pltpu.make_async_copy(ng_ref, ng_hbm, sems.at[11])
    store.start()
    store.wait()


def input_grad_kernel(members, x_ref, cot_ref, ng_ref, st_ref, gst_ref, o_ref):
    stats = moments(st_ref, members)
    gstats = group_totals(gst_ref)
    for f in range(2):
        mean, inv = stats[f]
        first, second = gstats[f][0] / members, gstats[f][1] / members

        def part(r, _):
            at = pl.ds(pl.multiple_of(r * 128, 128), 128)
            n = (x_ref[f, at, :].astype(F32) - mean) * inv
            term = inv * (ng_ref[f, at, :] - first - n * second)
            o_ref[f, at, :] = (cot_ref[f, at, :].astype(F32) + term).astype(BF16)
            return 0

        lax.fori_loop(0, 8, part, 0)


def block_kernel(x_ref, hid_ref, prev_ref, w_ref, o_ref):
    for f in range(2):

        def part(r, _):
            at = pl.ds(pl.multiple_of(r * 512, 512), 512)
            v = None
            for k in range(3):
                g = f - 2 + k
                lhs = hid_ref[g, at, :] if g >= 0 else prev_ref[g + 2, at, :]
                p = dot(lhs, w_ref[k])
                v = p if v is None else v + p
            o_ref[f, at, :] = (x_ref[f, at, :].astype(F32) + v).astype(BF16)
            return 0

        lax.fori_loop(0, 2, part, 0)


def coded(v):
    t = v * UNIT
    return (t * jnp.sqrt(jnp.abs(t))).astype(BF16)


def decoded(u):
    u = u.astype(F32)
    size = jnp.abs(u)
    root = jnp.exp(jnp.log(jnp.maximum(size, 1e-37)) * (2.0 / 3.0)) * (1.0 / UNIT)
    return jnp.where(size < 1e-37, 0.0, jnp.where(u < 0, -root, root))


def pair_kernel(g_ref, got_ref, own_ref, *sent):
    for k in range(4):

        def part(r, _):
            at = pl.multiple_of(r * 128, 128)
            rows = pl.ds(pl.multiple_of(at + k * 768, 128), 128)
            v = g_ref[rows, :] + got_ref[rows, :]
            if k == 0:
                own_ref[pl.ds(at, 128), :] = v
            else:
                sent[k - 1][pl.ds(at, 128), :] = coded(v)
            return 0

        lax.fori_loop(0, 6, part, 0)


def x_kernel(own_ref, a_ref, b_ref, c_ref, mine_ref, *sent):
    for k in range(4):

        def part(r, _):
            at = pl.multiple_of(r * 64, 64)
            rows = pl.ds(pl.multiple_of(at + k * 192, 64), 64)
            v = own_ref[rows, :] + decoded(a_ref[rows, :]) + decoded(b_ref[rows, :]) + decoded(c_ref[rows, :])
            (mine_ref, *sent)[k][pl.ds(at, 64), :] = v
            return 0

        lax.fori_loop(0, 3, part, 0)


def y_kernel(own_ref, a_ref, b_ref, c_ref, gst_ref, o_ref):
    code = coded(own_ref[...] + a_ref[...] + b_ref[...] + c_ref[...])
    rest, pieces = gst_ref[0], []
    for _ in range(3):
        piece = rest.astype(BF16).astype(F32)
        pieces.append(piece)
        rest = rest - piece
    sums = jnp.concatenate([*pieces, jnp.zeros_like(rest)], axis=0).astype(BF16)
    for peer in range(8):
        o_ref[peer, 0:192, :] = code
        o_ref[peer, 192:224, :] = sums


def z_kernel(u_ref, o_ref, gst_ref):
    def part(r, _):
        rows = pl.ds(pl.multiple_of(r * 64, 64), 64)
        total = decoded(u_ref[0, rows, :])
        for peer in range(1, 8):
            total = total + decoded(u_ref[peer, rows, :])
        o_ref[rows, :] = coded(total)
        return 0

    lax.fori_loop(0, 3, part, 0)
    sums = jnp.zeros((8, 128), F32)
    for peer in range(8):
        v = u_ref[peer, 192:224, :].astype(F32)
        sums = sums + ((v[0:8] + v[8:16]) + v[16:24])
    gst_ref[0] = sums


def half_kernel(info, u_ref, w_ref, acc_ref):
    acc = jnp.zeros((8, 128), F32)
    for unit in range(12):
        for part in range(4):
            v = decoded(u_ref[pl.ds(slab_rows(info, unit, part), 64), :])
            w_ref[unit * 256 + part * 64 : unit * 256 + part * 64 + 64, :] = v
            acc = acc + fold(v * v)
    acc_ref[...] = acc


def clip_kernel(clip_level, info, own_ref, acc_ref, other_ref, s_ref, t_ref, w_ref, b_ref, oacc_ref, sems):
    half_kernel(info, other_ref, b_ref, oacc_ref)
    acc = acc_ref[...] + oacc_ref[...]
    total = jnp.sum(jnp.sum(acc, axis=0, keepdims=True), axis=1, keepdims=True)
    scale = clip_level / jnp.maximum(jnp.sqrt(total), clip_level)
    copies = []
    for tap in range(12):
        mine = info[0] == tap // 6
        for lh in range(2):
            at = pl.ds(((tap % 6) * 2 + lh) * 256, 256)
            v = jnp.where(mine, own_ref[at, :], b_ref[at, :])
            w_ref[tap, :, lh * 128 : lh * 128 + 128] = v * scale
        target = s_ref.at[tap] if tap < 9 else t_ref.at[tap - 9]
        copies.append(pltpu.make_async_copy(w_ref.at[tap], target, sems.at[tap]))
        copies[-1].start()
    for c in copies:
        c.wait()


def in_hbm(x):
    return pltpu.with_memory_space_constraint(x, pltpu.HBM)


def swapped(x, axis):
    return lax.ppermute(x, axis, [(0, 1), (1, 0)])


def moved(x, axes, distance):
    n = lax.axis_size(axes)
    route = [(i, i + distance) for i in range(n) if 0 <= i + distance < n]
    return lax.ppermute(x, axes, route)


def shifts(sent, axis):
    n = lax.axis_size(axis)
    return [
        lax.ppermute(m, axis, [(i, (i + d) % n) for i in range(n)]) for d, m in enumerate(sent, 1)
    ]


def gathered(mine, axis):
    got = tied(shifts([mine] * 3, axis))
    return jnp.concatenate([mine, got[2], got[1], got[0]], axis=0)


def body(video_latents, cotangent, spatial_kernel, temporal_kernel):
    batch, frames, rows, columns, channels = video_latents.shape
    peers = lax.axis_size(HEIGHT)
    members = float(rows * peers * columns * (channels // GROUPS))
    clip_level = (
        channels * rows * peers * columns
        * math.sqrt(batch * lax.axis_size(DP) * frames * lax.axis_size(TM))
        / CLIP_DIVISOR
    )
    z = lax.axis_index(HEIGHT)
    info = jnp.stack(
        [lax.axis_index("core"), z, peers - 1 - z, lax.axis_index(TM), lax.axis_index("y")]
    ).astype(jnp.int32)
    pixels = rows * columns
    flat = (2, pixels, 256)
    x = video_latents.reshape(flat)
    cot = cotangent.reshape(flat)
    w9 = spatial_kernel
    w3 = spatial_kernel.reshape(3, 768, 256)
    gflop = 2 * 2048 * 256 * 256

    small = out((8, 8, 128), F32)
    edge = out((2, columns, 256), BF16)
    st, x_top, x_bot = call(stats_kernel, [small, edge, edge], [in_hbm(x)], 1 << 21)
    st = in_hbm(lax.all_to_all(st, HEIGHT, 0, 0, tiled=True))
    later = moved(cot, TM, -1)
    up = in_hbm(moved(x_bot, HEIGHT, 1))
    dn = in_hbm(moved(x_top, HEIGHT, -1))
    act, hid, slope = call(
        lambda *refs: forward_kernel(members, *refs),
        [out((2, 1280, 768), BF16), out(flat, BF16), out(flat, F32)],
        [info, in_hbm(x), up, dn, st, in_hbm(w3)],
        9 * gflop,
        smem=1,
        loose=(2, 3, 4, 5),
        scratch=[
            pltpu.VMEM(edge.shape, BF16),
            pltpu.VMEM(edge.shape, BF16),
            pltpu.VMEM(small.shape, F32),
            pltpu.VMEM(w3.shape, BF16),
            pltpu.SemaphoreType.DMA((4,)),
        ],
    )
    pg, top, bot = call(
        pregrad_kernel, [out(flat, BF16), edge, edge], [cot, later, slope, temporal_kernel], 3 * gflop
    )
    (g,) = call(
        grads_kernel, [out((6144, 128), F32)], [info, act, pg, hid, cot, later], 12 * gflop, smem=1
    )
    send, top, bot = tied((g[3072:], top, bot))
    got = swapped(send, "core")
    gup = moved(bot, HEIGHT, 1)
    gdn = moved(top, HEIGHT, -1)
    quarter = out((768, 128), BF16)
    own, *sent = call(
        pair_kernel, [out((768, 128), F32), quarter, quarter, quarter], [g, got], 1 << 21
    )
    got = shifts(sent, TM)
    ng, gst = call(
        lambda *refs: backward_kernel(members, *refs),
        [out(flat, F32), out((1, 8, 128), F32)],
        [pg, gup, gdn, in_hbm(w9), in_hbm(x), st],
        9 * gflop,
        loose=(3, 4, 5),
        outside=(0,),
        scratch=[
            pltpu.VMEM((2, 1280, 768), BF16),
            pltpu.VMEM((3, 256, 768), BF16),
            pltpu.VMEM(flat, BF16),
            pltpu.VMEM(small.shape, F32),
            pltpu.VMEM(flat, F32),
            pltpu.SemaphoreType.DMA((12,)),
        ],
    )
    got, gst = tied((got, gst))
    part = out((192, 128), F32)
    own, *sent = call(x_kernel, [part] * 4, [own, *got], 1 << 21)
    own, sent, hid_sent = tied((own, sent, hid))
    prev = moved(hid_sent, TM, 1)
    got = shifts(sent, "y")
    got = tied(got)
    (pieces,) = call(y_kernel, [out((8, 224, 128), BF16)], [own, *got, gst], 1 << 20)
    pieces = lax.all_to_all(pieces, HEIGHT, 0, 0, tiled=True)
    mine, gst = call(z_kernel, [out((192, 128), BF16), out((1, 8, 128), F32)], [pieces], 1 << 20)
    (input_grad,) = call(
        lambda *refs: input_grad_kernel(members, *refs),
        [out(flat, BF16)],
        [x, cot, in_hbm(ng), in_hbm(st), gst],
        1 << 21,
    )
    mine = gathered(mine, "y")
    mine, prev, input_grad = tied((mine, prev, input_grad))
    (block_output,) = call(block_kernel, [out(flat, BF16)], [x, hid, prev, temporal_kernel], 3 * gflop)
    mine = gathered(mine, TM)
    mine, block_output = tied((mine, block_output))
    slab = (3072, 128)
    tile = out((8, 128), F32)
    own, acc = call(half_kernel, [out(slab, F32), tile], [info, mine], 1 << 21, smem=1)
    clipped_spatial, clipped_temporal = call(
        lambda *refs: clip_kernel(clip_level, *refs),
        [out((9, 256, 256), F32), out((3, 256, 256), F32)],
        [info, own, acc, swapped(mine, "core")],
        1 << 21,
        smem=1,
        outside=(0, 1),
        scratch=[
            pltpu.VMEM((12, 256, 256), F32),
            pltpu.VMEM(slab, F32),
            pltpu.VMEM(tile.shape, F32),
            pltpu.SemaphoreType.DMA((12,)),
        ],
    )
    return (
        block_output.reshape(video_latents.shape),
        input_grad.reshape(video_latents.shape),
        clipped_spatial.reshape(spatial_kernel.shape),
        clipped_temporal,
    )


def solution(mesh):
    sizes = (mesh.shape["dp"] // 2, 2, mesh.shape[TM], mesh.shape[HEIGHT])
    torus = Mesh(mesh.devices.reshape(sizes), (*DP, TM, HEIGHT))
    field = P(DP, TM, HEIGHT, None, None)
    return jax.shard_map(
        body, mesh=torus, in_specs=(field, field, P(), P()), out_specs=(field, field, P(), P()), check_vma=False
    )
```

```python
import math

import jax
import jax.numpy as jnp
from jax import lax
from jax.experimental import pallas as pl
from jax.experimental.pallas import tpu as pltpu
from jax.sharding import Mesh
from jax.sharding import PartitionSpec as P


GROUPS = 32
tied = lax.optimization_barrier
EPSILON = 1e-05
CLIP_DIVISOR = 20.0
F32 = jnp.float32
BF16 = jnp.bfloat16
DP = ("y", "core")
TM = "tm"
HEIGHT = "height"
UNIT = 2.0**40
VMEM = pl.BlockSpec(memory_space=pltpu.VMEM)
SMEM = pl.BlockSpec(memory_space=pltpu.SMEM)
ANY = pl.BlockSpec(memory_space=pl.ANY)
HBM = pl.BlockSpec(memory_space=pltpu.HBM)
NT = (((1,), (1,)), ((), ()))
TN = (((0,), (0,)), ((), ()))


def call(kernel, outs, args, flops, scratch=(), smem=0, limit=16, loose=(), outside=()):
    nbytes = sum(a.size * a.dtype.itemsize for a in (*args, *outs))
    specs = [SMEM] * smem + [ANY if i in loose else VMEM for i in range(smem, len(args))]
    return pl.pallas_call(
        kernel,
        out_shape=tuple(pltpu.HBM(o.shape, o.dtype) if i in outside else o for i, o in enumerate(outs)),
        in_specs=specs,
        out_specs=tuple(HBM if i in outside else VMEM for i in range(len(outs))),
        scratch_shapes=list(scratch),
        compiler_params=pltpu.CompilerParams(vmem_limit_bytes=limit << 20),
        cost_estimate=pl.CostEstimate(flops=flops, bytes_accessed=nbytes, transcendentals=0),
    )(*args)


def out(shape, dtype):
    return jax.ShapeDtypeStruct(shape, dtype)


def dot(a, b, dims=None):
    if dims is None:
        return jnp.dot(a, b, preferred_element_type=F32)
    return lax.dot_general(a, b, dims, preferred_element_type=F32)


def sigmoid(v):
    return 0.5 + 0.5 * jnp.tanh(0.5 * v)


def store_stats(o_ref, sums):
    rows = []
    for first, second in sums:
        for v in (first, second):
            t = jnp.sum(v, axis=0, keepdims=True)
            rows += [t[:, :128], t[:, 128:]]
    packed = jnp.concatenate(rows, axis=0)
    for peer in range(o_ref.shape[0]):
        o_ref[peer] = packed


def group_totals(st_ref):
    tot = st_ref[0]
    for peer in range(1, st_ref.shape[0]):
        tot = tot + st_ref[peer]
    lane = lax.broadcasted_iota(jnp.int32, tot.shape, 1)
    for d in (1, 2, 4):
        low = (lane & d) == 0
        tot = tot + jnp.where(low, pltpu.roll(tot, 128 - d, 1), pltpu.roll(tot, d, 1))
    res = []
    for f in range(tot.shape[0] // 4):
        r = [tot[4 * f + k : 4 * f + k + 1] for k in range(4)]
        res.append((jnp.concatenate(r[:2], axis=1), jnp.concatenate(r[2:], axis=1)))
    return res


def moments(st_ref, members):
    res = []
    for first, second in group_totals(st_ref):
        mean = first / members
        res.append((mean, lax.rsqrt(second / members - mean * mean + EPSILON)))
    return res


CHUNK = 256


def woven(put, conv, ready):
    chunks = 1024 // CHUNK
    for line in range(10):
        put(0, line)
    ready()
    done = 0
    for c in range(chunks):
        conv(0, c * CHUNK)
        upto = 10 * (c + 1) // chunks
        for line in range(done, upto):
            put(1, line)
        done = upto
    for c in range(chunks):
        conv(1, c * CHUNK)


def fetched(*pairs, sems):
    copies = [pltpu.make_async_copy(a, b, sems.at[i]) for i, (a, b) in enumerate(pairs)]
    for c in copies:
        c.start()
    for c in copies:
        c.wait()


def fold(v):
    return jnp.sum(v.reshape(v.shape[0] // 8, 8, v.shape[1]), axis=0)


def stats_kernel(x_ref, o_ref, top_ref, bot_ref):
    sums = []
    for f in range(2):
        top_ref[f] = x_ref[f, 0:128, :]
        bot_ref[f] = x_ref[f, 896:1024, :]

        def step(r, carry):
            v = x_ref[f, pl.ds(pl.multiple_of(r * 128, 128), 128), :].astype(F32)
            return carry[0] + fold(v), carry[1] + fold(v * v)

        zero = jnp.zeros((8, 256), F32)
        sums.append(lax.fori_loop(0, 8, step, (zero, zero)))
    store_stats(o_ref, sums)


def shifted(v):
    row = lax.broadcasted_iota(jnp.int32, v.shape, 0)
    before = jnp.where(row == 0, 0.0, pltpu.roll(v, 1, 0))
    after = jnp.where(row == v.shape[0] - 1, 0.0, pltpu.roll(v, v.shape[0] - 1, 0))
    return before, after


def forward_kernel(
    members, info, x_ref, up_hbm, dn_hbm, st_hbm, w_hbm, act_ref, hid_ref, slope_ref,
    up_ref, dn_ref, st_ref, w_ref, sems,
):
    weights = pltpu.make_async_copy(w_hbm, w_ref, sems.at[3])
    weights.start()
    fetched((st_hbm, st_ref), (up_hbm, up_ref), (dn_hbm, dn_ref), sems=sems)
    keep_up = (info[1] > 0).astype(F32)
    keep_dn = (info[2] > 0).astype(F32)
    stats = moments(st_ref, members)

    def put(f, line):
        mean, inv = stats[f]
        v = up_ref[f] if line == 0 else dn_ref[f] if line == 9 else x_ref[f, line * 128 - 128 : line * 128, :]
        n = (v.astype(F32) - mean) * inv
        a = n * sigmoid(n)
        if line == 0:
            a = a * keep_up
        if line == 9:
            a = a * keep_dn
        before, after = shifted(a)
        rows = slice(line * 128, line * 128 + 128)
        act_ref[f, rows, 0:256] = before.astype(BF16)
        act_ref[f, rows, 256:512] = a.astype(BF16)
        act_ref[f, rows, 512:768] = after.astype(BF16)

    def conv(f, at):
        v = None
        for i in range(3):
            part = dot(act_ref[f, at + i * 128 : at + i * 128 + CHUNK, :], w_ref[i])
            v = part if v is None else v + part
        s = sigmoid(v)
        hid_ref[f, at : at + CHUNK, :] = (v * s).astype(BF16)
        slope_ref[f, at : at + CHUNK, :] = s * (1.0 + v * (1.0 - s))

    woven(put, conv, weights.wait)


def pregrad_kernel(cot_ref, later_ref, slope_ref, w_ref, pg_ref, top_ref, bot_ref):
    for f in range(2):

        def part(r, _):
            at = pl.ds(pl.multiple_of(r * 512, 512), 512)
            v = None
            for k in range(3):
                g = f + 2 - k
                lhs = cot_ref[g, at, :] if g < 2 else later_ref[g - 2, at, :]
                p = dot(lhs, w_ref[k], NT)
                v = p if v is None else v + p
            pg_ref[f, at, :] = (v * slope_ref[f, at, :]).astype(BF16)
            return 0

        lax.fori_loop(0, 2, part, 0)
        top_ref[f] = pg_ref[f, 0:128, :]
        bot_ref[f] = pg_ref[f, 896:1024, :]


def slab_rows(x, y, unit, part):
    piece = (unit % 3) * 4 + part
    x, y = (unit // 3 - x) & 3, (piece // 3 - y) & 3
    return pl.multiple_of(x * 768 + y * 192 + (piece % 3) * 64, 64)


def row_of(unit, part):
    piece = (unit % 3) * 4 + part
    return unit // 3 * 768 + piece // 3 * 192 + piece % 3 * 64


def grads_kernel(info, act_ref, pg_ref, hid_ref, cot_ref, later_ref, g_ref):
    def put(tap, v):
        base = ((tap // 6) ^ info[0]) * 3072
        for lh in range(2):
            for part in range(4):
                at = pl.multiple_of(base + row_of((tap % 6) * 2 + lh, part), 64)
                g_ref[pl.ds(at, 64), :] = v[part * 64 : part * 64 + 64, lh * 128 : lh * 128 + 128]

    for i in range(3):
        for j in range(3):
            v = None
            for f in range(2):
                lhs = act_ref[f, i * 128 : i * 128 + 1024, j * 256 : j * 256 + 256]
                p = dot(lhs, pg_ref[f], TN)
                v = p if v is None else v + p
            put(3 * i + j, v)
    for k in range(3):
        v = None
        for f in range(2):
            g = f + 2 - k
            rhs = cot_ref[g] if g < 2 else later_ref[g - 2]
            p = dot(hid_ref[f], rhs, TN)
            v = p if v is None else v + p
        put(9 + k, v)


def backward_kernel(
    members, pg_ref, up_ref, dn_ref, w_hbm, x_hbm, st_hbm, ng_hbm, o_ref,
    g_ref, w_ref, x_ref, st_ref, ng_ref, sems,
):
    loads = [(x_hbm, x_ref), (st_hbm, st_ref)]
    for i in range(3):
        for j in range(3):
            loads.append((w_hbm.at[i, j], w_ref.at[i, :, j * 256 : j * 256 + 256]))
    loads = [pltpu.make_async_copy(a, b, sems.at[i]) for i, (a, b) in enumerate(loads)]
    for c in loads:
        c.start()
    state = []
    sums = [[jnp.zeros((8, 256), F32)] * 2 for _ in range(2)]

    def ready():
        for c in loads:
            c.wait()
        state.extend(moments(st_ref, members))

    def put(f, line):
        v = up_ref[f] if line == 0 else dn_ref[f] if line == 9 else pg_ref[f, line * 128 - 128 : line * 128, :]
        before, after = shifted(v.astype(F32))
        rows = slice(line * 128, line * 128 + 128)
        g_ref[f, rows, 0:256] = after.astype(BF16)
        g_ref[f, rows, 256:512] = v
        g_ref[f, rows, 512:768] = before.astype(BF16)

    def conv(f, at):
        mean, inv = state[f]
        v = None
        for i in range(3):
            start = at + (2 - i) * 128
            p = dot(g_ref[f, start : start + CHUNK, :], w_ref[i], NT)
            v = p if v is None else v + p
        n = (x_ref[f, at : at + CHUNK, :].astype(F32) - mean) * inv
        s = sigmoid(n)
        ng = v * (s * (1.0 + n * (1.0 - s)))
        ng_ref[f, at : at + CHUNK, :] = ng
        sums[f] = [sums[f][0] + fold(ng), sums[f][1] + fold(ng * n)]

    woven(put, conv, ready)
    store_stats(o_ref, sums)
    store = pltpu.make_async_copy(ng_ref, ng_hbm, sems.at[11])
    store.start()
    store.wait()


def input_grad_kernel(members, x_ref, cot_ref, ng_ref, st_ref, gst_ref, o_ref):
    stats = moments(st_ref, members)
    gstats = group_totals(gst_ref)
    for f in range(2):
        mean, inv = stats[f]
        first, second = gstats[f][0] / members, gstats[f][1] / members

        def part(r, _):
            at = pl.ds(pl.multiple_of(r * 128, 128), 128)
            n = (x_ref[f, at, :].astype(F32) - mean) * inv
            term = inv * (ng_ref[f, at, :] - first - n * second)
            o_ref[f, at, :] = (cot_ref[f, at, :].astype(F32) + term).astype(BF16)
            return 0

        lax.fori_loop(0, 8, part, 0)


def block_kernel(x_ref, hid_ref, prev_ref, w_ref, o_ref):
    for f in range(2):

        def part(r, _):
            at = pl.ds(pl.multiple_of(r * 512, 512), 512)
            v = None
            for k in range(3):
                g = f - 2 + k
                lhs = hid_ref[g, at, :] if g >= 0 else prev_ref[g + 2, at, :]
                p = dot(lhs, w_ref[k])
                v = p if v is None else v + p
            o_ref[f, at, :] = (x_ref[f, at, :].astype(F32) + v).astype(BF16)
            return 0

        lax.fori_loop(0, 2, part, 0)


def coded(v):
    t = v * UNIT
    return (t * jnp.sqrt(jnp.abs(t))).astype(BF16)


def decoded(u):
    u = u.astype(F32)
    size = jnp.abs(u)
    root = jnp.exp(jnp.log(jnp.maximum(size, 1e-37)) * (2.0 / 3.0)) * (1.0 / UNIT)
    return jnp.where(size < 1e-37, 0.0, jnp.where(u < 0, -root, root))


def pair_kernel(g_ref, got_ref, o_hbm, o_ref, sems):
    copies = []
    for k in range(4):

        def part(r, _):
            rows = pl.ds(pl.multiple_of(r * 128 + k * 768, 128), 128)
            o_ref[rows, :] = coded(g_ref[rows, :] + got_ref[rows, :])
            return 0

        lax.fori_loop(0, 6, part, 0)
        rows = pl.ds(k * 768, 768)
        copies.append(pltpu.make_async_copy(o_ref.at[rows, :], o_hbm.at[rows, :], sems.at[k]))
        copies[-1].start()
    for c in copies:
        c.wait()


def xy_kernel(u_ref, gst_ref, o_ref):
    def part(r, _):
        rows = pl.ds(pl.multiple_of(r * 64, 64), 64)
        total = decoded(u_ref[0, rows, :])
        for peer in range(1, 16):
            total = total + decoded(u_ref[peer, rows, :])
        code = coded(total)
        for peer in range(8):
            o_ref[peer, rows, :] = code
        return 0

    lax.fori_loop(0, 3, part, 0)
    rest, pieces = gst_ref[0], []
    for _ in range(3):
        piece = rest.astype(BF16).astype(F32)
        pieces.append(piece)
        rest = rest - piece
    sums = jnp.concatenate([*pieces, jnp.zeros_like(rest)], axis=0).astype(BF16)
    for peer in range(8):
        o_ref[peer, 192:224, :] = sums


def z_kernel(u_ref, o_ref, gst_ref):
    def part(r, _):
        rows = pl.ds(pl.multiple_of(r * 64, 64), 64)
        total = decoded(u_ref[0, rows, :])
        for peer in range(1, 8):
            total = total + decoded(u_ref[peer, rows, :])
        o_ref[rows, :] = coded(total)
        return 0

    lax.fori_loop(0, 3, part, 0)
    sums = jnp.zeros((8, 128), F32)
    for peer in range(8):
        v = u_ref[peer, 192:224, :].astype(F32)
        sums = sums + ((v[0:8] + v[8:16]) + v[16:24])
    gst_ref[0] = sums


def half_kernel(info, u_ref, w_ref, acc_ref):
    acc = jnp.zeros((8, 128), F32)
    for unit in range(12):
        for part in range(4):
            v = decoded(u_ref[pl.ds(slab_rows(info[3], info[4], unit, part), 64), :])
            w_ref[unit * 256 + part * 64 : unit * 256 + part * 64 + 64, :] = v
            acc = acc + fold(v * v)
    acc_ref[...] = acc


def clip_kernel(clip_level, info, own_ref, acc_ref, other_ref, s_ref, t_ref, w_ref, b_ref, oacc_ref, sems):
    half_kernel(info, other_ref, b_ref, oacc_ref)
    acc = acc_ref[...] + oacc_ref[...]
    total = jnp.sum(jnp.sum(acc, axis=0, keepdims=True), axis=1, keepdims=True)
    scale = clip_level / jnp.maximum(jnp.sqrt(total), clip_level)
    copies = []
    for tap in range(12):
        mine = info[0] == tap // 6
        for lh in range(2):
            at = pl.ds(((tap % 6) * 2 + lh) * 256, 256)
            v = jnp.where(mine, own_ref[at, :], b_ref[at, :])
            w_ref[tap, :, lh * 128 : lh * 128 + 128] = v * scale
        target = s_ref.at[tap] if tap < 9 else t_ref.at[tap - 9]
        copies.append(pltpu.make_async_copy(w_ref.at[tap], target, sems.at[tap]))
        copies[-1].start()
    for c in copies:
        c.wait()


def in_hbm(x):
    return pltpu.with_memory_space_constraint(x, pltpu.HBM)


def swapped(x, axis):
    return lax.ppermute(x, axis, [(0, 1), (1, 0)])


def moved(x, axes, distance):
    n = lax.axis_size(axes)
    route = [(i, i + distance) for i in range(n) if 0 <= i + distance < n]
    return lax.ppermute(x, axes, route)


def shifts(sent, axis):
    n = lax.axis_size(axis)
    return [
        lax.ppermute(m, axis, [(i, (i + d) % n) for i in range(n)]) for d, m in enumerate(sent, 1)
    ]


def gathered(mine, axis):
    got = tied(shifts([mine] * 3, axis))
    return jnp.concatenate([mine, got[2], got[1], got[0]], axis=0)


def body(video_latents, cotangent, spatial_kernel, temporal_kernel):
    batch, frames, rows, columns, channels = video_latents.shape
    peers = lax.axis_size(HEIGHT)
    members = float(rows * peers * columns * (channels // GROUPS))
    clip_level = (
        channels * rows * peers * columns
        * math.sqrt(batch * lax.axis_size(DP) * frames * lax.axis_size(TM))
        / CLIP_DIVISOR
    )
    z = lax.axis_index(HEIGHT)
    info = jnp.stack(
        [lax.axis_index("core"), z, peers - 1 - z, lax.axis_index(TM), lax.axis_index("y")]
    ).astype(jnp.int32)
    pixels = rows * columns
    flat = (2, pixels, 256)
    x = video_latents.reshape(flat)
    cot = cotangent.reshape(flat)
    w9 = spatial_kernel
    w3 = spatial_kernel.reshape(3, 768, 256)
    gflop = 2 * 2048 * 256 * 256

    small = out((8, 8, 128), F32)
    edge = out((2, columns, 256), BF16)
    st, x_top, x_bot = call(stats_kernel, [small, edge, edge], [in_hbm(x)], 1 << 21)
    st = in_hbm(lax.all_to_all(st, HEIGHT, 0, 0, tiled=True))
    later = moved(cot, TM, -1)
    up = in_hbm(moved(x_bot, HEIGHT, 1))
    dn = in_hbm(moved(x_top, HEIGHT, -1))
    act, hid, slope = call(
        lambda *refs: forward_kernel(members, *refs),
        [out((2, 1280, 768), BF16), out(flat, BF16), out(flat, F32)],
        [info, in_hbm(x), up, dn, st, in_hbm(w3)],
        9 * gflop,
        smem=1,
        loose=(2, 3, 4, 5),
        scratch=[
            pltpu.VMEM(edge.shape, BF16),
            pltpu.VMEM(edge.shape, BF16),
            pltpu.VMEM(small.shape, F32),
            pltpu.VMEM(w3.shape, BF16),
            pltpu.SemaphoreType.DMA((4,)),
        ],
    )
    pg, top, bot = call(
        pregrad_kernel, [out(flat, BF16), edge, edge], [cot, later, slope, temporal_kernel], 3 * gflop
    )
    (g,) = call(
        grads_kernel, [out((6144, 128), F32)], [info, act, pg, hid, cot, later], 12 * gflop, smem=1
    )
    send, top, bot = tied((g[3072:], top, bot))
    got = swapped(send, "core")
    gup = moved(bot, HEIGHT, 1)
    gdn = moved(top, HEIGHT, -1)
    slab = (3072, 128)
    (code,) = call(
        pair_kernel,
        [out(slab, BF16)],
        [g, got],
        1 << 21,
        outside=(0,),
        scratch=[pltpu.VMEM(slab, BF16), pltpu.SemaphoreType.DMA((4,))],
    )
    code, pg_late = tied((code, pg))
    code = lax.all_to_all(code.reshape(16, 192, 128), (TM, "y"), 0, 0, tiled=True)
    ng, gst = call(
        lambda *refs: backward_kernel(members, *refs),
        [out(flat, F32), out((1, 8, 128), F32)],
        [pg_late, gup, gdn, in_hbm(w9), in_hbm(x), st],
        9 * gflop,
        loose=(3, 4, 5),
        outside=(0,),
        scratch=[
            pltpu.VMEM((2, 1280, 768), BF16),
            pltpu.VMEM((3, 256, 768), BF16),
            pltpu.VMEM(flat, BF16),
            pltpu.VMEM(small.shape, F32),
            pltpu.VMEM(flat, F32),
            pltpu.SemaphoreType.DMA((12,)),
        ],
    )
    gst, hid_sent = tied((gst, hid))
    prev = moved(hid_sent, TM, 1)
    code, gst = tied((code, gst))
    (pieces,) = call(xy_kernel, [out((8, 224, 128), BF16)], [code, gst], 1 << 20)
    pieces = lax.all_to_all(pieces, HEIGHT, 0, 0, tiled=True)
    mine, gst = call(z_kernel, [out((192, 128), BF16), out((1, 8, 128), F32)], [pieces], 1 << 20)
    (input_grad,) = call(
        lambda *refs: input_grad_kernel(members, *refs),
        [out(flat, BF16)],
        [x, cot, in_hbm(ng), in_hbm(st), gst],
        1 << 21,
    )
    mine = gathered(mine, "y")
    mine, prev, input_grad = tied((mine, prev, input_grad))
    (block_output,) = call(block_kernel, [out(flat, BF16)], [x, hid, prev, temporal_kernel], 3 * gflop)
    mine = gathered(mine, TM)
    mine, block_output = tied((mine, block_output))
    tile = out((8, 128), F32)
    own, acc = call(half_kernel, [out(slab, F32), tile], [info, mine], 1 << 21, smem=1)
    clipped_spatial, clipped_temporal = call(
        lambda *refs: clip_kernel(clip_level, *refs),
        [out((9, 256, 256), F32), out((3, 256, 256), F32)],
        [info, own, acc, swapped(mine, "core")],
        1 << 21,
        smem=1,
        outside=(0, 1),
        scratch=[
            pltpu.VMEM((12, 256, 256), F32),
            pltpu.VMEM(slab, F32),
            pltpu.VMEM(tile.shape, F32),
            pltpu.SemaphoreType.DMA((12,)),
        ],
    )
    return (
        block_output.reshape(video_latents.shape),
        input_grad.reshape(video_latents.shape),
        clipped_spatial.reshape(spatial_kernel.shape),
        clipped_temporal,
    )


def solution(mesh):
    sizes = (mesh.shape["dp"] // 2, 2, mesh.shape[TM], mesh.shape[HEIGHT])
    torus = Mesh(mesh.devices.reshape(sizes), (*DP, TM, HEIGHT))
    field = P(DP, TM, HEIGHT, None, None)
    return jax.shard_map(
        body, mesh=torus, in_specs=(field, field, P(), P()), out_specs=(field, field, P(), P()), check_vma=False
    )
```

```python
import math

import jax
import jax.numpy as jnp
from jax import lax
from jax.experimental import pallas as pl
from jax.experimental.pallas import tpu as pltpu
from jax.sharding import Mesh
from jax.sharding import PartitionSpec as P


GROUPS = 32
tied = lax.optimization_barrier
EPSILON = 1e-05
CLIP_DIVISOR = 20.0
F32 = jnp.float32
BF16 = jnp.bfloat16
DP = ("y", "core")
TM = "tm"
HEIGHT = "height"
UNIT = 2.0**40
VMEM = pl.BlockSpec(memory_space=pltpu.VMEM)
SMEM = pl.BlockSpec(memory_space=pltpu.SMEM)
ANY = pl.BlockSpec(memory_space=pl.ANY)
HBM = pl.BlockSpec(memory_space=pltpu.HBM)
NT = (((1,), (1,)), ((), ()))
TN = (((0,), (0,)), ((), ()))


def call(kernel, outs, args, flops, scratch=(), smem=0, limit=16, loose=(), outside=()):
    nbytes = sum(a.size * a.dtype.itemsize for a in (*args, *outs))
    specs = [SMEM] * smem + [ANY if i in loose else VMEM for i in range(smem, len(args))]
    return pl.pallas_call(
        kernel,
        out_shape=tuple(pltpu.HBM(o.shape, o.dtype) if i in outside else o for i, o in enumerate(outs)),
        in_specs=specs,
        out_specs=tuple(HBM if i in outside else VMEM for i in range(len(outs))),
        scratch_shapes=list(scratch),
        compiler_params=pltpu.CompilerParams(vmem_limit_bytes=limit << 20),
        cost_estimate=pl.CostEstimate(flops=flops, bytes_accessed=nbytes, transcendentals=0),
    )(*args)


def out(shape, dtype):
    return jax.ShapeDtypeStruct(shape, dtype)


def dot(a, b, dims=None):
    if dims is None:
        return jnp.dot(a, b, preferred_element_type=F32)
    return lax.dot_general(a, b, dims, preferred_element_type=F32)


def sigmoid(v):
    return 0.5 + 0.5 * jnp.tanh(0.5 * v)


def store_stats(o_ref, sums):
    rows = []
    for first, second in sums:
        for v in (first, second):
            t = jnp.sum(v, axis=0, keepdims=True)
            rows += [t[:, :128], t[:, 128:]]
    packed = jnp.concatenate(rows, axis=0)
    for peer in range(o_ref.shape[0]):
        o_ref[peer] = packed


def group_totals(st_ref):
    tot = st_ref[0]
    for peer in range(1, st_ref.shape[0]):
        tot = tot + st_ref[peer]
    lane = lax.broadcasted_iota(jnp.int32, tot.shape, 1)
    for d in (1, 2, 4):
        low = (lane & d) == 0
        tot = tot + jnp.where(low, pltpu.roll(tot, 128 - d, 1), pltpu.roll(tot, d, 1))
    res = []
    for f in range(tot.shape[0] // 4):
        r = [tot[4 * f + k : 4 * f + k + 1] for k in range(4)]
        res.append((jnp.concatenate(r[:2], axis=1), jnp.concatenate(r[2:], axis=1)))
    return res


def moments(st_ref, members):
    res = []
    for first, second in group_totals(st_ref):
        mean = first / members
        res.append((mean, lax.rsqrt(second / members - mean * mean + EPSILON)))
    return res


CHUNK = 256


def woven(put, conv, ready):
    chunks = 1024 // CHUNK
    for line in range(10):
        put(0, line)
    ready()
    done = 0
    for c in range(chunks):
        conv(0, c * CHUNK)
        upto = 10 * (c + 1) // chunks
        for line in range(done, upto):
            put(1, line)
        done = upto
    for c in range(chunks):
        conv(1, c * CHUNK)


def fetched(*pairs, sems):
    copies = [pltpu.make_async_copy(a, b, sems.at[i]) for i, (a, b) in enumerate(pairs)]
    for c in copies:
        c.start()
    for c in copies:
        c.wait()


def fold(v):
    return jnp.sum(v.reshape(v.shape[0] // 8, 8, v.shape[1]), axis=0)


def stats_kernel(x_ref, o_ref, top_ref, bot_ref):
    sums = []
    for f in range(2):
        top_ref[f] = x_ref[f, 0:128, :]
        bot_ref[f] = x_ref[f, 896:1024, :]

        def step(r, carry):
            v = x_ref[f, pl.ds(pl.multiple_of(r * 128, 128), 128), :].astype(F32)
            return carry[0] + fold(v), carry[1] + fold(v * v)

        zero = jnp.zeros((8, 256), F32)
        sums.append(lax.fori_loop(0, 8, step, (zero, zero)))
    store_stats(o_ref, sums)


def shifted(v):
    row = lax.broadcasted_iota(jnp.int32, v.shape, 0)
    before = jnp.where(row == 0, 0.0, pltpu.roll(v, 1, 0))
    after = jnp.where(row == v.shape[0] - 1, 0.0, pltpu.roll(v, v.shape[0] - 1, 0))
    return before, after


def forward_kernel(
    members, info, x_hbm, up_hbm, dn_hbm, st_hbm, w_hbm, act_ref, hid_ref, slope_ref, far_hbm,
    up_ref, dn_ref, st_ref, w_ref, x_ref, sems,
):
    fields = [pltpu.make_async_copy(x_hbm.at[f], x_ref.at[f], sems.at[6 + f]) for f in range(2)]
    fields[0].start()
    weights = pltpu.make_async_copy(w_hbm, w_ref, sems.at[3])
    weights.start()
    fields[1].start()
    fetched((st_hbm, st_ref), (up_hbm, up_ref), (dn_hbm, dn_ref), sems=sems)
    keep_up = (info[1] > 0).astype(F32)
    keep_dn = (info[2] > 0).astype(F32)
    stats = moments(st_ref, members)

    def put(f, line):
        if line == 0:
            fields[f].wait()
        mean, inv = stats[f]
        v = up_ref[f] if line == 0 else dn_ref[f] if line == 9 else x_ref[f, line * 128 - 128 : line * 128, :]
        n = (v.astype(F32) - mean) * inv
        a = n * sigmoid(n)
        if line == 0:
            a = a * keep_up
        if line == 9:
            a = a * keep_dn
        before, after = shifted(a)
        rows = slice(line * 128, line * 128 + 128)
        act_ref[f, rows, 0:256] = before.astype(BF16)
        act_ref[f, rows, 256:512] = a.astype(BF16)
        act_ref[f, rows, 512:768] = after.astype(BF16)

    def conv(f, at):
        v = None
        for i in range(3):
            part = dot(act_ref[f, at + i * 128 : at + i * 128 + CHUNK, :], w_ref[i])
            v = part if v is None else v + part
        s = sigmoid(v)
        hid_ref[f, at : at + CHUNK, :] = (v * s).astype(BF16)
        slope_ref[f, at : at + CHUNK, :] = s * (1.0 + v * (1.0 - s))

        if at + CHUNK == 1024:
            far[f].start()

    far = [pltpu.make_async_copy(hid_ref.at[f], far_hbm.at[f], sems.at[4 + f]) for f in range(2)]
    woven(put, conv, weights.wait)
    for c in far:
        c.wait()


def pregrad_kernel(cot_ref, later_ref, slope_ref, w_ref, pg_ref, top_ref, bot_ref):
    for f in range(2):

        def part(r, _):
            at = pl.ds(pl.multiple_of(r * 512, 512), 512)
            v = None
            for k in range(3):
                g = f + 2 - k
                lhs = cot_ref[g, at, :] if g < 2 else later_ref[g - 2, at, :]
                p = dot(lhs, w_ref[k], NT)
                v = p if v is None else v + p
            pg_ref[f, at, :] = (v * slope_ref[f, at, :]).astype(BF16)
            return 0

        lax.fori_loop(0, 2, part, 0)
        top_ref[f] = pg_ref[f, 0:128, :]
        bot_ref[f] = pg_ref[f, 896:1024, :]


def slab_rows(x, y, unit, part):
    piece = (unit % 3) * 4 + part
    x, y = (unit // 3 - x) & 3, (piece // 3 - y) & 3
    return pl.multiple_of(x * 768 + y * 192 + (piece % 3) * 64, 64)


def row_of(unit, part):
    piece = (unit % 3) * 4 + part
    return unit // 3 * 768 + piece // 3 * 192 + piece % 3 * 64


def grads_kernel(info, act_ref, pg_ref, hid_ref, cot_ref, later_ref, g_ref):
    def put(tap, v):
        base = ((tap // 6) ^ info[0]) * 3072
        for lh in range(2):
            for part in range(4):
                at = pl.multiple_of(base + row_of((tap % 6) * 2 + lh, part), 64)
                g_ref[pl.ds(at, 64), :] = v[part * 64 : part * 64 + 64, lh * 128 : lh * 128 + 128]

    for i in range(3):
        for j in range(3):
            v = None
            for f in range(2):
                lhs = act_ref[f, i * 128 : i * 128 + 1024, j * 256 : j * 256 + 256]
                p = dot(lhs, pg_ref[f], TN)
                v = p if v is None else v + p
            put(3 * i + j, v)
    for k in range(3):
        v = None
        for f in range(2):
            g = f + 2 - k
            rhs = cot_ref[g] if g < 2 else later_ref[g - 2]
            p = dot(hid_ref[f], rhs, TN)
            v = p if v is None else v + p
        put(9 + k, v)


def backward_kernel(
    members, pg_ref, up_ref, dn_ref, w_hbm, x_hbm, st_hbm, ng_hbm, o_ref,
    g_ref, w_ref, x_ref, st_ref, ng_ref, sems,
):
    loads = [(x_hbm, x_ref), (st_hbm, st_ref)]
    for i in range(3):
        for j in range(3):
            loads.append((w_hbm.at[i, j], w_ref.at[i, :, j * 256 : j * 256 + 256]))
    loads = [pltpu.make_async_copy(a, b, sems.at[i]) for i, (a, b) in enumerate(loads)]
    for c in loads:
        c.start()
    state = []
    sums = [[jnp.zeros((8, 256), F32)] * 2 for _ in range(2)]

    def ready():
        for c in loads:
            c.wait()
        state.extend(moments(st_ref, members))

    def put(f, line):
        v = up_ref[f] if line == 0 else dn_ref[f] if line == 9 else pg_ref[f, line * 128 - 128 : line * 128, :]
        before, after = shifted(v.astype(F32))
        rows = slice(line * 128, line * 128 + 128)
        g_ref[f, rows, 0:256] = after.astype(BF16)
        g_ref[f, rows, 256:512] = v
        g_ref[f, rows, 512:768] = before.astype(BF16)

    def conv(f, at):
        mean, inv = state[f]
        v = None
        for i in range(3):
            start = at + (2 - i) * 128
            p = dot(g_ref[f, start : start + CHUNK, :], w_ref[i], NT)
            v = p if v is None else v + p
        n = (x_ref[f, at : at + CHUNK, :].astype(F32) - mean) * inv
        s = sigmoid(n)
        ng = v * (s * (1.0 + n * (1.0 - s)))
        ng_ref[f, at : at + CHUNK, :] = ng
        sums[f] = [sums[f][0] + fold(ng), sums[f][1] + fold(ng * n)]

    woven(put, conv, ready)
    store_stats(o_ref, sums)
    store = pltpu.make_async_copy(ng_ref, ng_hbm, sems.at[11])
    store.start()
    store.wait()


def input_grad_kernel(members, x_ref, cot_ref, ng_ref, st_ref, gst_ref, o_ref):
    stats = moments(st_ref, members)
    gstats = group_totals(gst_ref)
    for f in range(2):
        mean, inv = stats[f]
        first, second = gstats[f][0] / members, gstats[f][1] / members

        def part(r, _):
            at = pl.ds(pl.multiple_of(r * 128, 128), 128)
            n = (x_ref[f, at, :].astype(F32) - mean) * inv
            term = inv * (ng_ref[f, at, :] - first - n * second)
            o_ref[f, at, :] = (cot_ref[f, at, :].astype(F32) + term).astype(BF16)
            return 0

        lax.fori_loop(0, 8, part, 0)


def block_kernel(x_ref, hid_ref, prev_ref, w_ref, o_ref):
    for f in range(2):

        def part(r, _):
            at = pl.ds(pl.multiple_of(r * 512, 512), 512)
            v = None
            for k in range(3):
                g = f - 2 + k
                lhs = hid_ref[g, at, :] if g >= 0 else prev_ref[g + 2, at, :]
                p = dot(lhs, w_ref[k])
                v = p if v is None else v + p
            o_ref[f, at, :] = (x_ref[f, at, :].astype(F32) + v).astype(BF16)
            return 0

        lax.fori_loop(0, 2, part, 0)


def coded(v):
    t = v * UNIT
    return (t * jnp.sqrt(jnp.abs(t))).astype(BF16)


def decoded(u):
    u = u.astype(F32)
    size = jnp.abs(u)
    root = jnp.exp(jnp.log(jnp.maximum(size, 1e-37)) * (2.0 / 3.0)) * (1.0 / UNIT)
    return jnp.where(size < 1e-37, 0.0, jnp.where(u < 0, -root, root))


def pair_kernel(g_ref, got_ref, o_hbm, o_ref, sems):
    copies = []
    for k in range(4):

        def part(r, _):
            rows = pl.ds(pl.multiple_of(r * 128 + k * 768, 128), 128)
            o_ref[rows, :] = coded(g_ref[rows, :] + got_ref[rows, :])
            return 0

        lax.fori_loop(0, 6, part, 0)
        rows = pl.ds(k * 768, 768)
        copies.append(pltpu.make_async_copy(o_ref.at[rows, :], o_hbm.at[rows, :], sems.at[k]))
        copies[-1].start()
    for c in copies:
        c.wait()


def xy_kernel(u_ref, gst_ref, o_ref):
    def part(r, _):
        rows = pl.ds(pl.multiple_of(r * 64, 64), 64)
        total = decoded(u_ref[0, rows, :])
        for peer in range(1, 16):
            total = total + decoded(u_ref[peer, rows, :])
        code = coded(total)
        for peer in range(8):
            o_ref[peer, rows, :] = code
        return 0

    lax.fori_loop(0, 3, part, 0)
    rest, pieces = gst_ref[0], []
    for _ in range(3):
        piece = rest.astype(BF16).astype(F32)
        pieces.append(piece)
        rest = rest - piece
    sums = jnp.concatenate([*pieces, jnp.zeros_like(rest)], axis=0).astype(BF16)
    for peer in range(8):
        o_ref[peer, 192:224, :] = sums


def z_kernel(u_ref, o_ref, gst_ref):
    def part(r, _):
        rows = pl.ds(pl.multiple_of(r * 64, 64), 64)
        total = decoded(u_ref[0, rows, :])
        for peer in range(1, 8):
            total = total + decoded(u_ref[peer, rows, :])
        o_ref[rows, :] = coded(total)
        return 0

    lax.fori_loop(0, 3, part, 0)
    sums = jnp.zeros((8, 128), F32)
    for peer in range(8):
        v = u_ref[peer, 192:224, :].astype(F32)
        sums = sums + ((v[0:8] + v[8:16]) + v[16:24])
    gst_ref[0] = sums


def half_kernel(info, u_ref, w_ref, acc_ref):
    acc = jnp.zeros((8, 128), F32)
    for unit in range(12):
        for part in range(4):
            v = decoded(u_ref[pl.ds(slab_rows(info[3], info[4], unit, part), 64), :])
            w_ref[unit * 256 + part * 64 : unit * 256 + part * 64 + 64, :] = v
            acc = acc + fold(v * v)
    acc_ref[...] = acc


def clip_kernel(clip_level, info, own_ref, acc_ref, other_ref, s_ref, t_ref, w_ref, b_ref, oacc_ref, sems):
    half_kernel(info, other_ref, b_ref, oacc_ref)
    acc = acc_ref[...] + oacc_ref[...]
    total = jnp.sum(jnp.sum(acc, axis=0, keepdims=True), axis=1, keepdims=True)
    scale = clip_level / jnp.maximum(jnp.sqrt(total), clip_level)
    copies = []
    for tap in range(12):
        mine = info[0] == tap // 6
        for lh in range(2):
            at = pl.ds(((tap % 6) * 2 + lh) * 256, 256)
            v = jnp.where(mine, own_ref[at, :], b_ref[at, :])
            w_ref[tap, :, lh * 128 : lh * 128 + 128] = v * scale
        target = s_ref.at[tap] if tap < 9 else t_ref.at[tap - 9]
        copies.append(pltpu.make_async_copy(w_ref.at[tap], target, sems.at[tap]))
        copies[-1].start()
    for c in copies:
        c.wait()


def in_hbm(x):
    return pltpu.with_memory_space_constraint(x, pltpu.HBM)


def swapped(x, axis):
    return lax.ppermute(x, axis, [(0, 1), (1, 0)])


def moved(x, axes, distance):
    n = lax.axis_size(axes)
    route = [(i, i + distance) for i in range(n) if 0 <= i + distance < n]
    return lax.ppermute(x, axes, route)


def shifts(sent, axis):
    n = lax.axis_size(axis)
    return [
        lax.ppermute(m, axis, [(i, (i + d) % n) for i in range(n)]) for d, m in enumerate(sent, 1)
    ]


def gathered(mine, axis):
    got = tied(shifts([mine] * 3, axis))
    return jnp.concatenate([mine, got[2], got[1], got[0]], axis=0)


def body(video_latents, cotangent, spatial_kernel, temporal_kernel):
    batch, frames, rows, columns, channels = video_latents.shape
    peers = lax.axis_size(HEIGHT)
    members = float(rows * peers * columns * (channels // GROUPS))
    clip_level = (
        channels * rows * peers * columns
        * math.sqrt(batch * lax.axis_size(DP) * frames * lax.axis_size(TM))
        / CLIP_DIVISOR
    )
    z = lax.axis_index(HEIGHT)
    info = jnp.stack(
        [lax.axis_index("core"), z, peers - 1 - z, lax.axis_index(TM), lax.axis_index("y")]
    ).astype(jnp.int32)
    pixels = rows * columns
    flat = (2, pixels, 256)
    x = video_latents.reshape(flat)
    cot = cotangent.reshape(flat)
    w9 = spatial_kernel
    w3 = spatial_kernel.reshape(3, 768, 256)
    gflop = 2 * 2048 * 256 * 256

    small = out((8, 8, 128), F32)
    edge = out((2, columns, 256), BF16)
    st, x_top, x_bot = call(stats_kernel, [small, edge, edge], [in_hbm(x)], 1 << 21)
    st = in_hbm(lax.all_to_all(st, HEIGHT, 0, 0, tiled=True))
    later = moved(cot, TM, -1)
    up = in_hbm(moved(x_bot, HEIGHT, 1))
    dn = in_hbm(moved(x_top, HEIGHT, -1))
    act, hid, slope, hid_far = call(
        lambda *refs: forward_kernel(members, *refs),
        [out((2, 1280, 768), BF16), out(flat, BF16), out(flat, F32), out(flat, BF16)],
        [info, in_hbm(x), up, dn, st, in_hbm(w3)],
        9 * gflop,
        smem=1,
        loose=(1, 2, 3, 4, 5),
        outside=(3,),
        scratch=[
            pltpu.VMEM(edge.shape, BF16),
            pltpu.VMEM(edge.shape, BF16),
            pltpu.VMEM(small.shape, F32),
            pltpu.VMEM(w3.shape, BF16),
            pltpu.VMEM(flat, BF16),
            pltpu.SemaphoreType.DMA((8,)),
        ],
    )
    pg, top, bot = call(
        pregrad_kernel, [out(flat, BF16), edge, edge], [cot, later, slope, temporal_kernel], 3 * gflop
    )
    (g,) = call(
        grads_kernel, [out((6144, 128), F32)], [info, act, pg, hid, cot, later], 12 * gflop, smem=1
    )
    send, top, bot = tied((g[3072:], top, bot))
    got = swapped(send, "core")
    gup = moved(bot, HEIGHT, 1)
    gdn = moved(top, HEIGHT, -1)
    slab = (3072, 128)
    (code,) = call(
        pair_kernel,
        [out(slab, BF16)],
        [g, got],
        1 << 21,
        outside=(0,),
        scratch=[pltpu.VMEM(slab, BF16), pltpu.SemaphoreType.DMA((4,))],
    )
    code, pg_late = tied((code, pg))
    code = lax.all_to_all(code.reshape(16, 192, 128), (TM, "y"), 0, 0, tiled=True)
    ng, gst = call(
        lambda *refs: backward_kernel(members, *refs),
        [out(flat, F32), out((1, 8, 128), F32)],
        [pg_late, gup, gdn, in_hbm(w9), in_hbm(x), st],
        9 * gflop,
        loose=(3, 4, 5),
        outside=(0,),
        scratch=[
            pltpu.VMEM((2, 1280, 768), BF16),
            pltpu.VMEM((3, 256, 768), BF16),
            pltpu.VMEM(flat, BF16),
            pltpu.VMEM(small.shape, F32),
            pltpu.VMEM(flat, F32),
            pltpu.SemaphoreType.DMA((12,)),
        ],
    )
    gst, hid_sent = tied((gst, hid_far))
    prev = moved(hid_sent, TM, 1)
    code, gst = tied((code, gst))
    (pieces,) = call(xy_kernel, [out((8, 224, 128), BF16)], [code, gst], 1 << 20)
    pieces = lax.all_to_all(pieces, HEIGHT, 0, 0, tiled=True)
    mine, gst = call(z_kernel, [out((192, 128), BF16), out((1, 8, 128), F32)], [pieces], 1 << 20)
    (input_grad,) = call(
        lambda *refs: input_grad_kernel(members, *refs),
        [out(flat, BF16)],
        [x, cot, in_hbm(ng), in_hbm(st), gst],
        1 << 21,
    )
    mine = gathered(mine, "y")
    mine, prev, input_grad = tied((mine, prev, input_grad))
    (block_output,) = call(block_kernel, [out(flat, BF16)], [x, hid_far, prev, temporal_kernel], 3 * gflop)
    mine = gathered(mine, TM)
    mine, block_output = tied((mine, block_output))
    tile = out((8, 128), F32)
    own, acc = call(half_kernel, [out(slab, F32), tile], [info, mine], 1 << 21, smem=1)
    clipped_spatial, clipped_temporal = call(
        lambda *refs: clip_kernel(clip_level, *refs),
        [out((9, 256, 256), F32), out((3, 256, 256), F32)],
        [info, own, acc, swapped(mine, "core")],
        1 << 21,
        smem=1,
        outside=(0, 1),
        scratch=[
            pltpu.VMEM((12, 256, 256), F32),
            pltpu.VMEM(slab, F32),
            pltpu.VMEM(tile.shape, F32),
            pltpu.SemaphoreType.DMA((12,)),
        ],
    )
    return (
        block_output.reshape(video_latents.shape),
        input_grad.reshape(video_latents.shape),
        clipped_spatial.reshape(spatial_kernel.shape),
        clipped_temporal,
    )


def solution(mesh):
    sizes = (mesh.shape["dp"] // 2, 2, mesh.shape[TM], mesh.shape[HEIGHT])
    torus = Mesh(mesh.devices.reshape(sizes), (*DP, TM, HEIGHT))
    field = P(DP, TM, HEIGHT, None, None)
    return jax.shard_map(
        body, mesh=torus, in_specs=(field, field, P(), P()), out_specs=(field, field, P(), P()), check_vma=False
    )
```

```python
import math

import jax
import jax.numpy as jnp
from jax import lax
from jax.experimental import pallas as pl
from jax.experimental.pallas import tpu as pltpu
from jax.sharding import Mesh
from jax.sharding import PartitionSpec as P


GROUPS = 32
tied = lax.optimization_barrier
EPSILON = 1e-05
CLIP_DIVISOR = 20.0
F32 = jnp.float32
BF16 = jnp.bfloat16
DP = ("y", "core")
TM = "tm"
HEIGHT = "height"
UNIT = 2.0**40
VMEM = pl.BlockSpec(memory_space=pltpu.VMEM)
SMEM = pl.BlockSpec(memory_space=pltpu.SMEM)
ANY = pl.BlockSpec(memory_space=pl.ANY)
HBM = pl.BlockSpec(memory_space=pltpu.HBM)
NT = (((1,), (1,)), ((), ()))
TN = (((0,), (0,)), ((), ()))


def call(kernel, outs, args, flops, scratch=(), smem=0, limit=16, loose=(), outside=()):
    nbytes = sum(a.size * a.dtype.itemsize for a in (*args, *outs))
    specs = [SMEM] * smem + [ANY if i in loose else VMEM for i in range(smem, len(args))]
    return pl.pallas_call(
        kernel,
        out_shape=tuple(pltpu.HBM(o.shape, o.dtype) if i in outside else o for i, o in enumerate(outs)),
        in_specs=specs,
        out_specs=tuple(HBM if i in outside else VMEM for i in range(len(outs))),
        scratch_shapes=list(scratch),
        compiler_params=pltpu.CompilerParams(vmem_limit_bytes=limit << 20),
        cost_estimate=pl.CostEstimate(flops=flops, bytes_accessed=nbytes, transcendentals=0),
    )(*args)


def out(shape, dtype):
    return jax.ShapeDtypeStruct(shape, dtype)


def dot(a, b, dims=None):
    if dims is None:
        return jnp.dot(a, b, preferred_element_type=F32)
    return lax.dot_general(a, b, dims, preferred_element_type=F32)


def sigmoid(v):
    return 0.5 + 0.5 * jnp.tanh(0.5 * v)


def store_stats(o_ref, sums):
    rows = []
    for first, second in sums:
        for v in (first, second):
            t = jnp.sum(v, axis=0, keepdims=True)
            rows += [t[:, :128], t[:, 128:]]
    packed = jnp.concatenate(rows, axis=0)
    for peer in range(o_ref.shape[0]):
        o_ref[peer] = packed


def group_totals(st_ref):
    tot = st_ref[0]
    for peer in range(1, st_ref.shape[0]):
        tot = tot + st_ref[peer]
    lane = lax.broadcasted_iota(jnp.int32, tot.shape, 1)
    for d in (1, 2, 4):
        low = (lane & d) == 0
        tot = tot + jnp.where(low, pltpu.roll(tot, 128 - d, 1), pltpu.roll(tot, d, 1))
    res = []
    for f in range(tot.shape[0] // 4):
        r = [tot[4 * f + k : 4 * f + k + 1] for k in range(4)]
        res.append((jnp.concatenate(r[:2], axis=1), jnp.concatenate(r[2:], axis=1)))
    return res


def moments(st_ref, members):
    res = []
    for first, second in group_totals(st_ref):
        mean = first / members
        res.append((mean, lax.rsqrt(second / members - mean * mean + EPSILON)))
    return res


CHUNK = 512


def woven(put, conv, ready):
    chunks = 1024 // CHUNK
    for line in range(10):
        put(0, line)
    ready()
    done = 0
    for c in range(chunks):
        conv(0, c * CHUNK)
        upto = 10 * (c + 1) // chunks
        for line in range(done, upto):
            put(1, line)
        done = upto
    for c in range(chunks):
        conv(1, c * CHUNK)


def fetched(*pairs, sems):
    copies = [pltpu.make_async_copy(a, b, sems.at[i]) for i, (a, b) in enumerate(pairs)]
    for c in copies:
        c.start()
    for c in copies:
        c.wait()


def fold(v):
    return jnp.sum(v.reshape(v.shape[0] // 8, 8, v.shape[1]), axis=0)


def stats_kernel(x_ref, o_ref, top_ref, bot_ref):
    sums = []
    for f in range(2):
        top_ref[f] = x_ref[f, 0:128, :]
        bot_ref[f] = x_ref[f, 896:1024, :]

        def step(r, carry):
            v = x_ref[f, pl.ds(pl.multiple_of(r * 128, 128), 128), :].astype(F32)
            return carry[0] + fold(v), carry[1] + fold(v * v)

        zero = jnp.zeros((8, 256), F32)
        sums.append(lax.fori_loop(0, 8, step, (zero, zero)))
    store_stats(o_ref, sums)


def shifted(v):
    row = lax.broadcasted_iota(jnp.int32, v.shape, 0)
    before = jnp.where(row == 0, 0.0, pltpu.roll(v, 1, 0))
    after = jnp.where(row == v.shape[0] - 1, 0.0, pltpu.roll(v, v.shape[0] - 1, 0))
    return before, after


def forward_kernel(
    members, info, x_ref, up_hbm, dn_hbm, st_hbm, w_hbm, act_ref, hid_ref, slope_ref, far_hbm,
    up_ref, dn_ref, st_ref, w_ref, sems,
):
    weights = pltpu.make_async_copy(w_hbm, w_ref, sems.at[3])
    weights.start()
    fetched((st_hbm, st_ref), (up_hbm, up_ref), (dn_hbm, dn_ref), sems=sems)
    keep_up = (info[1] > 0).astype(F32)
    keep_dn = (info[2] > 0).astype(F32)
    stats = moments(st_ref, members)

    def put(f, line):
        mean, inv = stats[f]
        v = up_ref[f] if line == 0 else dn_ref[f] if line == 9 else x_ref[f, line * 128 - 128 : line * 128, :]
        n = (v.astype(F32) - mean) * inv
        a = n * sigmoid(n)
        if line == 0:
            a = a * keep_up
        if line == 9:
            a = a * keep_dn
        before, after = shifted(a)
        rows = slice(line * 128, line * 128 + 128)
        act_ref[f, rows, 0:256] = before.astype(BF16)
        act_ref[f, rows, 256:512] = a.astype(BF16)
        act_ref[f, rows, 512:768] = after.astype(BF16)

    def conv(f, at):
        v = None
        for i in range(3):
            part = dot(act_ref[f, at + i * 128 : at + i * 128 + CHUNK, :], w_ref[i])
            v = part if v is None else v + part
        s = sigmoid(v)
        hid_ref[f, at : at + CHUNK, :] = (v * s).astype(BF16)
        slope_ref[f, at : at + CHUNK, :] = s * (1.0 + v * (1.0 - s))

        if at + CHUNK == 1024:
            far[f].start()

    far = [pltpu.make_async_copy(hid_ref.at[f], far_hbm.at[f], sems.at[4 + f]) for f in range(2)]
    woven(put, conv, weights.wait)
    for c in far:
        c.wait()


def pregrad_kernel(cot_ref, later_ref, slope_ref, w_ref, pg_ref, top_ref, bot_ref):
    for f in range(2):

        def part(r, _):
            at = pl.ds(pl.multiple_of(r * 512, 512), 512)
            v = None
            for k in range(3):
                g = f + 2 - k
                lhs = cot_ref[g, at, :] if g < 2 else later_ref[g - 2, at, :]
                p = dot(lhs, w_ref[k], NT)
                v = p if v is None else v + p
            pg_ref[f, at, :] = (v * slope_ref[f, at, :]).astype(BF16)
            return 0

        lax.fori_loop(0, 2, part, 0)
        top_ref[f] = pg_ref[f, 0:128, :]
        bot_ref[f] = pg_ref[f, 896:1024, :]


def slab_rows(x, y, unit, part):
    piece = (unit % 3) * 4 + part
    x, y = (unit // 3 - x) & 3, (piece // 3 - y) & 3
    return pl.multiple_of(x * 768 + y * 192 + (piece % 3) * 64, 64)


def row_of(unit, part):
    piece = (unit % 3) * 4 + part
    return unit // 3 * 768 + piece // 3 * 192 + piece % 3 * 64


def grads_kernel(info, act_ref, pg_ref, hid_ref, cot_ref, later_ref, g_ref):
    def put(tap, v):
        base = ((tap // 6) ^ info[0]) * 3072
        for lh in range(2):
            for part in range(4):
                at = pl.multiple_of(base + row_of((tap % 6) * 2 + lh, part), 64)
                g_ref[pl.ds(at, 64), :] = v[part * 64 : part * 64 + 64, lh * 128 : lh * 128 + 128]

    for i in range(3):
        for j in range(3):
            v = None
            for f in range(2):
                lhs = act_ref[f, i * 128 : i * 128 + 1024, j * 256 : j * 256 + 256]
                p = dot(lhs, pg_ref[f], TN)
                v = p if v is None else v + p
            put(3 * i + j, v)
    for k in range(3):
        v = None
        for f in range(2):
            g = f + 2 - k
            rhs = cot_ref[g] if g < 2 else later_ref[g - 2]
            p = dot(hid_ref[f], rhs, TN)
            v = p if v is None else v + p
        put(9 + k, v)


def backward_kernel(
    members, pg_ref, up_ref, dn_ref, w_hbm, x_hbm, st_hbm, ng_hbm, o_ref,
    g_ref, w_ref, x_ref, st_ref, ng_ref, sems,
):
    loads = [(x_hbm, x_ref), (st_hbm, st_ref)]
    for i in range(3):
        for j in range(3):
            loads.append((w_hbm.at[i, j], w_ref.at[i, :, j * 256 : j * 256 + 256]))
    loads = [pltpu.make_async_copy(a, b, sems.at[i]) for i, (a, b) in enumerate(loads)]
    for c in loads:
        c.start()
    state = []
    sums = [[jnp.zeros((8, 256), F32)] * 2 for _ in range(2)]

    def ready():
        for c in loads:
            c.wait()
        state.extend(moments(st_ref, members))

    def put(f, line):
        v = up_ref[f] if line == 0 else dn_ref[f] if line == 9 else pg_ref[f, line * 128 - 128 : line * 128, :]
        before, after = shifted(v.astype(F32))
        rows = slice(line * 128, line * 128 + 128)
        g_ref[f, rows, 0:256] = after.astype(BF16)
        g_ref[f, rows, 256:512] = v
        g_ref[f, rows, 512:768] = before.astype(BF16)

    def conv(f, at):
        mean, inv = state[f]
        v = None
        for i in range(3):
            start = at + (2 - i) * 128
            p = dot(g_ref[f, start : start + CHUNK, :], w_ref[i], NT)
            v = p if v is None else v + p
        n = (x_ref[f, at : at + CHUNK, :].astype(F32) - mean) * inv
        s = sigmoid(n)
        ng = v * (s * (1.0 + n * (1.0 - s)))
        ng_ref[f, at : at + CHUNK, :] = ng
        sums[f] = [sums[f][0] + fold(ng), sums[f][1] + fold(ng * n)]

    woven(put, conv, ready)
    store_stats(o_ref, sums)
    store = pltpu.make_async_copy(ng_ref, ng_hbm, sems.at[11])
    store.start()
    store.wait()


def input_grad_kernel(members, x_ref, cot_ref, ng_ref, st_ref, gst_ref, o_ref):
    stats = moments(st_ref, members)
    gstats = group_totals(gst_ref)
    for f in range(2):
        mean, inv = stats[f]
        first, second = gstats[f][0] / members, gstats[f][1] / members

        def part(r, _):
            at = pl.ds(pl.multiple_of(r * 128, 128), 128)
            n = (x_ref[f, at, :].astype(F32) - mean) * inv
            term = inv * (ng_ref[f, at, :] - first - n * second)
            o_ref[f, at, :] = (cot_ref[f, at, :].astype(F32) + term).astype(BF16)
            return 0

        lax.fori_loop(0, 8, part, 0)


def block_kernel(x_ref, hid_ref, prev_ref, w_ref, o_ref):
    for f in range(2):

        def part(r, _):
            at = pl.ds(pl.multiple_of(r * 512, 512), 512)
            v = None
            for k in range(3):
                g = f - 2 + k
                lhs = hid_ref[g, at, :] if g >= 0 else prev_ref[g + 2, at, :]
                p = dot(lhs, w_ref[k])
                v = p if v is None else v + p
            o_ref[f, at, :] = (x_ref[f, at, :].astype(F32) + v).astype(BF16)
            return 0

        lax.fori_loop(0, 2, part, 0)


def coded(v):
    t = v * UNIT
    return (t * jnp.sqrt(jnp.abs(t))).astype(BF16)


def decoded(u):
    u = u.astype(F32)
    size = jnp.abs(u)
    root = jnp.exp(jnp.log(jnp.maximum(size, 1e-37)) * (2.0 / 3.0)) * (1.0 / UNIT)
    return jnp.where(size < 1e-37, 0.0, jnp.where(u < 0, -root, root))


def pair_kernel(g_ref, got_ref, o_hbm, o_ref, sems):
    copies = []
    for k in range(4):

        def part(r, _):
            rows = pl.ds(pl.multiple_of(r * 128 + k * 768, 128), 128)
            o_ref[rows, :] = coded(g_ref[rows, :] + got_ref[rows, :])
            return 0

        lax.fori_loop(0, 6, part, 0)
        rows = pl.ds(k * 768, 768)
        copies.append(pltpu.make_async_copy(o_ref.at[rows, :], o_hbm.at[rows, :], sems.at[k]))
        copies[-1].start()
    for c in copies:
        c.wait()


def xy_kernel(u_ref, gst_ref, o_ref):
    def part(r, _):
        rows = pl.ds(pl.multiple_of(r * 64, 64), 64)
        total = decoded(u_ref[0, rows, :])
        for peer in range(1, 16):
            total = total + decoded(u_ref[peer, rows, :])
        code = coded(total)
        for peer in range(8):
            o_ref[peer, rows, :] = code
        return 0

    lax.fori_loop(0, 3, part, 0)
    rest, pieces = gst_ref[0], []
    for _ in range(3):
        piece = rest.astype(BF16).astype(F32)
        pieces.append(piece)
        rest = rest - piece
    sums = jnp.concatenate([*pieces, jnp.zeros_like(rest)], axis=0).astype(BF16)
    for peer in range(8):
        o_ref[peer, 192:224, :] = sums


def z_kernel(u_ref, o_ref, gst_ref):
    def part(r, _):
        rows = pl.ds(pl.multiple_of(r * 64, 64), 64)
        total = decoded(u_ref[0, rows, :])
        for peer in range(1, 8):
            total = total + decoded(u_ref[peer, rows, :])
        o_ref[rows, :] = coded(total)
        return 0

    lax.fori_loop(0, 3, part, 0)
    sums = jnp.zeros((8, 128), F32)
    for peer in range(8):
        v = u_ref[peer, 192:224, :].astype(F32)
        sums = sums + ((v[0:8] + v[8:16]) + v[16:24])
    gst_ref[0] = sums


def half_kernel(info, u_ref, w_ref, acc_ref):
    acc = jnp.zeros((8, 128), F32)
    for unit in range(12):
        for part in range(4):
            v = decoded(u_ref[pl.ds(slab_rows(info[3], info[4], unit, part), 64), :])
            w_ref[unit * 256 + part * 64 : unit * 256 + part * 64 + 64, :] = v
            acc = acc + fold(v * v)
    acc_ref[...] = acc


def clip_kernel(clip_level, info, own_ref, acc_ref, other_ref, s_ref, t_ref, w_ref, b_ref, oacc_ref, sems):
    half_kernel(info, other_ref, b_ref, oacc_ref)
    acc = acc_ref[...] + oacc_ref[...]
    total = jnp.sum(jnp.sum(acc, axis=0, keepdims=True), axis=1, keepdims=True)
    scale = clip_level / jnp.maximum(jnp.sqrt(total), clip_level)
    copies = []
    for tap in range(12):
        mine = info[0] == tap // 6
        for lh in range(2):
            at = pl.ds(((tap % 6) * 2 + lh) * 256, 256)
            v = jnp.where(mine, own_ref[at, :], b_ref[at, :])
            w_ref[tap, :, lh * 128 : lh * 128 + 128] = v * scale
        target = s_ref.at[tap] if tap < 9 else t_ref.at[tap - 9]
        copies.append(pltpu.make_async_copy(w_ref.at[tap], target, sems.at[tap]))
        copies[-1].start()
    for c in copies:
        c.wait()


def in_hbm(x):
    return pltpu.with_memory_space_constraint(x, pltpu.HBM)


def swapped(x, axis):
    return lax.ppermute(x, axis, [(0, 1), (1, 0)])


def moved(x, axes, distance):
    n = lax.axis_size(axes)
    route = [(i, i + distance) for i in range(n) if 0 <= i + distance < n]
    return lax.ppermute(x, axes, route)


def shifts(sent, axis):
    n = lax.axis_size(axis)
    return [
        lax.ppermute(m, axis, [(i, (i + d) % n) for i in range(n)]) for d, m in enumerate(sent, 1)
    ]


def gathered(mine, axis):
    got = tied(shifts([mine] * 3, axis))
    return jnp.concatenate([mine, got[2], got[1], got[0]], axis=0)


def body(video_latents, cotangent, spatial_kernel, temporal_kernel):
    batch, frames, rows, columns, channels = video_latents.shape
    peers = lax.axis_size(HEIGHT)
    members = float(rows * peers * columns * (channels // GROUPS))
    clip_level = (
        channels * rows * peers * columns
        * math.sqrt(batch * lax.axis_size(DP) * frames * lax.axis_size(TM))
        / CLIP_DIVISOR
    )
    z = lax.axis_index(HEIGHT)
    info = jnp.stack(
        [lax.axis_index("core"), z, peers - 1 - z, lax.axis_index(TM), lax.axis_index("y")]
    ).astype(jnp.int32)
    pixels = rows * columns
    flat = (2, pixels, 256)
    x = video_latents.reshape(flat)
    cot = cotangent.reshape(flat)
    w9 = spatial_kernel
    w3 = spatial_kernel.reshape(3, 768, 256)
    gflop = 2 * 2048 * 256 * 256

    small = out((8, 8, 128), F32)
    edge = out((2, columns, 256), BF16)
    st, x_top, x_bot = call(stats_kernel, [small, edge, edge], [in_hbm(x)], 1 << 21)
    st = in_hbm(lax.all_to_all(st, HEIGHT, 0, 0, tiled=True))
    later = moved(cot, TM, -1)
    up = in_hbm(moved(x_bot, HEIGHT, 1))
    dn = in_hbm(moved(x_top, HEIGHT, -1))
    act, hid, slope, hid_far = call(
        lambda *refs: forward_kernel(members, *refs),
        [out((2, 1280, 768), BF16), out(flat, BF16), out(flat, F32), out(flat, BF16)],
        [info, in_hbm(x), up, dn, st, in_hbm(w3)],
        9 * gflop,
        smem=1,
        loose=(2, 3, 4, 5),
        outside=(3,),
        scratch=[
            pltpu.VMEM(edge.shape, BF16),
            pltpu.VMEM(edge.shape, BF16),
            pltpu.VMEM(small.shape, F32),
            pltpu.VMEM(w3.shape, BF16),
            pltpu.SemaphoreType.DMA((6,)),
        ],
    )
    pg, top, bot = call(
        pregrad_kernel, [out(flat, BF16), edge, edge], [cot, later, slope, temporal_kernel], 3 * gflop
    )
    (g,) = call(
        grads_kernel, [out((6144, 128), F32)], [info, act, pg, hid, cot, later], 12 * gflop, smem=1
    )
    send, top, bot = tied((g[3072:], top, bot))
    got = swapped(send, "core")
    gup = moved(bot, HEIGHT, 1)
    gdn = moved(top, HEIGHT, -1)
    slab = (3072, 128)
    (code,) = call(
        pair_kernel,
        [out(slab, BF16)],
        [g, got],
        1 << 21,
        outside=(0,),
        scratch=[pltpu.VMEM(slab, BF16), pltpu.SemaphoreType.DMA((4,))],
    )
    code, pg_late = tied((code, pg))
    code = lax.all_to_all(code.reshape(16, 192, 128), (TM, "y"), 0, 0, tiled=True)
    ng, gst = call(
        lambda *refs: backward_kernel(members, *refs),
        [out(flat, F32), out((1, 8, 128), F32)],
        [pg_late, gup, gdn, in_hbm(w9), in_hbm(x), st],
        9 * gflop,
        loose=(3, 4, 5),
        outside=(0,),
        scratch=[
            pltpu.VMEM((2, 1280, 768), BF16),
            pltpu.VMEM((3, 256, 768), BF16),
            pltpu.VMEM(flat, BF16),
            pltpu.VMEM(small.shape, F32),
            pltpu.VMEM(flat, F32),
            pltpu.SemaphoreType.DMA((12,)),
        ],
    )
    gst, hid_sent = tied((gst, hid_far))
    prev = moved(hid_sent, TM, 1)
    code, gst = tied((code, gst))
    (pieces,) = call(xy_kernel, [out((8, 224, 128), BF16)], [code, gst], 1 << 20)
    pieces = lax.all_to_all(pieces, HEIGHT, 0, 0, tiled=True)
    mine, gst = call(z_kernel, [out((192, 128), BF16), out((1, 8, 128), F32)], [pieces], 1 << 20)
    (input_grad,) = call(
        lambda *refs: input_grad_kernel(members, *refs),
        [out(flat, BF16)],
        [x, cot, in_hbm(ng), in_hbm(st), gst],
        1 << 21,
    )
    mine = gathered(mine, "y")
    mine, prev, input_grad = tied((mine, prev, input_grad))
    (block_output,) = call(block_kernel, [out(flat, BF16)], [x, hid_far, prev, temporal_kernel], 3 * gflop)
    mine = gathered(mine, TM)
    mine, block_output = tied((mine, block_output))
    tile = out((8, 128), F32)
    own, acc = call(half_kernel, [out(slab, F32), tile], [info, mine], 1 << 21, smem=1)
    clipped_spatial, clipped_temporal = call(
        lambda *refs: clip_kernel(clip_level, *refs),
        [out((9, 256, 256), F32), out((3, 256, 256), F32)],
        [info, own, acc, swapped(mine, "core")],
        1 << 21,
        smem=1,
        outside=(0, 1),
        scratch=[
            pltpu.VMEM((12, 256, 256), F32),
            pltpu.VMEM(slab, F32),
            pltpu.VMEM(tile.shape, F32),
            pltpu.SemaphoreType.DMA((12,)),
        ],
    )
    return (
        block_output.reshape(video_latents.shape),
        input_grad.reshape(video_latents.shape),
        clipped_spatial.reshape(spatial_kernel.shape),
        clipped_temporal,
    )


def solution(mesh):
    sizes = (mesh.shape["dp"] // 2, 2, mesh.shape[TM], mesh.shape[HEIGHT])
    torus = Mesh(mesh.devices.reshape(sizes), (*DP, TM, HEIGHT))
    field = P(DP, TM, HEIGHT, None, None)
    return jax.shard_map(
        body, mesh=torus, in_specs=(field, field, P(), P()), out_specs=(field, field, P(), P()), check_vma=False
    )
```
